256 devices in a mesh: cuts: 8 (over y, core), dom: 32 (over z, x).
Axes of the slice: x: 4, y: 4, z: 8, core: 2. Of those that a mesh axis runs over, the one named last changes fastest.
Arguments:
- feats: bfloat16 [65536, 4096], P('dom', 'cuts'), may hold values from -6 to 6
- adjacency: bfloat16 [2048, 128, 128], P('dom'), may hold values from 0 to 0.024658203
- blk_dst: int32 [2048], P('dom'), may hold values from 0 to 31
- blk_src: int32 [2048], P('dom'), may hold values from 0 to 15
- blk_count: int32 [32], P('dom'), may hold values from 1 to 64, as said below
- nbr_ids: int32 [4096, 8], P('dom'), may hold values from 0 to 4095
- edge_types: int32 [4096, 8], P('dom'), may hold values from 0 to 3
- w_first: bfloat16 [4096, 128], P('cuts'), may hold values from -0.09375 to 0.09375
- w_edge: bfloat16 [128, 512], replicated, may hold values from -0.1875 to 0.1875
- w_gate_in: bfloat16 [128, 384], replicated, may hold values from -0.5 to 0.5
- w_gate_state: bfloat16 [128, 256], replicated, may hold values from -0.5 to 0.5
- w_cand: bfloat16 [128, 128], replicated, may hold values from -0.5 to 0.5
- out_grad: bfloat16 [4096, 128], P('dom'), may hold values from -0.5 to 0.5
Outputs:
- new_state: bfloat16 [4096, 128], P('dom')
- w_first_grad: float32 [4096, 128], P(('cuts', 'dom'))
The draws below stay inside these ranges and needn't reach their ends.
Inputs may be any that keep to these rules, and one draw needn't show every extreme that they name: `blk_count`: slot b counts for partition b // 64 only if b mod 64 is below this count; the other slots are padding; some partition has all 64 slots live. `blk_dst`: a destination block number. `blk_src`: a source block number within the partition.
All inputs are finite; a program needn't handle non-finite values.
Results may differ from the reference program's by a relative error of at most 0.0075.
Values may be sent and summed in bfloat16 or wider, within the bound.
No kernel may reach another device: no remote copies, remote signals or barrier semaphores. Data moves between devices by JAX's collectives and lax.ppermute only.
A program may use at most 64 MiB of HBM per device.

```python
import math
import jax
import jax.numpy as jnp
from jax import lax

F = 4096
HID = 128
BLK = 128
ETYPES = 4
KNBR = 8
NBLK = 64
ROWS_DEV = 128
NODES_DEV = 2048
MB = 4096
NODES = 65536
BLOCKS = 2048
N_DOM = 32


def draw_blk_count(key, part):
    first_key, second_key = jax.random.split(jax.random.fold_in(key, 17))
    domains = MB // ROWS_DEV
    counts = jax.random.randint(first_key, (domains,), max(1, NBLK // 8), NBLK + 1)
    chosen = jax.random.randint(second_key, (), 0, domains)
    return jnp.where(jnp.arange(domains) == chosen, NBLK, counts).astype(jnp.int32)


def plant(drawn, stream_key, low, high):
    longest = drawn.shape.index(max(drawn.shape))
    spots = []
    for shift in (0, 1):
        where = [jax.random.randint(jax.random.fold_in(stream_key, axis), (), 0, length) for axis, length in enumerate(drawn.shape)]
        where[longest] = (where[longest] + shift) % drawn.shape[longest]
        spots.append(tuple(where))
    return drawn.at[spots[0]].set(low).at[spots[1]].set(high)


def spiked(drawn, stream_key, source, target, parts, factor):
    owner, partner = [(jnp.arange(drawn.shape[position]) // (drawn.shape[position] // parts)).reshape([-1 if axis == position else 1 for axis in range(drawn.ndim)]) for position in (source, target)]
    chosen = jax.random.permutation(stream_key, parts)[partner]
    strong = (owner == chosen) | (owner == (partner + parts // 2) % parts)
    return jnp.where(strong, factor * drawn, drawn)


def block_levels(own_key, shape, pieces, smallest, high):
    level, own = 1.0, jax.random.fold_in(own_key, 6)
    for axis_at, shards_of in pieces:
        steps = jnp.exp(jax.random.uniform(jax.random.fold_in(own, axis_at), (shards_of,), jnp.float32, smallest / len(pieces), high / len(pieces)))
        level = level * jnp.repeat(steps, shape[axis_at] // shards_of).reshape([-1 if axis == axis_at else 1 for axis in range(len(shape))])
    return level


def noise(rng, shape, scale, limit, cuts=(), kind=jnp.bfloat16):
    values = jax.random.normal(rng, shape, jnp.float32) * scale
    if len(cuts) > 0:
        values = block_levels(rng, shape, cuts, -0.22, 0.18) * values
    return jnp.clip(values, min=-limit, max=limit).astype(kind)


def bell_draw_with(own_key, extent, spread, most, cuts, heavy, kind=jnp.bfloat16):
    values = spread * jax.random.normal(own_key, extent, jnp.float32)
    if cuts:
        values = values * block_levels(own_key, extent, cuts, -0.22, 0.18)
    return jnp.clip(spiked(values, jax.random.fold_in(own_key, 3), *heavy), -most, most).astype(kind)


def setup_inputs(seed: int = 0) -> dict:
    key_list = jax.random.split(jax.random.key(seed), 14)
    feats = bell_draw_with(key_list[0], (NODES, F), 1.0, 6.0, ((0, 32), (1, 8)), (0, 1, 32, 2.75))
    adjacency = jnp.clip(0.024658203 * jax.random.uniform(key_list[1], (BLOCKS, BLK, BLK), jnp.float32) ** block_levels(key_list[1], (BLOCKS, BLK, BLK), ((0, 32),), -0.2, 0.2), 0.0, 0.024658203).astype(jnp.bfloat16)
    blk_dst = plant(jax.random.randint(key_list[2], (BLOCKS,), 0, MB // BLK), jax.random.fold_in(key_list[2], 1), 0, (MB // BLK) - 1).astype(jnp.int32)
    blk_src = plant(jax.random.randint(key_list[3], (BLOCKS,), 0, NODES_DEV // BLK), jax.random.fold_in(key_list[3], 1), 0, (NODES_DEV // BLK) - 1).astype(jnp.int32)
    blk_count = draw_blk_count(jax.random.fold_in(key_list[13], 71), 0)
    nbr_ids = plant(jax.random.randint(key_list[5], (MB, KNBR), 0, MB), jax.random.fold_in(key_list[5], 1), 0, MB - 1).astype(jnp.int32)
    edge_types = plant(jax.random.randint(key_list[6], (MB, KNBR), 0, ETYPES), jax.random.fold_in(key_list[6], 1), 0, ETYPES - 1).astype(jnp.int32)
    w_first = noise(key_list[7], (F, HID), F ** -0.5, 0.09375, ((0, 8),))
    w_edge = noise(key_list[8], (HID, ETYPES * HID), (HID * KNBR) ** -0.5, 0.1875)
    w_gate_in = noise(key_list[9], (HID, 3 * HID), HID ** -0.5, 0.5)
    w_gate_state = noise(key_list[10], (HID, 2 * HID), HID ** -0.5, 0.5)
    w_cand = noise(key_list[11], (HID, HID), HID ** -0.5, 0.5)
    out_grad = noise(key_list[12], (MB, HID), (2 * MB ** -0.5), 0.5, ((0, 32),))
    return dict(feats=feats, adjacency=adjacency, blk_dst=blk_dst, blk_src=blk_src, blk_count=blk_count, nbr_ids=nbr_ids, edge_types=edge_types, w_first=w_first, w_edge=w_edge, w_gate_in=w_gate_in, w_gate_state=w_gate_state, w_cand=w_cand, out_grad=out_grad)


def edge_messages(states, nbr_ids, edge_types, w_edge):
    row_count, fanout = nbr_ids.shape
    hidden = states.shape[1]
    num_types = w_edge.shape[1] // hidden
    picked = states[nbr_ids.reshape(-1)]
    projected = jnp.dot(picked, w_edge, preferred_element_type=jnp.float32).reshape(row_count, fanout, num_types, hidden)
    one_hot = (edge_types[:, :, None] == jnp.arange(num_types, dtype=jnp.int32)[None, None, :]).astype(jnp.float32)
    return jnp.sum(projected * one_hot[:, :, :, None], axis=(1, 2))


def edge_backward(message_grad, nbr_ids, edge_types, w_edge):
    row_count, fanout = nbr_ids.shape
    hidden = message_grad.shape[1]
    num_types = w_edge.shape[1] // hidden
    w_back = w_edge.reshape(hidden, num_types, hidden).transpose(2, 1, 0).reshape(hidden, num_types * hidden)
    per_type = jnp.dot(message_grad, w_back, preferred_element_type=jnp.float32).reshape(row_count, 1, num_types, hidden)
    one_hot = (edge_types[:, :, None] == jnp.arange(num_types, dtype=jnp.int32)[None, None, :]).astype(jnp.float32)
    return jnp.sum(per_type * one_hot[:, :, :, None], axis=2)


def gated_update(message, states, out_grad, w_gate_in, w_gate_state, w_cand):
    hidden = states.shape[1]
    message_in = message.astype(jnp.bfloat16)
    gate_in = jnp.dot(message_in, w_gate_in, preferred_element_type=jnp.float32)
    gate_state = jnp.dot(states, w_gate_state, preferred_element_type=jnp.float32)
    state_value = states.astype(jnp.float32)
    update = jax.nn.sigmoid(gate_in[:, :hidden] + gate_state[:, :hidden])
    reset = jax.nn.sigmoid(gate_in[:, hidden:2 * hidden] + gate_state[:, hidden:])
    reset_state = (reset * state_value).astype(jnp.bfloat16)
    candidate = jnp.tanh(gate_in[:, 2 * hidden:] + jnp.dot(reset_state, w_cand, preferred_element_type=jnp.float32))
    new_state = ((1.0 - update) * candidate + update * state_value).astype(jnp.bfloat16)
    out_value = out_grad.astype(jnp.float32)
    cand_pre = out_value * (1.0 - update) * (1.0 - candidate * candidate)
    update_pre = out_value * (state_value - candidate) * update * (1.0 - update)
    cand_grad = cand_pre.astype(jnp.bfloat16)
    reset_grad_in = jnp.dot(cand_grad, w_cand.T, preferred_element_type=jnp.float32)
    reset_pre = reset_grad_in * state_value * reset * (1.0 - reset)
    gate_grads = jnp.concatenate([update_pre, reset_pre, cand_pre], axis=1).astype(jnp.bfloat16)
    message_grad = jnp.dot(gate_grads, w_gate_in.T, preferred_element_type=jnp.float32).astype(jnp.bfloat16)
    state_grad = out_value * update + reset_grad_in * reset + jnp.dot(gate_grads[:, :2 * hidden], w_gate_state.T, preferred_element_type=jnp.float32)
    return new_state, message_grad, state_grad


def reference(feats, adjacency, blk_dst, blk_src, blk_count, nbr_ids, edge_types, w_first, w_edge, w_gate_in, w_gate_state, w_cand, out_grad):
    src_blocks = NODES_DEV // BLK
    total_rows = ROWS_DEV * N_DOM
    dst_blocks = total_rows // BLK
    feat_tiles = feats.reshape(N_DOM * src_blocks, BLK, F)
    block_ids = jnp.arange(N_DOM * NBLK, dtype=jnp.int32)
    owner = block_ids // NBLK
    live_mask = (block_ids - owner * NBLK) < blk_count[owner]
    global_src = (owner * src_blocks + blk_src).astype(jnp.int32)
    group_size = math.gcd(NBLK, 16)
    groups = N_DOM * NBLK // group_size
    inputs = (adjacency.reshape(groups, group_size, BLK, BLK), global_src.reshape(groups, group_size), blk_dst.reshape(groups, group_size), live_mask.reshape(groups, group_size))
    w_wide = w_first.astype(jnp.float32)

    def aggregate(adj_group, src_group):
        src_rows = feat_tiles[src_group].astype(jnp.float32)
        return jnp.einsum("bij,bjf->bif", adj_group.astype(jnp.float32), src_rows).astype(jnp.bfloat16)

    def forward_step(running, group):
        adj_group, src_group, dst_group, live_group = group
        aggregated = aggregate(adj_group, src_group)
        projected = jnp.einsum("bif,fh->bih", aggregated.astype(jnp.float32), w_wide)
        projected = jnp.where(live_group[:, None, None], projected, 0.0)
        return running.at[dst_group].add(projected), None

    first = lax.scan(forward_step, jnp.zeros((dst_blocks, BLK, HID), jnp.float32), inputs)[0]
    first = first.reshape(total_rows, HID)
    state_exact = jnp.tanh(first)
    states = state_exact.astype(jnp.bfloat16)
    message = edge_messages(states, nbr_ids, edge_types, w_edge)
    new_state, message_grad, state_grad = gated_update(message, states, out_grad, w_gate_in, w_gate_state, w_cand)
    contrib = edge_backward(message_grad, nbr_ids, edge_types, w_edge)
    state_grad = state_grad + jax.ops.segment_sum(contrib.reshape(-1, HID), nbr_ids.reshape(-1), num_segments=total_rows)
    first_grad = (state_grad * (1.0 - state_exact * state_exact)).astype(jnp.bfloat16).reshape(dst_blocks, BLK, HID)

    def backward_step(running, group):
        adj_group, src_group, dst_group, live_group = group
        aggregated = aggregate(adj_group, src_group)
        picked = jnp.where(live_group[:, None, None], first_grad[dst_group].astype(jnp.float32), 0.0)
        return running + jnp.einsum("bif,bih->fh", aggregated.astype(jnp.float32), picked), None

    w_first_grad = lax.scan(backward_step, jnp.zeros((F, HID), jnp.float32), inputs)[0]
    return new_state, w_first_grad
```

```python
import jax
import jax.numpy as jnp
from jax import lax
from jax.experimental import pallas as pl
from jax.experimental.pallas import tpu as pltpu
from jax.sharding import PartitionSpec as P

F32 = jnp.float32
BF16 = jnp.bfloat16
VMEM = pltpu.VMEM
SMEM = pltpu.SMEM


def vspec():
    return pl.BlockSpec(memory_space=pltpu.VMEM)


def sspec():
    return pl.BlockSpec(memory_space=pltpu.SMEM)


def hspec():
    return pl.BlockSpec(memory_space=pl.ANY)


def params():
    return pltpu.CompilerParams(vmem_limit_bytes=48 * 1024 * 1024)


def dot(a, b):
    return jnp.dot(a, b, preferred_element_type=F32)


def partial_kernel(
    core_ref, dst_ref, src_ref, count_ref, feats_hbm, adj_hbm, w_ref,
    keep_ref, send_ref, feats, adj, projected, acc, sems,
):
    slots, block, _ = adj.shape
    cuts, _, _ = acc.shape
    piece = block // cuts
    nodes = feats.shape[0]
    chunk = nodes // 4
    feat_copies = [
        pltpu.make_async_copy(
            feats_hbm.at[pl.ds(i * chunk, chunk)], feats.at[pl.ds(i * chunk, chunk)], sems.at[i]
        )
        for i in range(4)
    ]
    adj_copy = pltpu.make_async_copy(adj_hbm, adj, sems.at[4])
    for copy in feat_copies:
        copy.start()
    adj_copy.start()
    acc[...] = jnp.zeros_like(acc)
    for i in range(4):
        feat_copies[i].wait()
        rows = pl.ds(i * chunk, chunk)
        projected[rows, :] = dot(feats[rows, :], w_ref[...]).astype(BF16)
    adj_copy.wait()
    count = count_ref[0]
    step = 8

    def some_slots(group, carry):
        for j in range(step):
            slot = group * step + j
            rows = pl.ds(pl.multiple_of(src_ref[slot] * block, block), block)
            right = projected[rows, :]
            right = jnp.where(slot < count, right, jnp.zeros_like(right))
            result = dot(adj[slot], right)
            at = pl.ds(pl.multiple_of(dst_ref[slot] * piece, piece), piece)
            for c in range(cuts):
                acc[c, at, :] += result[c * piece : (c + 1) * piece]
        return carry

    lax.fori_loop(0, slots // step, some_slots, 0)
    core = core_ref[0]
    for y in range(cuts // 2):
        keep_ref[y] = acc[2 * y + core]
        send_ref[y] = acc[2 * y + 1 - core]


def count_kernel(cut_ref, nbr_ref, type_ref, count_ref, *, cuts, block):
    rows, fanout = nbr_ref.shape
    cells = count_ref.shape[1]
    piece = block // cuts
    nbr = nbr_ref[...]
    within = nbr % block
    local = (nbr // block) * piece + within % piece
    per_type = cells // 4
    key = jnp.where(within // piece == cut_ref[0], type_ref[...] * per_type + local, -1)
    tile = 512
    for start in range(0, cells, tile):
        place = lax.broadcasted_iota(jnp.int32, (rows, tile), 1) + start
        total = jnp.zeros((rows, tile), F32)
        for k in range(fanout):
            total += jnp.where(key[:, k : k + 1] == place, 1.0, 0.0)
        count_ref[:, start : start + tile] = total.astype(BF16)


def state_kernel(part_ref, first_ref, out_ref):
    total = jnp.sum(part_ref[...].astype(F32), axis=0)
    exact = jnp.tanh(total)
    first_ref[...] = exact
    states = exact.astype(BF16)
    for q in range(out_ref.shape[0]):
        out_ref[q] = states


def message_kernel(count_ref, states_ref, own_ref, w_ref, out_ref):
    hidden = own_ref.shape[2]
    rows = count_ref.shape[0]
    domains, piece, _ = states_ref.shape
    local = domains * piece
    states = states_ref[...].reshape(local, hidden)
    message = jnp.zeros((rows, hidden), F32)
    for e in range(count_ref.shape[1] // local):
        picked = dot(count_ref[:, e * local : (e + 1) * local], states).astype(BF16)
        message += dot(picked, w_ref[:, e * hidden : (e + 1) * hidden])
    message = message.astype(BF16)
    for c in range(out_ref.shape[0]):
        out_ref[c, :rows] = message
        out_ref[c, rows:] = own_ref[0]


def gate_kernel(
    cut_ref, recv_ref, count_ref, grad_ref, w_edge_ref, w_in_ref, w_state_ref, w_cand_ref,
    new_ref, direct_ref, back_ref, own,
):
    rows, hidden = grad_ref.shape
    cuts = recv_ref.shape[0]
    piece = recv_ref.shape[1] - rows
    local = count_ref.shape[1] // 4
    message = jnp.sum(recv_ref[:, :rows, :].astype(F32), axis=0)
    states = recv_ref[:, rows:, :].reshape(cuts * piece, hidden)
    message_in = message.astype(BF16)
    w_in = w_in_ref[...]
    w_state = w_state_ref[...]
    w_cand = w_cand_ref[...]
    gate_in = dot(message_in, w_in)
    gate_state = dot(states, w_state)
    value = states.astype(F32)
    update = jax.nn.sigmoid(gate_in[:, :hidden] + gate_state[:, :hidden])
    reset = jax.nn.sigmoid(gate_in[:, hidden : 2 * hidden] + gate_state[:, hidden:])
    candidate = jnp.tanh(gate_in[:, 2 * hidden :] + dot((reset * value).astype(BF16), w_cand))
    new_ref[...] = ((1.0 - update) * candidate + update * value).astype(BF16)
    out_grad = grad_ref[...].astype(F32)
    cand_pre = out_grad * (1.0 - update) * (1.0 - candidate * candidate)
    update_pre = out_grad * (value - candidate) * update * (1.0 - update)
    contract = (((1,), (1,)), ((), ()))
    cand_grad = cand_pre.astype(BF16)
    reset_in = lax.dot_general(cand_grad, w_cand, contract, preferred_element_type=F32)
    reset_pre = reset_in * value * reset * (1.0 - reset)
    gates = jnp.concatenate([update_pre.astype(BF16), reset_pre.astype(BF16), cand_grad], axis=1)
    message_grad_t = lax.dot_general(w_in, gates, contract, preferred_element_type=F32).astype(BF16)
    own[...] = (
        out_grad * update
        + reset_in * reset
        + lax.dot_general(gates[:, : 2 * hidden], w_state, contract, preferred_element_type=F32)
    )
    direct_ref[...] = own[pl.ds(pl.multiple_of(cut_ref[0] * piece, piece), piece), :]
    total = jnp.zeros((hidden, local), F32)
    for e in range(count_ref.shape[1] // local):
        spread = dot(message_grad_t, count_ref[:, e * local : (e + 1) * local]).astype(BF16)
        total += dot(w_edge_ref[:, e * hidden : (e + 1) * hidden], spread)
    back_ref[...] = total.T.astype(BF16).reshape(back_ref.shape)


def grad_kernel(part_ref, direct_ref, exact_ref, out_ref):
    total = direct_ref[...] + jnp.sum(part_ref[...].astype(F32), axis=0)
    exact = exact_ref[...]
    grad = (total * (1.0 - exact * exact)).astype(BF16)
    for q in range(out_ref.shape[0]):
        out_ref[q] = grad


def weight_kernel(
    core_ref, dst_ref, src_ref, count_ref, mine_ref, other_ref, feats_hbm, adj_hbm,
    out_ref, feats, adj, grads, acc, wide, sems,
):
    slots, block, _ = adj.shape
    pairs, domains, piece, hidden = mine_ref.shape
    blocks = acc.shape[0]
    adj_copy = pltpu.make_async_copy(adj_hbm, adj, sems.at[0])
    feat_copy = pltpu.make_async_copy(feats_hbm, feats, sems.at[1])
    adj_copy.start()
    feat_copy.start()
    acc[...] = jnp.zeros_like(acc)
    core = core_ref[0]
    for y in range(pairs):
        at = pl.ds(pl.multiple_of((2 * y + core) * piece, piece), piece)
        grads[:, at, :] = mine_ref[y]
        at = pl.ds(pl.multiple_of((2 * y + 1 - core) * piece, piece), piece)
        grads[:, at, :] = other_ref[y]

    def turn(d, carry):
        grads[d] = grads[d].T
        return carry

    lax.fori_loop(0, domains, turn, 0, unroll=4)
    adj_copy.wait()
    count = count_ref[0]
    step = 8

    def some_slots(group, carry):
        for j in range(step):
            slot = group * step + j
            left = grads[dst_ref[slot]]
            left = jnp.where(slot < count, left, jnp.zeros_like(left))
            acc[src_ref[slot]] += dot(left, adj[slot])
        return carry

    lax.fori_loop(0, slots // step, some_slots, 0)
    for s in range(blocks):
        wide[:, s * block : (s + 1) * block] = acc[s].astype(BF16)
    feat_copy.wait()
    result = dot(wide[...], feats[...])
    out_ref[...] = result.T.astype(BF16).reshape(out_ref.shape)


def body(
    feats,
    adjacency,
    blk_dst,
    blk_src,
    blk_count,
    nbr_ids,
    edge_types,
    w_first,
    w_edge,
    w_gate_in,
    w_gate_state,
    w_cand,
    out_grad,
):
    slots, block, _ = adjacency.shape
    nodes, feat_cols = feats.shape
    hidden = w_first.shape[1]
    rows = out_grad.shape[0]
    domains = lax.axis_size("dom")
    cuts = lax.axis_size("cuts")
    pairs = cuts // 2
    piece = block // cuts
    local = domains * piece
    cut = lax.axis_index("cuts").reshape(1)
    core = cut % 2
    same_core = [[2 * y + k for y in range(pairs)] for k in range(2)]
    partner = [(i, i ^ 1) for i in range(cuts)]

    def over_dom(x):
        return lax.all_to_all(x, "dom", 0, 0, tiled=True)

    def over_y(x):
        return lax.all_to_all(x, "cuts", 0, 0, tiled=True, axis_index_groups=same_core)

    half = jax.ShapeDtypeStruct((pairs, local, hidden), F32)
    keep, send = pl.pallas_call(
        partial_kernel,
        out_shape=(half, half),
        in_specs=[sspec()] * 4 + [hspec(), hspec(), vspec()],
        out_specs=(vspec(), vspec()),
        scratch_shapes=[
            VMEM((nodes, feat_cols), BF16),
            VMEM((slots, block, block), BF16),
            VMEM((nodes, hidden), BF16),
            VMEM((cuts, local, hidden), F32),
            pltpu.SemaphoreType.DMA((5,)),
        ],
        compiler_params=params(),
        name="partial",
    )(core, blk_dst, blk_src, blk_count, feats, adjacency, w_first)
    got = lax.ppermute(send, "cuts", partner)
    counts = pl.pallas_call(
        lambda *refs: count_kernel(*refs, cuts=cuts, block=block),
        out_shape=jax.ShapeDtypeStruct((rows, 4 * local), BF16),
        in_specs=[sspec(), vspec(), vspec()],
        out_specs=vspec(),
        compiler_params=params(),
        name="counts",
    )(cut, nbr_ids, edge_types)
    by_y = over_y((keep + got).astype(BF16))
    by_dom = over_dom(
        jnp.sum(by_y.astype(F32), axis=0).astype(BF16).reshape(domains, piece, hidden)
    )
    spread = jax.ShapeDtypeStruct((domains, piece, hidden), BF16)
    small = jax.ShapeDtypeStruct((piece, hidden), F32)
    exact, own_states = pl.pallas_call(
        state_kernel,
        out_shape=(small, spread),
        in_specs=[vspec()],
        out_specs=(vspec(), vspec()),
        compiler_params=params(),
        name="state",
    )(by_dom)
    states = over_dom(own_states)
    sent = pl.pallas_call(
        message_kernel,
        out_shape=jax.ShapeDtypeStruct((cuts, rows + piece, hidden), BF16),
        in_specs=[vspec(), vspec(), vspec(), vspec()],
        out_specs=vspec(),
        compiler_params=params(),
        name="message",
    )(counts, states, own_states, w_edge)
    recv = lax.all_to_all(sent, "cuts", 0, 0, tiled=True)
    new_state, direct, back = pl.pallas_call(
        gate_kernel,
        out_shape=(jax.ShapeDtypeStruct((rows, hidden), BF16), small, spread),
        in_specs=[sspec()] + [vspec()] * 7,
        out_specs=(vspec(), vspec(), vspec()),
        scratch_shapes=[VMEM((rows, hidden), F32)],
        compiler_params=params(),
        name="gates",
    )(cut, recv, counts, out_grad, w_edge, w_gate_in, w_gate_state, w_cand)
    grad_part = over_dom(back)
    own_grad = pl.pallas_call(
        grad_kernel,
        out_shape=spread,
        in_specs=[vspec()] * 3,
        out_specs=vspec(),
        compiler_params=params(),
        name="first_grad",
    )(grad_part, direct, exact)
    slice_grads = over_dom(own_grad)
    mine = over_y(jnp.broadcast_to(slice_grads[None], (pairs, domains, piece, hidden)))
    other = lax.ppermute(mine, "cuts", partner)
    weight_part = pl.pallas_call(
        weight_kernel,
        out_shape=jax.ShapeDtypeStruct((domains, feat_cols // domains, hidden), BF16),
        in_specs=[sspec()] * 4 + [vspec(), vspec(), hspec(), hspec()],
        out_specs=vspec(),
        scratch_shapes=[
            VMEM((nodes, feat_cols), BF16),
            VMEM((slots, block, block), BF16),
            VMEM((domains, block, hidden), BF16),
            VMEM((nodes // block, hidden, block), F32),
            VMEM((hidden, nodes), BF16),
            pltpu.SemaphoreType.DMA((2,)),
        ],
        compiler_params=params(),
        name="weight_grad",
    )(core, blk_dst, blk_src, blk_count, mine, other, feats, adjacency)
    w_first_grad = jnp.sum(over_dom(weight_part).astype(F32), axis=0)
    return (new_state, w_first_grad)


def solution(mesh):
    return jax.shard_map(
        body,
        mesh=mesh,
        in_specs=(
            P("dom", "cuts"),
            P("dom", None, None),
            P("dom"),
            P("dom"),
            P("dom"),
            P("dom", None),
            P("dom", None),
            P("cuts", None),
            P(),
            P(),
            P(),
            P(),
            P("dom", None),
        ),
        out_specs=(P("dom", None), P(("cuts", "dom"), None)),
        check_vma=False,
    )
```

```python
import jax
import jax.numpy as jnp
from jax import lax
from jax.experimental import pallas as pl
from jax.experimental.pallas import tpu as pltpu
from jax.sharding import PartitionSpec as P

F32 = jnp.float32
BF16 = jnp.bfloat16
VMEM = pltpu.VMEM
SMEM = pltpu.SMEM


def vspec():
    return pl.BlockSpec(memory_space=pltpu.VMEM)


def sspec():
    return pl.BlockSpec(memory_space=pltpu.SMEM)


def hspec():
    return pl.BlockSpec(memory_space=pltpu.HBM)


def params():
    return pltpu.CompilerParams(vmem_limit_bytes=48 * 1024 * 1024)


def dot(a, b):
    return jnp.dot(a, b, preferred_element_type=F32)


def project_kernel(feats_hbm, w_hbm, out_ref, feats, w, sems, *, start):
    rows = feats.shape[0]
    parts = 4
    chunk = rows // parts
    w_copy = pltpu.make_async_copy(w_hbm, w, sems.at[parts])
    w_copy.start()
    copies = [
        pltpu.make_async_copy(
            feats_hbm.at[pl.ds(start + i * chunk, chunk)],
            feats.at[pl.ds(i * chunk, chunk)],
            sems.at[i],
        )
        for i in range(parts)
    ]
    for copy in copies:
        copy.start()
    w_copy.wait()
    for i in range(parts):
        copies[i].wait()
        at = pl.ds(i * chunk, chunk)
        out_ref[at, :] = dot(feats[at, :], w[...])


def own_rows(adj, slot, core, piece):
    pairs = adj.shape[1] // (2 * piece)
    return jnp.concatenate(
        [
            adj[slot, pl.ds(pl.multiple_of((2 * y + core) * piece, piece), piece), :]
            for y in range(pairs)
        ],
        axis=0,
    )


def partial_kernel(
    core_ref, dst_ref, src_ref, count_ref, adj, *refs, near, far,
):
    parts = refs[: -3]
    out_ref, projected, acc = refs[-3:]
    slots, block, _ = adj.shape
    pairs = acc.shape[0]
    piece = acc.shape[1] // (near * far)
    hidden = acc.shape[2]
    half = len(parts) // 2
    rows = parts[0].shape[0]
    acc[...] = jnp.zeros_like(acc)
    for i in range(half):
        both = parts[i][...] + parts[half + i][...]
        high = both.astype(BF16)
        at = pl.ds(i * rows, rows)
        projected[at, :hidden] = high
        projected[at, hidden:] = (both - high.astype(F32)).astype(BF16)
    core = core_ref[0]
    count = count_ref[0]
    step = 8

    def some_slots(group, carry):
        for j in range(step):
            slot = group * step + j
            right = projected[pl.ds(pl.multiple_of(src_ref[slot] * block, block), block), :]
            result = dot(own_rows(adj, slot, core, piece), right)
            result = result[:, :hidden] + result[:, hidden:]
            result = jnp.where(slot < count, result, 0.0)
            d = dst_ref[slot]
            place = ((d % near) * far + d // near) * piece
            at = pl.ds(pl.multiple_of(place, piece), piece)
            for y in range(pairs):
                acc[y, at, :] += result[y * piece : (y + 1) * piece]
        return carry

    lax.fori_loop(0, slots // step, some_slots, 0)
    out_ref[...] = acc[...].astype(BF16).reshape(out_ref.shape)


def count_kernel(cut_ref, nbr_ref, type_ref, count_ref, *, cuts, block):
    rows, fanout = nbr_ref.shape
    cells = count_ref.shape[1]
    piece = block // cuts
    nbr = nbr_ref[...]
    within = nbr % block
    local = (nbr // block) * piece + within % piece
    per_type = cells // 4
    key = jnp.where(within // piece == cut_ref[0], type_ref[...] * per_type + local, -1)
    tile = 512
    for start in range(0, cells, tile):
        place = lax.broadcasted_iota(jnp.int32, (rows, tile), 1) + start
        total = jnp.zeros((rows, tile), F32)
        for k in range(fanout):
            total += jnp.where(key[:, k : k + 1] == place, 1.0, 0.0)
        count_ref[:, start : start + tile] = total.astype(BF16)


def state_kernel(part_ref, first_ref, out_ref):
    total = jnp.sum(part_ref[...].astype(F32), axis=0)
    exact = jnp.tanh(total)
    first_ref[...] = exact
    states = exact.astype(BF16)
    for q in range(out_ref.shape[0]):
        out_ref[q] = states


def message_kernel(count_ref, states_ref, own_ref, w_ref, out_ref):
    hidden = own_ref.shape[2]
    rows = count_ref.shape[0]
    domains, piece, _ = states_ref.shape
    local = domains * piece
    states = states_ref[...].reshape(local, hidden)
    message = jnp.zeros((rows, hidden), F32)
    for e in range(count_ref.shape[1] // local):
        picked = dot(count_ref[:, e * local : (e + 1) * local], states).astype(BF16)
        message += dot(picked, w_ref[:, e * hidden : (e + 1) * hidden])
    message = message.astype(BF16)
    for c in range(out_ref.shape[0]):
        out_ref[c, :rows] = message
        out_ref[c, rows:] = own_ref[0]


def gate_kernel(
    cut_ref, recv_ref, count_ref, grad_ref, w_edge_ref, w_in_ref, w_state_ref, w_cand_ref,
    new_ref, direct_ref, back_ref, own,
):
    rows, hidden = grad_ref.shape
    cuts = recv_ref.shape[0]
    piece = recv_ref.shape[1] - rows
    local = count_ref.shape[1] // 4
    message = jnp.sum(recv_ref[:, :rows, :].astype(F32), axis=0)
    states = recv_ref[:, rows:, :].reshape(cuts * piece, hidden)
    message_in = message.astype(BF16)
    w_in = w_in_ref[...]
    w_state = w_state_ref[...]
    w_cand = w_cand_ref[...]
    gate_in = dot(message_in, w_in)
    gate_state = dot(states, w_state)
    value = states.astype(F32)
    update = jax.nn.sigmoid(gate_in[:, :hidden] + gate_state[:, :hidden])
    reset = jax.nn.sigmoid(gate_in[:, hidden : 2 * hidden] + gate_state[:, hidden:])
    candidate = jnp.tanh(gate_in[:, 2 * hidden :] + dot((reset * value).astype(BF16), w_cand))
    new_ref[...] = ((1.0 - update) * candidate + update * value).astype(BF16)
    out_grad = grad_ref[...].astype(F32)
    cand_pre = out_grad * (1.0 - update) * (1.0 - candidate * candidate)
    update_pre = out_grad * (value - candidate) * update * (1.0 - update)
    contract = (((1,), (1,)), ((), ()))
    cand_grad = cand_pre.astype(BF16)
    reset_in = lax.dot_general(cand_grad, w_cand, contract, preferred_element_type=F32)
    reset_pre = reset_in * value * reset * (1.0 - reset)
    gates = jnp.concatenate([update_pre.astype(BF16), reset_pre.astype(BF16), cand_grad], axis=1)
    message_grad_t = lax.dot_general(w_in, gates, contract, preferred_element_type=F32).astype(BF16)
    own[...] = (
        out_grad * update
        + reset_in * reset
        + lax.dot_general(gates[:, : 2 * hidden], w_state, contract, preferred_element_type=F32)
    )
    direct_ref[...] = own[pl.ds(pl.multiple_of(cut_ref[0] * piece, piece), piece), :]
    total = jnp.zeros((hidden, local), F32)
    for e in range(count_ref.shape[1] // local):
        spread = dot(message_grad_t, count_ref[:, e * local : (e + 1) * local]).astype(BF16)
        total += dot(w_edge_ref[:, e * hidden : (e + 1) * hidden], spread)
    back_ref[...] = total.T.astype(BF16).reshape(back_ref.shape)


def grad_kernel(part_ref, direct_ref, exact_ref, out_ref):
    total = direct_ref[...] + jnp.sum(part_ref[...].astype(F32), axis=0)
    exact = exact_ref[...]
    grad = (total * (1.0 - exact * exact)).astype(BF16)
    for q in range(out_ref.shape[0]):
        out_ref[q] = grad


def spread_kernel(
    core_ref, dst_ref, src_ref, count_ref, grads_ref, adj, out_ref, turned, acc, *, near, far
):
    slots, block, _ = adj.shape
    hidden = grads_ref.shape[2]
    piece = grads_ref.shape[1] // far
    pairs = grads_ref.shape[0] // near
    acc[...] = jnp.zeros_like(acc)
    for z in range(far):
        for x in range(near):
            rows = jnp.concatenate(
                [grads_ref[y * near + x, z * piece : (z + 1) * piece, :] for y in range(pairs)],
                axis=0,
            )
            turned[z * near + x] = rows.T
    core = core_ref[0]
    count = count_ref[0]
    step = 8

    def some_slots(group, carry):
        for j in range(step):
            slot = group * step + j
            result = dot(turned[dst_ref[slot]], own_rows(adj, slot, core, piece))
            acc[src_ref[slot]] += jnp.where(slot < count, result, 0.0)
        return carry

    lax.fori_loop(0, slots // step, some_slots, 0)
    for s in range(acc.shape[0]):
        out_ref[:, s * block : (s + 1) * block] = acc[s].astype(BF16)


def weight_kernel(spread_ref, feats_ref, out_ref):
    out_ref[...] = dot(spread_ref[...], feats_ref[...])


def weight_out_kernel(spread_ref, feats_ref, part_ref, out_ref):
    total = part_ref[...] + dot(spread_ref[...], feats_ref[...])
    out_ref[...] = total.T.astype(BF16).reshape(out_ref.shape)


def body(
    feats,
    adjacency,
    blk_dst,
    blk_src,
    blk_count,
    nbr_ids,
    edge_types,
    w_first,
    w_edge,
    w_gate_in,
    w_gate_state,
    w_cand,
    out_grad,
):
    slots, block, _ = adjacency.shape
    nodes, feat_cols = feats.shape
    hidden = w_first.shape[1]
    rows = out_grad.shape[0]
    far = lax.axis_size("z")
    near = lax.axis_size("x")
    pairs = lax.axis_size("y")
    domains = far * near
    cuts = 2 * pairs
    piece = block // cuts
    local = domains * piece
    core = lax.axis_index("core").reshape(1)
    cut = (2 * lax.axis_index("y") + lax.axis_index("core")).reshape(1)

    def over_dom(x):
        return lax.all_to_all(x, ("z", "x"), 0, 0, tiled=True)

    def over_plane(x):
        return lax.all_to_all(x, ("y", "x"), 0, 0, tiled=True)

    def over_far(x):
        return lax.all_to_all(x, "z", 0, 0, tiled=True)

    def swap(x):
        return lax.ppermute(x, "core", [(0, 1), (1, 0)])

    halves = 2
    rows_half = nodes // halves
    projected = [
        pl.pallas_call(
            lambda *refs, i=i: project_kernel(*refs, start=i * rows_half),
            out_shape=jax.ShapeDtypeStruct((rows_half, hidden), F32),
            in_specs=[hspec(), hspec()],
            out_specs=vspec(),
            scratch_shapes=[
                VMEM((rows_half, feat_cols), BF16),
                VMEM((feat_cols, hidden), BF16),
                pltpu.SemaphoreType.DMA((5,)),
            ],
            compiler_params=params(),
            name=f"project{i}",
        )(feats, w_first)
        for i in range(halves)
    ]
    swapped = [swap(p) for p in projected]
    counts = pl.pallas_call(
        lambda *refs: count_kernel(*refs, cuts=cuts, block=block),
        out_shape=jax.ShapeDtypeStruct((rows, 4 * local), BF16),
        in_specs=[sspec(), vspec(), vspec()],
        out_specs=vspec(),
        compiler_params=params(),
        name="counts",
    )(cut, nbr_ids, edge_types)
    partial = pl.pallas_call(
        lambda *refs: partial_kernel(*refs, near=near, far=far),
        out_shape=jax.ShapeDtypeStruct((pairs * near, far * piece, hidden), BF16),
        in_specs=[sspec()] * 4 + [vspec()] * (1 + 2 * halves),
        out_specs=vspec(),
        scratch_shapes=[VMEM((nodes, 2 * hidden), BF16), VMEM((pairs, local, hidden), F32)],
        compiler_params=params(),
        name="partial",
    )(core, blk_dst, blk_src, blk_count, adjacency, *projected, *swapped)
    by_plane = jnp.sum(over_plane(partial).astype(F32), axis=0)
    by_far = over_far(by_plane.reshape(far, piece, hidden))
    spread = jax.ShapeDtypeStruct((domains, piece, hidden), BF16)
    small = jax.ShapeDtypeStruct((piece, hidden), F32)
    exact, own_states = pl.pallas_call(
        state_kernel,
        out_shape=(small, spread),
        in_specs=[vspec()],
        out_specs=(vspec(), vspec()),
        compiler_params=params(),
        name="state",
    )(by_far)
    states = over_dom(own_states)
    sent = pl.pallas_call(
        message_kernel,
        out_shape=jax.ShapeDtypeStruct((cuts, rows + piece, hidden), BF16),
        in_specs=[vspec(), vspec(), vspec(), vspec()],
        out_specs=vspec(),
        compiler_params=params(),
        name="message",
    )(counts, states, own_states, w_edge)
    recv = lax.all_to_all(sent, ("y", "core"), 0, 0, tiled=True)
    new_state, direct, back = pl.pallas_call(
        gate_kernel,
        out_shape=(jax.ShapeDtypeStruct((rows, hidden), BF16), small, spread),
        in_specs=[sspec()] + [vspec()] * 7,
        out_specs=(vspec(), vspec(), vspec()),
        scratch_shapes=[VMEM((rows, hidden), F32)],
        compiler_params=params(),
        name="gates",
    )(cut, recv, counts, out_grad, w_edge, w_gate_in, w_gate_state, w_cand)
    grad_part = over_dom(back)
    own_grad = pl.pallas_call(
        grad_kernel,
        out_shape=jax.ShapeDtypeStruct((far, piece, hidden), BF16),
        in_specs=[vspec()] * 3,
        out_specs=vspec(),
        compiler_params=params(),
        name="first_grad",
    )(grad_part, direct, exact)
    far_grads = over_far(own_grad).reshape(1, far * piece, hidden)
    grads = over_plane(jnp.broadcast_to(far_grads, (pairs * near, far * piece, hidden)))
    mine = pl.pallas_call(
        lambda *refs: spread_kernel(*refs, near=near, far=far),
        out_shape=jax.ShapeDtypeStruct((hidden, nodes), BF16),
        in_specs=[sspec()] * 4 + [vspec()] * 2,
        out_specs=vspec(),
        scratch_shapes=[
            VMEM((domains, hidden, pairs * piece), BF16),
            VMEM((nodes // block, hidden, block), F32),
        ],
        compiler_params=params(),
        name="spread",
    )(core, blk_dst, blk_src, blk_count, grads, adjacency)
    other = swap(mine)
    own_part = pl.pallas_call(
        weight_kernel,
        out_shape=jax.ShapeDtypeStruct((hidden, feat_cols), F32),
        in_specs=[vspec()] * 2,
        out_specs=vspec(),
        compiler_params=params(),
        name="weight_own",
    )(mine, feats)
    weight_part = pl.pallas_call(
        weight_out_kernel,
        out_shape=jax.ShapeDtypeStruct((domains, feat_cols // domains, hidden), BF16),
        in_specs=[vspec()] * 3,
        out_specs=vspec(),
        compiler_params=params(),
        name="weight_all",
    )(other, feats, own_part)
    w_first_grad = jnp.sum(over_dom(weight_part).astype(F32), axis=0)
    return (new_state, w_first_grad)


def solution(mesh):
    cuts, domains = mesh.devices.shape
    fine = jax.sharding.Mesh(
        mesh.devices.reshape(cuts // 2, 2, domains // 4, 4), ("y", "core", "z", "x")
    )
    dom = ("z", "x")
    cut = ("y", "core")
    return jax.shard_map(
        body,
        mesh=fine,
        in_specs=(
            P(dom, cut),
            P(dom, None, None),
            P(dom),
            P(dom),
            P(dom),
            P(dom, None),
            P(dom, None),
            P(cut, None),
            P(),
            P(),
            P(),
            P(),
            P(dom, None),
        ),
        out_specs=(P(dom, None), P(cut + dom, None)),
        check_vma=False,
    )
```

```python
import jax
import jax.numpy as jnp
from jax import lax
from jax.experimental import pallas as pl
from jax.experimental.pallas import tpu as pltpu
from jax.sharding import PartitionSpec as P

F32 = jnp.float32
BF16 = jnp.bfloat16
VMEM = pltpu.VMEM
SMEM = pltpu.SMEM


def vspec():
    return pl.BlockSpec(memory_space=pltpu.VMEM)


def sspec():
    return pl.BlockSpec(memory_space=pltpu.SMEM)


def hspec():
    return pl.BlockSpec(memory_space=pltpu.HBM)


def aspec():
    return pl.BlockSpec(memory_space=pl.ANY)


def start_all(pairs, sems):
    copies = [
        pltpu.make_async_copy(source, target, sems.at[i])
        for i, (source, target) in enumerate(pairs)
    ]
    for copy in copies:
        copy.start()
    return copies


def params():
    return pltpu.CompilerParams(vmem_limit_bytes=12 * 1024 * 1024)


def dot(a, b):
    return jnp.dot(a, b, preferred_element_type=F32)


def project_kernel(feats_hbm, w_hbm, out_ref, feats, w, sems, *, start):
    rows = feats.shape[0]
    parts = 4
    chunk = rows // parts
    w_copy = pltpu.make_async_copy(w_hbm, w, sems.at[parts])
    w_copy.start()
    copies = [
        pltpu.make_async_copy(
            feats_hbm.at[pl.ds(start + i * chunk, chunk)],
            feats.at[pl.ds(i * chunk, chunk)],
            sems.at[i],
        )
        for i in range(parts)
    ]
    for copy in copies:
        copy.start()
    w_copy.wait()
    for i in range(parts):
        copies[i].wait()
        at = pl.ds(i * chunk, chunk)
        out_ref[at, :] = dot(feats[at, :], w[...])


def own_rows(adj, slot, core, piece):
    pairs = adj.shape[1] // (2 * piece)
    return jnp.concatenate(
        [
            adj[slot, pl.ds(pl.multiple_of((2 * y + core) * piece, piece), piece), :]
            for y in range(pairs)
        ],
        axis=0,
    )


def partial_kernel(
    core_ref, dst_any, src_any, count_any, counts_any, adj, *refs, near, far,
):
    parts = refs[:-7]
    out_ref, projected, acc, dst_ref, src_ref, count_ref, sems = refs[-7:]
    copies = start_all(
        [(dst_any, dst_ref), (src_any, src_ref), (count_any, count_ref)], sems
    )
    slots, block, _ = adj.shape
    pairs = acc.shape[0]
    piece = acc.shape[1] // (near * far)
    hidden = acc.shape[2]
    half = len(parts) // 2
    rows = parts[0].shape[0]
    acc[...] = jnp.zeros_like(acc)
    for i in range(half):
        both = parts[i][...] + parts[half + i][...]
        high = both.astype(BF16)
        at = pl.ds(i * rows, rows)
        projected[at, :hidden] = high
        projected[at, hidden:] = (both - high.astype(F32)).astype(BF16)
    for copy in copies:
        copy.wait()
    core = core_ref[0]
    count = count_ref[0]
    step = 8

    def some_slots(group, carry):
        for j in range(step):
            slot = group * step + j
            right = projected[pl.ds(pl.multiple_of(src_ref[slot] * block, block), block), :]
            result = dot(own_rows(adj, slot, core, piece), right)
            result = result[:, :hidden] + result[:, hidden:]
            result = jnp.where(slot < count, result, 0.0)
            d = dst_ref[slot]
            place = ((d % near) * far + d // near) * piece
            at = pl.ds(pl.multiple_of(place, piece), piece)
            for y in range(pairs):
                acc[y, at, :] += result[y * piece : (y + 1) * piece]
        return carry

    lax.fori_loop(0, slots // step, some_slots, 0)
    out_ref[...] = acc[...].astype(BF16).reshape(out_ref.shape)


def count_kernel(cut_ref, nbr_ref, type_ref, count_ref, *, cuts, block):
    rows, fanout = nbr_ref.shape
    cells = count_ref.shape[1]
    piece = block // cuts
    nbr = nbr_ref[...]
    within = nbr % block
    local = (nbr // block) * piece + within % piece
    per_type = cells // 4
    key = jnp.where(within // piece == cut_ref[0], type_ref[...] * per_type + local, -1)
    tile = 512
    for start in range(0, cells, tile):
        place = lax.broadcasted_iota(jnp.int32, (rows, tile), 1) + start
        total = jnp.zeros((rows, tile), F32)
        for k in range(fanout):
            total += jnp.where(key[:, k : k + 1] == place, 1.0, 0.0)
        count_ref[:, start : start + tile] = total.astype(BF16)


def state_kernel(part_ref, first_ref, own_ref, out_ref):
    total = jnp.sum(part_ref[...].astype(F32), axis=0)
    exact = jnp.tanh(total)
    first_ref[...] = exact
    states = exact.astype(BF16)
    own_ref[...] = states
    for q in range(out_ref.shape[0]):
        out_ref[q] = states


def message_kernel(count_ref, states_ref, own_ref, w_ref, out_ref):
    hidden = own_ref.shape[1]
    rows = count_ref.shape[0]
    domains, piece, _ = states_ref.shape
    local = domains * piece
    states = states_ref[...].reshape(local, hidden)
    message = jnp.zeros((rows, hidden), F32)
    for e in range(count_ref.shape[1] // local):
        picked = dot(count_ref[:, e * local : (e + 1) * local], states).astype(BF16)
        message += dot(picked, w_ref[:, e * hidden : (e + 1) * hidden])
    message = message.astype(BF16)
    for c in range(out_ref.shape[0]):
        out_ref[c, :rows] = message
        out_ref[c, rows:] = own_ref[...]


def gate_kernel(
    cut_ref, recv_ref, count_ref, grad_ref, w_edge_ref, w_in_ref, w_state_ref, w_cand_ref,
    new_ref, direct_ref, back_ref, own,
):
    rows, hidden = grad_ref.shape
    cuts = recv_ref.shape[0]
    piece = recv_ref.shape[1] - rows
    local = count_ref.shape[1] // 4
    message = jnp.sum(recv_ref[:, :rows, :].astype(F32), axis=0)
    states = recv_ref[:, rows:, :].reshape(cuts * piece, hidden)
    message_in = message.astype(BF16)
    w_in = w_in_ref[...]
    w_state = w_state_ref[...]
    w_cand = w_cand_ref[...]
    gate_in = dot(message_in, w_in)
    gate_state = dot(states, w_state)
    value = states.astype(F32)
    update = jax.nn.sigmoid(gate_in[:, :hidden] + gate_state[:, :hidden])
    reset = jax.nn.sigmoid(gate_in[:, hidden : 2 * hidden] + gate_state[:, hidden:])
    candidate = jnp.tanh(gate_in[:, 2 * hidden :] + dot((reset * value).astype(BF16), w_cand))
    new_ref[...] = ((1.0 - update) * candidate + update * value).astype(BF16)
    out_grad = grad_ref[...].astype(F32)
    cand_pre = out_grad * (1.0 - update) * (1.0 - candidate * candidate)
    update_pre = out_grad * (value - candidate) * update * (1.0 - update)
    contract = (((1,), (1,)), ((), ()))
    cand_grad = cand_pre.astype(BF16)
    reset_in = lax.dot_general(cand_grad, w_cand, contract, preferred_element_type=F32)
    reset_pre = reset_in * value * reset * (1.0 - reset)
    gates = jnp.concatenate([update_pre.astype(BF16), reset_pre.astype(BF16), cand_grad], axis=1)
    message_grad_t = lax.dot_general(w_in, gates, contract, preferred_element_type=F32).astype(BF16)
    own[...] = (
        out_grad * update
        + reset_in * reset
        + lax.dot_general(gates[:, : 2 * hidden], w_state, contract, preferred_element_type=F32)
    )
    direct_ref[...] = own[pl.ds(pl.multiple_of(cut_ref[0] * piece, piece), piece), :]
    total = jnp.zeros((hidden, local), F32)
    for e in range(count_ref.shape[1] // local):
        spread = dot(message_grad_t, count_ref[:, e * local : (e + 1) * local]).astype(BF16)
        total += dot(w_edge_ref[:, e * hidden : (e + 1) * hidden], spread)
    back_ref[...] = total.T.astype(BF16).reshape(back_ref.shape)


def grad_kernel(part_ref, direct_ref, exact_ref, out_ref):
    total = direct_ref[...] + jnp.sum(part_ref[...].astype(F32), axis=0)
    exact = exact_ref[...]
    grad = (total * (1.0 - exact * exact)).astype(BF16)
    for q in range(out_ref.shape[0]):
        out_ref[q] = grad


def spread_kernel(
    core_ref, dst_any, src_any, count_any, new_any, grads_ref, adj, out_ref, new_out,
    turned, acc, dst_ref, src_ref, count_ref, sems, *, near, far,
):
    slots, block, _ = adj.shape
    hidden = grads_ref.shape[2]
    piece = grads_ref.shape[1] // far
    pairs = grads_ref.shape[0] // near
    copies = start_all(
        [(dst_any, dst_ref), (src_any, src_ref), (count_any, count_ref), (new_any, new_out)], sems
    )
    acc[...] = jnp.zeros_like(acc)
    for z in range(far):
        for x in range(near):
            rows = jnp.concatenate(
                [grads_ref[y * near + x, z * piece : (z + 1) * piece, :] for y in range(pairs)],
                axis=0,
            )
            turned[z * near + x] = rows.T
    for copy in copies[:3]:
        copy.wait()
    core = core_ref[0]
    count = count_ref[0]
    step = 8

    def some_slots(group, carry):
        for j in range(step):
            slot = group * step + j
            result = dot(turned[dst_ref[slot]], own_rows(adj, slot, core, piece))
            acc[src_ref[slot]] += jnp.where(slot < count, result, 0.0)
        return carry

    lax.fori_loop(0, slots // step, some_slots, 0)
    for s in range(acc.shape[0]):
        out_ref[:, s * block : (s + 1) * block] = acc[s].astype(BF16)
    copies[3].wait()


def weight_kernel(spread_ref, feats_ref, out_ref):
    out_ref[...] = dot(spread_ref[...], feats_ref[...])


def weight_out_kernel(spread_ref, feats_ref, part_ref, out_ref):
    total = part_ref[...] + dot(spread_ref[...], feats_ref[...])
    out_ref[...] = total.T.astype(BF16).reshape(out_ref.shape)


def body(
    feats,
    adjacency,
    blk_dst,
    blk_src,
    blk_count,
    nbr_ids,
    edge_types,
    w_first,
    w_edge,
    w_gate_in,
    w_gate_state,
    w_cand,
    out_grad,
):
    slots, block, _ = adjacency.shape
    nodes, feat_cols = feats.shape
    hidden = w_first.shape[1]
    rows = out_grad.shape[0]
    far = lax.axis_size("z")
    near = lax.axis_size("x")
    pairs = lax.axis_size("y")
    domains = far * near
    cuts = 2 * pairs
    piece = block // cuts
    local = domains * piece
    core = lax.axis_index("core").reshape(1)
    cut = (2 * lax.axis_index("y") + lax.axis_index("core")).reshape(1)

    def over_dom(x):
        return lax.all_to_all(x, ("z", "x"), 0, 0, tiled=True)

    def over_plane(x):
        return lax.all_to_all(x, ("y", "x"), 0, 0, tiled=True)

    def over_far(x):
        return lax.all_to_all(x, "z", 0, 0, tiled=True)

    def swap(x):
        return lax.ppermute(x, "core", [(0, 1), (1, 0)])

    halves = 2
    feats_far = pltpu.with_memory_space_constraint(feats, pltpu.HBM)
    w_far = pltpu.with_memory_space_constraint(w_first, pltpu.HBM)
    rows_half = nodes // halves
    projected = [
        pl.pallas_call(
            lambda *refs, i=i: project_kernel(*refs, start=i * rows_half),
            out_shape=jax.ShapeDtypeStruct((rows_half, hidden), F32),
            in_specs=[hspec(), hspec()],
            out_specs=vspec(),
            scratch_shapes=[
                VMEM((rows_half, feat_cols), BF16),
                VMEM((feat_cols, hidden), BF16),
                pltpu.SemaphoreType.DMA((5,)),
            ],
            compiler_params=params(),
            name=f"project{i}",
        )(feats_far, w_far)
        for i in range(halves)
    ]
    swapped = [swap(p) for p in projected]
    counts = pl.pallas_call(
        lambda *refs: count_kernel(*refs, cuts=cuts, block=block),
        out_shape=jax.ShapeDtypeStruct((rows, 4 * local), BF16),
        in_specs=[sspec(), vspec(), vspec()],
        out_specs=vspec(),
        compiler_params=params(),
        name="counts",
    )(cut, nbr_ids, edge_types)
    partial = pl.pallas_call(
        lambda *refs: partial_kernel(*refs, near=near, far=far),
        out_shape=jax.ShapeDtypeStruct((pairs * near, far * piece, hidden), BF16),
        in_specs=[sspec()] + [aspec()] * 4 + [vspec()] * (1 + 2 * halves),
        out_specs=vspec(),
        scratch_shapes=[
            VMEM((nodes, 2 * hidden), BF16),
            VMEM((pairs, local, hidden), F32),
            SMEM((slots,), jnp.int32),
            SMEM((slots,), jnp.int32),
            SMEM((1,), jnp.int32),
            pltpu.SemaphoreType.DMA((3,)),
        ],
        compiler_params=params(),
        name="partial",
    )(core, blk_dst, blk_src, blk_count, counts, adjacency, *projected, *swapped)
    by_plane = jnp.sum(over_plane(partial).astype(F32), axis=0)
    by_far = over_far(by_plane.reshape(far, piece, hidden))
    spread = jax.ShapeDtypeStruct((domains, piece, hidden), BF16)
    small = jax.ShapeDtypeStruct((piece, hidden), F32)
    exact, own_states, tiled_states = pl.pallas_call(
        state_kernel,
        out_shape=(small, jax.ShapeDtypeStruct((piece, hidden), BF16), spread),
        in_specs=[vspec()],
        out_specs=(vspec(), vspec(), vspec()),
        compiler_params=params(),
        name="state",
    )(by_far)
    states = over_dom(tiled_states)
    sent = pl.pallas_call(
        message_kernel,
        out_shape=jax.ShapeDtypeStruct((cuts, rows + piece, hidden), BF16),
        in_specs=[vspec(), vspec(), vspec(), vspec()],
        out_specs=vspec(),
        compiler_params=params(),
        name="message",
    )(counts, states, own_states, w_edge)
    recv = lax.all_to_all(sent, ("y", "core"), 0, 0, tiled=True)
    new_rows, direct, back = pl.pallas_call(
        gate_kernel,
        out_shape=(jax.ShapeDtypeStruct((rows, hidden), BF16), small, spread),
        in_specs=[sspec()] + [vspec()] * 7,
        out_specs=(vspec(), vspec(), vspec()),
        scratch_shapes=[VMEM((rows, hidden), F32)],
        compiler_params=params(),
        name="gates",
    )(cut, recv, counts, out_grad, w_edge, w_gate_in, w_gate_state, w_cand)
    grad_part = over_dom(back)
    own_grad = pl.pallas_call(
        grad_kernel,
        out_shape=jax.ShapeDtypeStruct((far, piece, hidden), BF16),
        in_specs=[vspec()] * 3,
        out_specs=vspec(),
        compiler_params=params(),
        name="first_grad",
    )(grad_part, direct, exact)
    far_grads = over_far(own_grad).reshape(1, far * piece, hidden)
    grads = over_plane(jnp.broadcast_to(far_grads, (pairs * near, far * piece, hidden)))
    mine, new_state = pl.pallas_call(
        lambda *refs: spread_kernel(*refs, near=near, far=far),
        out_shape=(
            jax.ShapeDtypeStruct((hidden, nodes), BF16),
            jax.ShapeDtypeStruct((rows, hidden), BF16),
        ),
        in_specs=[sspec()] + [aspec()] * 4 + [vspec()] * 2,
        out_specs=(vspec(), aspec()),
        scratch_shapes=[
            VMEM((domains, hidden, pairs * piece), BF16),
            VMEM((nodes // block, hidden, block), F32),
            SMEM((slots,), jnp.int32),
            SMEM((slots,), jnp.int32),
            SMEM((1,), jnp.int32),
            pltpu.SemaphoreType.DMA((4,)),
        ],
        compiler_params=params(),
        name="spread",
    )(core, blk_dst, blk_src, blk_count, new_rows, grads, adjacency)
    other = swap(mine)
    own_part = pl.pallas_call(
        weight_kernel,
        out_shape=jax.ShapeDtypeStruct((hidden, feat_cols), F32),
        in_specs=[vspec()] * 2,
        out_specs=vspec(),
        compiler_params=params(),
        name="weight_own",
    )(mine, feats)
    weight_part = pl.pallas_call(
        weight_out_kernel,
        out_shape=jax.ShapeDtypeStruct((domains, feat_cols // domains, hidden), BF16),
        in_specs=[vspec()] * 3,
        out_specs=vspec(),
        compiler_params=params(),
        name="weight_all",
    )(other, feats, own_part)
    w_first_grad = jnp.sum(over_dom(weight_part).astype(F32), axis=0)
    return (new_state, w_first_grad)


def solution(mesh):
    cuts, domains = mesh.devices.shape
    fine = jax.sharding.Mesh(
        mesh.devices.reshape(cuts // 2, 2, domains // 4, 4), ("y", "core", "z", "x")
    )
    dom = ("z", "x")
    cut = ("y", "core")
    return jax.shard_map(
        body,
        mesh=fine,
        in_specs=(
            P(dom, cut),
            P(dom, None, None),
            P(dom),
            P(dom),
            P(dom),
            P(dom, None),
            P(dom, None),
            P(cut, None),
            P(),
            P(),
            P(),
            P(),
            P(dom, None),
        ),
        out_specs=(P(dom, None), P(cut + dom, None)),
        check_vma=False,
    )
```

```python
import jax
import jax.numpy as jnp
from jax import lax
from jax.experimental import pallas as pl
from jax.experimental.pallas import tpu as pltpu
from jax.sharding import PartitionSpec as P

F32 = jnp.float32
BF16 = jnp.bfloat16
VMEM = pltpu.VMEM
SMEM = pltpu.SMEM


def vspec():
    return pl.BlockSpec(memory_space=pltpu.VMEM)


def sspec():
    return pl.BlockSpec(memory_space=pltpu.SMEM)


def hspec():
    return pl.BlockSpec(memory_space=pltpu.HBM)


def aspec():
    return pl.BlockSpec(memory_space=pl.ANY)


def start_all(pairs, sems):
    copies = [
        pltpu.make_async_copy(source, target, sems.at[i])
        for i, (source, target) in enumerate(pairs)
    ]
    for copy in copies:
        copy.start()
    return copies


def params():
    return pltpu.CompilerParams(vmem_limit_bytes=12 * 1024 * 1024)


def cut_index():
    return 2 * lax.axis_index("y") + lax.axis_index("core")


def dot(a, b):
    return jnp.dot(a, b, preferred_element_type=F32)


def project_kernel(feats_hbm, w_hbm, out_ref, rest_ref, w_ref, feats, sems):
    rows, rest = feats.shape[0], rest_ref.shape[0]
    parts = 4
    chunk, rest_chunk = rows // parts, rest // parts
    copies = start_all(
        [(w_hbm, w_ref)]
        + [
            (feats_hbm.at[pl.ds(i * chunk, chunk)], feats.at[pl.ds(i * chunk, chunk)])
            for i in range(parts)
        ]
        + [
            (
                feats_hbm.at[pl.ds(rows + i * rest_chunk, rest_chunk)],
                rest_ref.at[pl.ds(i * rest_chunk, rest_chunk)],
            )
            for i in range(parts)
        ],
        sems,
    )
    copies[0].wait()
    for i in range(parts):
        copies[1 + i].wait()
        at = pl.ds(i * chunk, chunk)
        out_ref[at, :] = dot(feats[at, :], w_ref[...])
    for copy in copies[1 + parts :]:
        copy.wait()


def project_rest_kernel(rest_ref, w_ref, out_ref):
    out_ref[...] = dot(rest_ref[...], w_ref[...])


def own_rows(adj, slot, core, piece):
    pairs = adj.shape[1] // (2 * piece)
    return jnp.concatenate(
        [
            adj[slot, pl.ds(pl.multiple_of((2 * y + core) * piece, piece), piece), :]
            for y in range(pairs)
        ],
        axis=0,
    )


def partial_kernel(
    dst_any, src_any, count_any, counts_any, adj, *refs, near, far,
):
    parts = refs[:-7]
    out_ref, projected, acc, dst_ref, src_ref, count_ref, sems = refs[-7:]
    copies = start_all(
        [(dst_any, dst_ref), (src_any, src_ref), (count_any, count_ref)], sems
    )
    slots, block, _ = adj.shape
    pairs = acc.shape[0]
    piece = acc.shape[1] // (near * far)
    hidden = acc.shape[2]
    half = len(parts) // 2
    acc[...] = jnp.zeros_like(acc)
    start = 0
    for i in range(half):
        both = parts[i][...] + parts[half + i][...]
        high = both.astype(BF16)
        at = pl.ds(start, both.shape[0])
        start += both.shape[0]
        projected[at, :hidden] = high
        projected[at, hidden:] = (both - high.astype(F32)).astype(BF16)
    for copy in copies:
        copy.wait()
    core = lax.axis_index("core")
    count = count_ref[0]
    step = 8

    def some_slots(group, carry):
        for j in range(step):
            slot = group * step + j
            right = projected[pl.ds(pl.multiple_of(src_ref[slot] * block, block), block), :]
            result = dot(own_rows(adj, slot, core, piece), right)
            result = result[:, :hidden] + result[:, hidden:]
            result = jnp.where(slot < count, result, 0.0)
            d = dst_ref[slot]
            place = ((d % near) * far + d // near) * piece
            at = pl.ds(pl.multiple_of(place, piece), piece)
            for y in range(pairs):
                acc[y, at, :] += result[y * piece : (y + 1) * piece]
        return carry

    lax.fori_loop(0, slots // step, some_slots, 0)
    out_ref[...] = acc[...].astype(BF16).reshape(out_ref.shape)


def count_kernel(nbr_ref, type_ref, count_ref, *, cuts, block):
    fanout, rows = nbr_ref.shape
    cells = count_ref.shape[1]
    piece = block // cuts
    nbr = nbr_ref[...]
    within = nbr % block
    local = (nbr // block) * piece + within % piece
    per_type = cells // 4
    key = jnp.where(within // piece == cut_index(), type_ref[...] * per_type + local, -1)
    key = jnp.concatenate([key, jnp.zeros((rows - fanout, rows), jnp.int32)], axis=0).T
    tile = 512
    for start in range(0, cells, tile):
        place = lax.broadcasted_iota(jnp.int32, (rows, tile), 1) + start
        total = jnp.zeros((rows, tile), F32)
        for k in range(fanout):
            total += jnp.where(key[:, k : k + 1] == place, 1.0, 0.0)
        count_ref[:, start : start + tile] = total.astype(BF16)


def state_kernel(part_ref, first_ref, own_ref, out_ref):
    total = jnp.sum(part_ref[...].astype(F32), axis=0)
    exact = jnp.tanh(total)
    first_ref[...] = exact
    states = exact.astype(BF16)
    own_ref[...] = states
    for q in range(out_ref.shape[0]):
        out_ref[q] = states


def message_kernel(count_ref, states_ref, own_ref, w_ref, out_ref):
    hidden = own_ref.shape[1]
    rows = count_ref.shape[0]
    domains, piece, _ = states_ref.shape
    local = domains * piece
    states = states_ref[...].reshape(local, hidden)
    message = jnp.zeros((rows, hidden), F32)
    for e in range(count_ref.shape[1] // local):
        picked = dot(count_ref[:, e * local : (e + 1) * local], states).astype(BF16)
        message += dot(picked, w_ref[:, e * hidden : (e + 1) * hidden])
    message = message.astype(BF16)
    for c in range(out_ref.shape[0]):
        out_ref[c, :rows] = message
        out_ref[c, rows:] = own_ref[...]


def gate_kernel(
    recv_ref, count_ref, grad_ref, w_edge_ref, w_in_ref, w_state_ref, w_cand_ref,
    new_ref, direct_ref, back_ref, own,
):
    rows, hidden = grad_ref.shape
    cuts = recv_ref.shape[0]
    piece = recv_ref.shape[1] - rows
    local = count_ref.shape[1] // 4
    message = jnp.sum(recv_ref[:, :rows, :].astype(F32), axis=0)
    states = recv_ref[:, rows:, :].reshape(cuts * piece, hidden)
    message_in = message.astype(BF16)
    w_in = w_in_ref[...]
    w_state = w_state_ref[...]
    w_cand = w_cand_ref[...]
    gate_in = dot(message_in, w_in)
    gate_state = dot(states, w_state)
    value = states.astype(F32)
    update = jax.nn.sigmoid(gate_in[:, :hidden] + gate_state[:, :hidden])
    reset = jax.nn.sigmoid(gate_in[:, hidden : 2 * hidden] + gate_state[:, hidden:])
    candidate = jnp.tanh(gate_in[:, 2 * hidden :] + dot((reset * value).astype(BF16), w_cand))
    new_ref[...] = ((1.0 - update) * candidate + update * value).astype(BF16)
    out_grad = grad_ref[...].astype(F32)
    cand_pre = out_grad * (1.0 - update) * (1.0 - candidate * candidate)
    update_pre = out_grad * (value - candidate) * update * (1.0 - update)
    contract = (((1,), (1,)), ((), ()))
    cand_grad = cand_pre.astype(BF16)
    reset_in = lax.dot_general(cand_grad, w_cand, contract, preferred_element_type=F32)
    reset_pre = reset_in * value * reset * (1.0 - reset)
    gates = jnp.concatenate([update_pre.astype(BF16), reset_pre.astype(BF16), cand_grad], axis=1)
    message_grad_t = lax.dot_general(w_in, gates, contract, preferred_element_type=F32).astype(BF16)
    own[...] = (
        out_grad * update
        + reset_in * reset
        + lax.dot_general(gates[:, : 2 * hidden], w_state, contract, preferred_element_type=F32)
    )
    direct_ref[...] = own[pl.ds(pl.multiple_of(cut_index() * piece, piece), piece), :]
    total = jnp.zeros((hidden, local), F32)
    for e in range(count_ref.shape[1] // local):
        spread = dot(message_grad_t, count_ref[:, e * local : (e + 1) * local]).astype(BF16)
        total += dot(w_edge_ref[:, e * hidden : (e + 1) * hidden], spread)
    back_ref[...] = total.T.astype(BF16).reshape(back_ref.shape)


def grad_kernel(part_ref, direct_ref, exact_ref, out_ref):
    total = direct_ref[...] + jnp.sum(part_ref[...].astype(F32), axis=0)
    exact = exact_ref[...]
    grad = (total * (1.0 - exact * exact)).astype(BF16)
    for q in range(out_ref.shape[0]):
        out_ref[q] = grad


def spread_kernel(
    dst_any, src_any, count_any, new_any, grads_ref, adj, out_ref, new_out,
    turned, acc, dst_ref, src_ref, count_ref, sems, *, near, far,
):
    slots, block, _ = adj.shape
    hidden = grads_ref.shape[2]
    piece = grads_ref.shape[1] // far
    pairs = grads_ref.shape[0] // near
    copies = start_all(
        [(dst_any, dst_ref), (src_any, src_ref), (count_any, count_ref), (new_any, new_out)], sems
    )
    acc[...] = jnp.zeros_like(acc)
    for z in range(far):
        for x in range(near):
            rows = jnp.concatenate(
                [grads_ref[y * near + x, z * piece : (z + 1) * piece, :] for y in range(pairs)],
                axis=0,
            )
            turned[z * near + x] = rows.T
    for copy in copies[:3]:
        copy.wait()
    core = lax.axis_index("core")
    count = count_ref[0]
    step = 8

    def some_slots(group, carry):
        for j in range(step):
            slot = group * step + j
            result = dot(turned[dst_ref[slot]], own_rows(adj, slot, core, piece))
            acc[src_ref[slot]] += jnp.where(slot < count, result, 0.0)
        return carry

    lax.fori_loop(0, slots // step, some_slots, 0)
    for s in range(acc.shape[0]):
        out_ref[:, s * block : (s + 1) * block] = acc[s].astype(BF16)
    copies[3].wait()


def weight_kernel(spread_ref, feats_ref, out_ref):
    out_ref[...] = dot(spread_ref[...], feats_ref[...])


def weight_out_kernel(spread_ref, feats_ref, part_ref, out_ref):
    total = part_ref[...] + dot(spread_ref[...], feats_ref[...])
    out_ref[...] = total.T.astype(BF16).reshape(out_ref.shape)


def body(
    feats,
    adjacency,
    blk_dst,
    blk_src,
    blk_count,
    nbr_ids,
    edge_types,
    w_first,
    w_edge,
    w_gate_in,
    w_gate_state,
    w_cand,
    out_grad,
):
    slots, block, _ = adjacency.shape
    nodes, feat_cols = feats.shape
    hidden = w_first.shape[1]
    rows = out_grad.shape[0]
    far = lax.axis_size("z")
    near = lax.axis_size("x")
    pairs = lax.axis_size("y")
    domains = far * near
    cuts = 2 * pairs
    piece = block // cuts
    local = domains * piece

    def over_dom(x):
        return lax.all_to_all(x, ("z", "x"), 0, 0, tiled=True)

    def over_plane(x):
        return lax.all_to_all(x, ("y", "x"), 0, 0, tiled=True)

    def over_far(x):
        return lax.all_to_all(x, "z", 0, 0, tiled=True)

    def swap(x):
        return lax.ppermute(x, "core", [(0, 1), (1, 0)])

    first_rows = nodes // 2
    rest_rows = nodes - first_rows
    projected, rest, w = pl.pallas_call(
        project_kernel,
        out_shape=(
            jax.ShapeDtypeStruct((first_rows, hidden), F32),
            jax.ShapeDtypeStruct((rest_rows, feat_cols), BF16),
            jax.ShapeDtypeStruct((feat_cols, hidden), BF16),
        ),
        in_specs=[hspec(), hspec()],
        out_specs=(vspec(), vspec(), vspec()),
        scratch_shapes=[VMEM((first_rows, feat_cols), BF16), pltpu.SemaphoreType.DMA((9,))],
        compiler_params=params(),
        name="project",
    )(
        pltpu.with_memory_space_constraint(feats, pltpu.HBM),
        pltpu.with_memory_space_constraint(w_first, pltpu.HBM),
    )
    projected_rest = pl.pallas_call(
        project_rest_kernel,
        out_shape=jax.ShapeDtypeStruct((rest_rows, hidden), F32),
        in_specs=[vspec(), vspec()],
        out_specs=vspec(),
        compiler_params=params(),
        name="project_rest",
    )(rest, w)
    mine_parts = [projected, projected_rest]
    swapped = [swap(p) for p in mine_parts]
    counts = pl.pallas_call(
        lambda *refs: count_kernel(*refs, cuts=cuts, block=block),
        out_shape=jax.ShapeDtypeStruct((rows, 4 * local), BF16),
        in_specs=[vspec(), vspec()],
        out_specs=vspec(),
        compiler_params=params(),
        name="counts",
    )(nbr_ids.T, edge_types.T)
    partial = pl.pallas_call(
        lambda *refs: partial_kernel(*refs, near=near, far=far),
        out_shape=jax.ShapeDtypeStruct((pairs * near, far * piece, hidden), BF16),
        in_specs=[aspec()] * 4 + [vspec()] * (1 + 2 * len(mine_parts)),
        out_specs=vspec(),
        scratch_shapes=[
            VMEM((nodes, 2 * hidden), BF16),
            VMEM((pairs, local, hidden), F32),
            SMEM((slots,), jnp.int32),
            SMEM((slots,), jnp.int32),
            SMEM((1,), jnp.int32),
            pltpu.SemaphoreType.DMA((3,)),
        ],
        compiler_params=params(),
        name="partial",
    )(blk_dst, blk_src, blk_count, counts, adjacency, *mine_parts, *swapped)
    by_plane = jnp.sum(over_plane(partial).astype(F32), axis=0)
    by_far = over_far(by_plane.reshape(far, piece, hidden))
    spread = jax.ShapeDtypeStruct((domains, piece, hidden), BF16)
    small = jax.ShapeDtypeStruct((piece, hidden), F32)
    exact, own_states, tiled_states = pl.pallas_call(
        state_kernel,
        out_shape=(small, jax.ShapeDtypeStruct((piece, hidden), BF16), spread),
        in_specs=[vspec()],
        out_specs=(vspec(), vspec(), vspec()),
        compiler_params=params(),
        name="state",
    )(by_far)
    states = over_dom(tiled_states)
    sent = pl.pallas_call(
        message_kernel,
        out_shape=jax.ShapeDtypeStruct((cuts, rows + piece, hidden), BF16),
        in_specs=[vspec(), vspec(), vspec(), vspec()],
        out_specs=vspec(),
        compiler_params=params(),
        name="message",
    )(counts, states, own_states, w_edge)
    recv = lax.all_to_all(sent, ("y", "core"), 0, 0, tiled=True)
    new_rows, direct, back = pl.pallas_call(
        gate_kernel,
        out_shape=(jax.ShapeDtypeStruct((rows, hidden), BF16), small, spread),
        in_specs=[vspec()] * 7,
        out_specs=(vspec(), vspec(), vspec()),
        scratch_shapes=[VMEM((rows, hidden), F32)],
        compiler_params=params(),
        name="gates",
    )(recv, counts, out_grad, w_edge, w_gate_in, w_gate_state, w_cand)
    grad_part = over_dom(back)
    own_grad = pl.pallas_call(
        grad_kernel,
        out_shape=jax.ShapeDtypeStruct((far, piece, hidden), BF16),
        in_specs=[vspec()] * 3,
        out_specs=vspec(),
        compiler_params=params(),
        name="first_grad",
    )(grad_part, direct, exact)
    far_grads = over_far(own_grad).reshape(1, far * piece, hidden)
    grads = over_plane(jnp.broadcast_to(far_grads, (pairs * near, far * piece, hidden)))
    mine, new_state = pl.pallas_call(
        lambda *refs: spread_kernel(*refs, near=near, far=far),
        out_shape=(
            jax.ShapeDtypeStruct((hidden, nodes), BF16),
            jax.ShapeDtypeStruct((rows, hidden), BF16),
        ),
        in_specs=[aspec()] * 4 + [vspec()] * 2,
        out_specs=(vspec(), aspec()),
        scratch_shapes=[
            VMEM((domains, hidden, pairs * piece), BF16),
            VMEM((nodes // block, hidden, block), F32),
            SMEM((slots,), jnp.int32),
            SMEM((slots,), jnp.int32),
            SMEM((1,), jnp.int32),
            pltpu.SemaphoreType.DMA((4,)),
        ],
        compiler_params=params(),
        name="spread",
    )(blk_dst, blk_src, blk_count, new_rows, grads, adjacency)
    other = swap(mine)
    own_part = pl.pallas_call(
        weight_kernel,
        out_shape=jax.ShapeDtypeStruct((hidden, feat_cols), F32),
        in_specs=[vspec()] * 2,
        out_specs=vspec(),
        compiler_params=params(),
        name="weight_own",
    )(mine, feats)
    weight_part = pl.pallas_call(
        weight_out_kernel,
        out_shape=jax.ShapeDtypeStruct((domains, feat_cols // domains, hidden), BF16),
        in_specs=[vspec()] * 3,
        out_specs=vspec(),
        compiler_params=params(),
        name="weight_all",
    )(other, feats, own_part)
    w_first_grad = jnp.sum(over_dom(weight_part).astype(F32), axis=0)
    return (new_state, w_first_grad)


def solution(mesh):
    cuts, domains = mesh.devices.shape
    fine = jax.sharding.Mesh(
        mesh.devices.reshape(cuts // 2, 2, domains // 4, 4), ("y", "core", "z", "x")
    )
    dom = ("z", "x")
    cut = ("y", "core")
    return jax.shard_map(
        body,
        mesh=fine,
        in_specs=(
            P(dom, cut),
            P(dom, None, None),
            P(dom),
            P(dom),
            P(dom),
            P(dom, None),
            P(dom, None),
            P(cut, None),
            P(),
            P(),
            P(),
            P(),
            P(dom, None),
        ),
        out_specs=(P(dom, None), P(cut + dom, None)),
        check_vma=False,
    )
```

```python
import jax
import jax.numpy as jnp
from jax import lax
from jax.experimental import pallas as pl
from jax.experimental.pallas import tpu as pltpu
from jax.sharding import PartitionSpec as P

F32 = jnp.float32
BF16 = jnp.bfloat16
VMEM = pltpu.VMEM
SMEM = pltpu.SMEM


def vspec():
    return pl.BlockSpec(memory_space=pltpu.VMEM)


def sspec():
    return pl.BlockSpec(memory_space=pltpu.SMEM)


def hspec():
    return pl.BlockSpec(memory_space=pltpu.HBM)


def aspec():
    return pl.BlockSpec(memory_space=pl.ANY)


def start_all(pairs, sems):
    copies = [
        pltpu.make_async_copy(source, target, sems.at[i])
        for i, (source, target) in enumerate(pairs)
    ]
    for copy in copies:
        copy.start()
    return copies


def params():
    return pltpu.CompilerParams(vmem_limit_bytes=12 * 1024 * 1024)


def cut_index():
    return 2 * lax.axis_index("y") + lax.axis_index("core")


def dot(a, b):
    return jnp.dot(a, b, preferred_element_type=F32)


def project_kernel(feats_hbm, w_hbm, out_ref, rest_ref, w_ref, feats, sems):
    rows, rest = feats.shape[0], rest_ref.shape[0]
    parts = 4
    chunk, rest_chunk = rows // parts, rest // parts
    copies = start_all(
        [(w_hbm, w_ref)]
        + [
            (feats_hbm.at[pl.ds(i * chunk, chunk)], feats.at[pl.ds(i * chunk, chunk)])
            for i in range(parts)
        ]
        + [
            (
                feats_hbm.at[pl.ds(rows + i * rest_chunk, rest_chunk)],
                rest_ref.at[pl.ds(i * rest_chunk, rest_chunk)],
            )
            for i in range(parts)
        ],
        sems,
    )
    copies[0].wait()
    for i in range(parts):
        copies[1 + i].wait()
        at = pl.ds(i * chunk, chunk)
        out_ref[at, :] = dot(feats[at, :], w_ref[...])
    for copy in copies[1 + parts :]:
        copy.wait()


def project_rest_kernel(rest_ref, w_ref, out_ref):
    out_ref[...] = dot(rest_ref[...], w_ref[...])


def own_rows(adj, slot, core, piece):
    pairs = adj.shape[1] // (2 * piece)
    return jnp.concatenate(
        [
            adj[slot, pl.ds(pl.multiple_of((2 * y + core) * piece, piece), piece), :]
            for y in range(pairs)
        ],
        axis=0,
    )


def partial_kernel(
    dst_any, src_any, count_any, counts_any, adj, *refs, near, far,
):
    parts = refs[:-7]
    out_ref, projected, acc, dst_ref, src_ref, count_ref, sems = refs[-7:]
    copies = start_all(
        [(dst_any, dst_ref), (src_any, src_ref), (count_any, count_ref)], sems
    )
    slots, block, _ = adj.shape
    pairs = acc.shape[0]
    piece = acc.shape[1] // (near * far)
    hidden = acc.shape[2]
    half = len(parts) // 2
    acc[...] = jnp.zeros_like(acc)
    start = 0
    for i in range(half):
        both = parts[i][...] + parts[half + i][...]
        high = both.astype(BF16)
        at = pl.ds(start, both.shape[0])
        start += both.shape[0]
        projected[at, :hidden] = high
        projected[at, hidden:] = (both - high.astype(F32)).astype(BF16)
    for copy in copies:
        copy.wait()
    core = lax.axis_index("core")
    count = count_ref[0]
    step = 16

    def some_slots(group, carry):
        for j in range(step):
            slot = group * step + j
            right = projected[pl.ds(pl.multiple_of(src_ref[slot] * block, block), block), :]
            result = dot(own_rows(adj, slot, core, piece), right)
            result = result[:, :hidden] + result[:, hidden:]
            result = jnp.where(slot < count, result, 0.0)
            d = dst_ref[slot]
            place = ((d % near) * far + d // near) * piece
            at = pl.ds(pl.multiple_of(place, piece), piece)
            for y in range(pairs):
                acc[y, at, :] += result[y * piece : (y + 1) * piece]
        return carry

    lax.fori_loop(0, slots // step, some_slots, 0)
    out_ref[...] = acc[...].astype(BF16).reshape(out_ref.shape)


def count_kernel(nbr_ref, type_ref, count_ref, *, cuts, block, near, far):
    fanout, rows = nbr_ref.shape
    cells = count_ref.shape[1]
    piece = block // cuts
    nbr = nbr_ref[...]
    within = nbr % block
    owner = nbr // block
    local = ((owner % near) * far + owner // near) * piece + within % piece
    per_type = cells // 4
    key = jnp.where(within // piece == cut_index(), type_ref[...] * per_type + local, -1)
    key = jnp.concatenate([key, jnp.zeros((rows - fanout, rows), jnp.int32)], axis=0).T
    tile = 512
    for start in range(0, cells, tile):
        place = lax.broadcasted_iota(jnp.int32, (rows, tile), 1) + start
        total = jnp.zeros((rows, tile), F32)
        for k in range(fanout):
            total += jnp.where(key[:, k : k + 1] == place, 1.0, 0.0)
        count_ref[:, start : start + tile] = total.astype(BF16)


def fold_kernel(part_ref, out_ref):
    total = jnp.sum(part_ref[...].astype(F32), axis=0).astype(BF16)
    for i in range(out_ref.shape[0]):
        out_ref[i] = total


def state_kernel(part_ref, exact_ref, own_ref, out_ref):
    total = jnp.sum(part_ref[...].astype(F32), axis=0)
    exact = jnp.tanh(total)
    exact_ref[...] = exact
    states = exact.astype(BF16)
    for i in range(out_ref.shape[0]):
        out_ref[i] = states
    piece = own_ref.shape[0]
    own_ref[...] = out_ref[0, pl.ds(pl.multiple_of(lax.axis_index("z") * piece, piece), piece), :]


def message_kernel(count_ref, states_ref, own_ref, w_ref, out_ref):
    hidden = own_ref.shape[1]
    rows = count_ref.shape[0]
    local = states_ref.shape[0] * states_ref.shape[1]
    states = states_ref[...].reshape(local, hidden)
    message = jnp.zeros((rows, hidden), F32)
    for e in range(count_ref.shape[1] // local):
        picked = dot(count_ref[:, e * local : (e + 1) * local], states).astype(BF16)
        message += dot(picked, w_ref[:, e * hidden : (e + 1) * hidden])
    message = message.astype(BF16)
    for c in range(out_ref.shape[0]):
        out_ref[c, :rows] = message
        out_ref[c, rows:] = own_ref[...]


def gate_kernel(
    recv_ref, count_ref, grad_ref, w_edge_ref, w_in_ref, w_state_ref, w_cand_ref,
    new_ref, back_ref, own, spread,
):
    rows, hidden = grad_ref.shape
    cuts = recv_ref.shape[0]
    piece = recv_ref.shape[1] - rows
    local = count_ref.shape[1] // 4
    message = jnp.sum(recv_ref[:, :rows, :].astype(F32), axis=0)
    states = recv_ref[:, rows:, :].reshape(cuts * piece, hidden)
    message_in = message.astype(BF16)
    w_in = w_in_ref[...]
    w_state = w_state_ref[...]
    w_cand = w_cand_ref[...]
    gate_in = dot(message_in, w_in)
    gate_state = dot(states, w_state)
    value = states.astype(F32)
    update = jax.nn.sigmoid(gate_in[:, :hidden] + gate_state[:, :hidden])
    reset = jax.nn.sigmoid(gate_in[:, hidden : 2 * hidden] + gate_state[:, hidden:])
    candidate = jnp.tanh(gate_in[:, 2 * hidden :] + dot((reset * value).astype(BF16), w_cand))
    new_ref[...] = ((1.0 - update) * candidate + update * value).astype(BF16)
    out_grad = grad_ref[...].astype(F32)
    cand_pre = out_grad * (1.0 - update) * (1.0 - candidate * candidate)
    update_pre = out_grad * (value - candidate) * update * (1.0 - update)
    contract = (((1,), (1,)), ((), ()))
    cand_grad = cand_pre.astype(BF16)
    reset_in = lax.dot_general(cand_grad, w_cand, contract, preferred_element_type=F32)
    reset_pre = reset_in * value * reset * (1.0 - reset)
    gates = jnp.concatenate([update_pre.astype(BF16), reset_pre.astype(BF16), cand_grad], axis=1)
    message_grad_t = lax.dot_general(w_in, gates, contract, preferred_element_type=F32).astype(BF16)
    own[...] = (
        out_grad * update
        + reset_in * reset
        + lax.dot_general(gates[:, : 2 * hidden], w_state, contract, preferred_element_type=F32)
    )
    total = jnp.zeros((hidden, local), F32)
    for e in range(count_ref.shape[1] // local):
        picked = dot(message_grad_t, count_ref[:, e * local : (e + 1) * local]).astype(BF16)
        total += dot(w_edge_ref[:, e * hidden : (e + 1) * hidden], picked)
    spread[...] = total.T
    far = back_ref.shape[1] // piece
    place = (lax.axis_index("x") * far + lax.axis_index("z")) * piece
    spread[pl.ds(pl.multiple_of(place, piece), piece), :] += own[
        pl.ds(pl.multiple_of(cut_index() * piece, piece), piece), :
    ]
    back_ref[...] = spread[...].astype(BF16).reshape(back_ref.shape)


def grad_kernel(part_ref, exact_ref, out_ref):
    total = jnp.sum(part_ref[...].astype(F32), axis=0)
    exact = exact_ref[...]
    grad = (total * (1.0 - exact * exact)).astype(BF16)
    for q in range(out_ref.shape[0]):
        out_ref[q] = grad


def spread_kernel(
    dst_any, src_any, count_any, new_any, grads_ref, adj, out_ref, low_ref, new_out,
    turned, acc, dst_ref, src_ref, count_ref, sems, *, near, far,
):
    slots, block, _ = adj.shape
    hidden = grads_ref.shape[2]
    piece = grads_ref.shape[1] // far
    pairs = grads_ref.shape[0] // near
    copies = start_all(
        [(dst_any, dst_ref), (src_any, src_ref), (count_any, count_ref), (new_any, new_out)], sems
    )
    acc[...] = jnp.zeros_like(acc)
    for z in range(far):
        for x in range(near):
            rows = jnp.concatenate(
                [grads_ref[y * near + x, z * piece : (z + 1) * piece, :] for y in range(pairs)],
                axis=0,
            )
            turned[z * near + x] = rows.T
    for copy in copies[:3]:
        copy.wait()
    core = lax.axis_index("core")
    count = count_ref[0]
    step = 16

    def some_slots(group, carry):
        for j in range(step):
            slot = group * step + j
            result = dot(turned[dst_ref[slot]], own_rows(adj, slot, core, piece))
            acc[src_ref[slot]] += jnp.where(slot < count, result, 0.0)
        return carry

    lax.fori_loop(0, slots // step, some_slots, 0)
    for s in range(acc.shape[0]):
        high = acc[s].astype(BF16)
        out_ref[:, s * block : (s + 1) * block] = high
        low_ref[:, s * block : (s + 1) * block] = (acc[s] - high.astype(F32)).astype(BF16)
    copies[3].wait()


def weight_kernel(high_ref, low_ref, feats_ref, out_ref):
    hidden = high_ref.shape[0]
    both = jnp.concatenate([high_ref[...], low_ref[...]], axis=0)
    total = dot(both, feats_ref[...])
    out_ref[...] = total[:hidden] + total[hidden:]


def weight_out_kernel(spread_ref, feats_ref, part_ref, out_ref):
    total = part_ref[...] + dot(spread_ref[...], feats_ref[...])
    out_ref[...] = total.T.astype(BF16).reshape(out_ref.shape)


def body(
    feats,
    adjacency,
    blk_dst,
    blk_src,
    blk_count,
    nbr_ids,
    edge_types,
    w_first,
    w_edge,
    w_gate_in,
    w_gate_state,
    w_cand,
    out_grad,
):
    slots, block, _ = adjacency.shape
    nodes, feat_cols = feats.shape
    hidden = w_first.shape[1]
    rows = out_grad.shape[0]
    far = lax.axis_size("z")
    near = lax.axis_size("x")
    pairs = lax.axis_size("y")
    domains = far * near
    cuts = 2 * pairs
    piece = block // cuts
    local = domains * piece

    def over_dom(x):
        return lax.all_to_all(x, ("z", "x"), 0, 0, tiled=True)

    def over_plane(x):
        return lax.all_to_all(x, ("y", "x"), 0, 0, tiled=True)

    def over_near(x):
        return lax.all_to_all(x, "x", 0, 0, tiled=True)

    def over_far(x):
        return lax.all_to_all(x, "z", 0, 0, tiled=True)

    def swap(x):
        return lax.ppermute(x, "core", [(0, 1), (1, 0)])

    first_rows = nodes // 2
    rest_rows = nodes - first_rows
    projected, rest, w = pl.pallas_call(
        project_kernel,
        out_shape=(
            jax.ShapeDtypeStruct((first_rows, hidden), F32),
            jax.ShapeDtypeStruct((rest_rows, feat_cols), BF16),
            jax.ShapeDtypeStruct((feat_cols, hidden), BF16),
        ),
        in_specs=[hspec()] * 2,
        out_specs=(vspec(), vspec(), vspec()),
        scratch_shapes=[VMEM((first_rows, feat_cols), BF16), pltpu.SemaphoreType.DMA((9,))],
        compiler_params=params(),
        name="project",
    )(
        pltpu.with_memory_space_constraint(feats, pltpu.HBM),
        pltpu.with_memory_space_constraint(w_first, pltpu.HBM),
    )
    projected_rest = pl.pallas_call(
        project_rest_kernel,
        out_shape=jax.ShapeDtypeStruct((rest_rows, hidden), F32),
        in_specs=[vspec(), vspec()],
        out_specs=vspec(),
        compiler_params=params(),
        name="project_rest",
    )(rest, w)
    mine_parts = [projected, projected_rest]
    swapped = [swap(p) for p in mine_parts]
    counts = pl.pallas_call(
        lambda *refs: count_kernel(*refs, cuts=cuts, block=block, near=near, far=far),
        out_shape=jax.ShapeDtypeStruct((rows, 4 * local), BF16),
        in_specs=[vspec(), vspec()],
        out_specs=vspec(),
        compiler_params=params(),
        name="counts",
    )(nbr_ids.T, edge_types.T)
    partial = pl.pallas_call(
        lambda *refs: partial_kernel(*refs, near=near, far=far),
        out_shape=jax.ShapeDtypeStruct((pairs * near, far * piece, hidden), BF16),
        in_specs=[aspec()] * 4 + [vspec()] * (1 + 2 * len(mine_parts)),
        out_specs=vspec(),
        scratch_shapes=[
            VMEM((nodes, 2 * hidden), BF16),
            VMEM((pairs, local, hidden), F32),
            SMEM((slots,), jnp.int32),
            SMEM((slots,), jnp.int32),
            SMEM((1,), jnp.int32),
            pltpu.SemaphoreType.DMA((3,)),
        ],
        compiler_params=params(),
        name="partial",
    )(blk_dst, blk_src, blk_count, counts, adjacency, *mine_parts, *swapped)
    group = far * piece
    tiled = lambda n: jax.ShapeDtypeStruct((n, group, hidden), BF16)

    def fold(x):
        return pl.pallas_call(
            fold_kernel,
            out_shape=tiled(far),
            in_specs=[vspec()],
            out_specs=vspec(),
            compiler_params=params(),
            name="fold",
        )(x)

    by_far = over_far(fold(over_plane(partial)))
    exact, own_states, tiled_states = pl.pallas_call(
        state_kernel,
        out_shape=(
            jax.ShapeDtypeStruct((group, hidden), F32),
            jax.ShapeDtypeStruct((piece, hidden), BF16),
            tiled(near),
        ),
        in_specs=[vspec()],
        out_specs=(vspec(), vspec(), vspec()),
        compiler_params=params(),
        name="state",
    )(by_far)
    states = over_near(tiled_states)
    sent = pl.pallas_call(
        message_kernel,
        out_shape=jax.ShapeDtypeStruct((cuts, rows + piece, hidden), BF16),
        in_specs=[vspec(), vspec(), vspec(), vspec()],
        out_specs=vspec(),
        compiler_params=params(),
        name="message",
    )(counts, states, own_states, w_edge)
    recv = lax.all_to_all(sent, ("y", "core"), 0, 0, tiled=True)
    new_rows, back = pl.pallas_call(
        gate_kernel,
        out_shape=(jax.ShapeDtypeStruct((rows, hidden), BF16), tiled(near)),
        in_specs=[vspec()] * 7,
        out_specs=(vspec(), vspec()),
        scratch_shapes=[VMEM((rows, hidden), F32), VMEM((local, hidden), F32)],
        compiler_params=params(),
        name="gates",
    )(recv, counts, out_grad, w_edge, w_gate_in, w_gate_state, w_cand)
    grad_part = over_far(fold(over_near(back)))
    own_grad = pl.pallas_call(
        grad_kernel,
        out_shape=tiled(pairs * near),
        in_specs=[vspec()] * 2,
        out_specs=vspec(),
        compiler_params=params(),
        name="first_grad",
    )(grad_part, exact)
    grads = over_plane(own_grad)
    mine, mine_low, new_state = pl.pallas_call(
        lambda *refs: spread_kernel(*refs, near=near, far=far),
        out_shape=(
            jax.ShapeDtypeStruct((hidden, nodes), BF16),
            jax.ShapeDtypeStruct((hidden, nodes), BF16),
            jax.ShapeDtypeStruct((rows, hidden), BF16),
        ),
        in_specs=[aspec()] * 4 + [vspec()] * 2,
        out_specs=(vspec(), vspec(), aspec()),
        scratch_shapes=[
            VMEM((domains, hidden, pairs * piece), BF16),
            VMEM((nodes // block, hidden, block), F32),
            SMEM((slots,), jnp.int32),
            SMEM((slots,), jnp.int32),
            SMEM((1,), jnp.int32),
            pltpu.SemaphoreType.DMA((4,)),
        ],
        compiler_params=params(),
        name="spread",
    )(blk_dst, blk_src, blk_count, new_rows, grads, adjacency)
    other = swap(mine)
    own_part = pl.pallas_call(
        weight_kernel,
        out_shape=jax.ShapeDtypeStruct((hidden, feat_cols), F32),
        in_specs=[vspec()] * 3,
        out_specs=vspec(),
        compiler_params=params(),
        name="weight_own",
    )(mine, mine_low, feats)
    weight_part = pl.pallas_call(
        weight_out_kernel,
        out_shape=jax.ShapeDtypeStruct((domains, feat_cols // domains, hidden), BF16),
        in_specs=[vspec()] * 3,
        out_specs=vspec(),
        compiler_params=params(),
        name="weight_all",
    )(other, feats, own_part)
    w_first_grad = jnp.sum(over_dom(weight_part).astype(F32), axis=0)
    return (new_state, w_first_grad)


def solution(mesh):
    cuts, domains = mesh.devices.shape
    fine = jax.sharding.Mesh(
        mesh.devices.reshape(cuts // 2, 2, domains // 4, 4), ("y", "core", "z", "x")
    )
    dom = ("z", "x")
    cut = ("y", "core")
    return jax.shard_map(
        body,
        mesh=fine,
        in_specs=(
            P(dom, cut),
            P(dom, None, None),
            P(dom),
            P(dom),
            P(dom),
            P(dom, None),
            P(dom, None),
            P(cut, None),
            P(),
            P(),
            P(),
            P(),
            P(dom, None),
        ),
        out_specs=(P(dom, None), P(cut + dom, None)),
        check_vma=False,
    )
```

```python
import jax
import jax.numpy as jnp
from jax import lax
from jax.experimental import pallas as pl
from jax.experimental.pallas import tpu as pltpu
from jax.sharding import PartitionSpec as P

F32 = jnp.float32
BF16 = jnp.bfloat16
VMEM = pltpu.VMEM
SMEM = pltpu.SMEM


def vspec():
    return pl.BlockSpec(memory_space=pltpu.VMEM)


def sspec():
    return pl.BlockSpec(memory_space=pltpu.SMEM)


def hspec():
    return pl.BlockSpec(memory_space=pltpu.HBM)


def aspec():
    return pl.BlockSpec(memory_space=pl.ANY)


def start_all(pairs, sems):
    copies = [
        pltpu.make_async_copy(source, target, sems.at[i])
        for i, (source, target) in enumerate(pairs)
    ]
    for copy in copies:
        copy.start()
    return copies


def params():
    return pltpu.CompilerParams(vmem_limit_bytes=12 * 1024 * 1024)


def cut_index():
    return 2 * lax.axis_index("y") + lax.axis_index("core")


def dot(a, b):
    return jnp.dot(a, b, preferred_element_type=F32)


def project_kernel(feats_hbm, w_hbm, out_ref, rest_ref, w_ref, feats, sems):
    rows, rest = feats.shape[0], rest_ref.shape[0]
    parts = 4
    chunk, rest_chunk = rows // parts, rest // parts
    copies = start_all(
        [(w_hbm, w_ref)]
        + [
            (feats_hbm.at[pl.ds(i * chunk, chunk)], feats.at[pl.ds(i * chunk, chunk)])
            for i in range(parts)
        ]
        + [
            (
                feats_hbm.at[pl.ds(rows + i * rest_chunk, rest_chunk)],
                rest_ref.at[pl.ds(i * rest_chunk, rest_chunk)],
            )
            for i in range(parts)
        ],
        sems,
    )
    copies[0].wait()
    for i in range(parts):
        copies[1 + i].wait()
        at = pl.ds(i * chunk, chunk)
        out_ref[at, :] = dot(feats[at, :], w_ref[...])
    for copy in copies[1 + parts :]:
        copy.wait()


def project_rest_kernel(rest_ref, w_ref, out_ref):
    out_ref[...] = dot(rest_ref[...], w_ref[...])


def own_rows(adj, slot, core, piece):
    pairs = adj.shape[1] // (2 * piece)
    return jnp.concatenate(
        [
            adj[slot, pl.ds(pl.multiple_of((2 * y + core) * piece, piece), piece), :]
            for y in range(pairs)
        ],
        axis=0,
    )


def partial_kernel(
    dst_any, src_any, count_any, counts_any, adj, *refs, near, far,
):
    parts = refs[:-7]
    out_ref, projected, acc, dst_ref, src_ref, count_ref, sems = refs[-7:]
    copies = start_all(
        [(dst_any, dst_ref), (src_any, src_ref), (count_any, count_ref)], sems
    )
    slots, block, _ = adj.shape
    pairs = acc.shape[0]
    piece = acc.shape[1] // (near * far)
    hidden = acc.shape[2]
    half = len(parts) // 2
    acc[...] = jnp.zeros_like(acc)
    start = 0
    for i in range(half):
        both = parts[i][...] + parts[half + i][...]
        high = both.astype(BF16)
        at = pl.ds(start, both.shape[0])
        start += both.shape[0]
        projected[at, :hidden] = high
        projected[at, hidden:] = (both - high.astype(F32)).astype(BF16)
    for copy in copies:
        copy.wait()
    core = lax.axis_index("core")
    count = count_ref[0]
    step = 32

    def some_slots(group, carry):
        for j in range(step):
            slot = group * step + j
            right = projected[pl.ds(pl.multiple_of(src_ref[slot] * block, block), block), :]
            result = dot(own_rows(adj, slot, core, piece), right)
            result = result[:, :hidden] + result[:, hidden:]
            result = jnp.where(slot < count, result, 0.0)
            d = dst_ref[slot]
            place = ((d % near) * far + d // near) * piece
            at = pl.ds(pl.multiple_of(place, piece), piece)
            for y in range(pairs):
                acc[y, at, :] += result[y * piece : (y + 1) * piece]
        return carry

    lax.fori_loop(0, slots // step, some_slots, 0)
    out_ref[...] = acc[...].astype(BF16).reshape(out_ref.shape)


def count_kernel(
    nbr_ref, type_ref, adj_hbm, count_ref, adj_ref, sems, *, cuts, block, near, far
):
    copies = start_all([(adj_hbm, adj_ref)], sems)
    fanout, rows = nbr_ref.shape
    cells = count_ref.shape[1]
    piece = block // cuts
    nbr = nbr_ref[...]
    within = nbr % block
    owner = nbr // block
    local = ((owner % near) * far + owner // near) * piece + within % piece
    per_type = cells // 4
    key = jnp.where(within // piece == cut_index(), type_ref[...] * per_type + local, -1)
    key = jnp.concatenate([key, jnp.zeros((rows - fanout, rows), jnp.int32)], axis=0).T
    tile = 512
    for start in range(0, cells, tile):
        place = lax.broadcasted_iota(jnp.int32, (rows, tile), 1) + start
        total = jnp.zeros((rows, tile), F32)
        for k in range(fanout):
            total += jnp.where(key[:, k : k + 1] == place, 1.0, 0.0)
        count_ref[:, start : start + tile] = total.astype(BF16)
    copies[0].wait()


def fold_kernel(part_ref, out_ref):
    total = jnp.sum(part_ref[...].astype(F32), axis=0).astype(BF16)
    for i in range(out_ref.shape[0]):
        out_ref[i] = total


def state_kernel(part_ref, exact_ref, own_ref, out_ref):
    total = jnp.sum(part_ref[...].astype(F32), axis=0)
    exact = jnp.tanh(total)
    exact_ref[...] = exact
    states = exact.astype(BF16)
    for i in range(out_ref.shape[0]):
        out_ref[i] = states
    piece = own_ref.shape[0]
    own_ref[...] = out_ref[0, pl.ds(pl.multiple_of(lax.axis_index("z") * piece, piece), piece), :]


def message_kernel(count_ref, states_ref, own_ref, w_ref, out_ref):
    hidden = own_ref.shape[1]
    rows = count_ref.shape[0]
    local = states_ref.shape[0] * states_ref.shape[1]
    states = states_ref[...].reshape(local, hidden)
    message = jnp.zeros((rows, hidden), F32)
    for e in range(count_ref.shape[1] // local):
        picked = dot(count_ref[:, e * local : (e + 1) * local], states).astype(BF16)
        message += dot(picked, w_ref[:, e * hidden : (e + 1) * hidden])
    message = message.astype(BF16)
    for c in range(out_ref.shape[0]):
        out_ref[c, :rows] = message
        out_ref[c, rows:] = own_ref[...]


def gate_kernel(
    recv_ref, count_ref, grad_ref, w_edge_ref, w_in_ref, w_state_ref, w_cand_ref,
    new_ref, back_ref, own, spread,
):
    rows, hidden = grad_ref.shape
    cuts = recv_ref.shape[0]
    piece = recv_ref.shape[1] - rows
    local = count_ref.shape[1] // 4
    message = jnp.sum(recv_ref[:, :rows, :].astype(F32), axis=0)
    states = recv_ref[:, rows:, :].reshape(cuts * piece, hidden)
    message_in = message.astype(BF16)
    w_in = w_in_ref[...]
    w_state = w_state_ref[...]
    w_cand = w_cand_ref[...]
    gate_in = dot(message_in, w_in)
    gate_state = dot(states, w_state)
    value = states.astype(F32)
    update = jax.nn.sigmoid(gate_in[:, :hidden] + gate_state[:, :hidden])
    reset = jax.nn.sigmoid(gate_in[:, hidden : 2 * hidden] + gate_state[:, hidden:])
    candidate = jnp.tanh(gate_in[:, 2 * hidden :] + dot((reset * value).astype(BF16), w_cand))
    new_ref[...] = ((1.0 - update) * candidate + update * value).astype(BF16)
    out_grad = grad_ref[...].astype(F32)
    cand_pre = out_grad * (1.0 - update) * (1.0 - candidate * candidate)
    update_pre = out_grad * (value - candidate) * update * (1.0 - update)
    contract = (((1,), (1,)), ((), ()))
    cand_grad = cand_pre.astype(BF16)
    reset_in = lax.dot_general(cand_grad, w_cand, contract, preferred_element_type=F32)
    reset_pre = reset_in * value * reset * (1.0 - reset)
    gates = jnp.concatenate([update_pre.astype(BF16), reset_pre.astype(BF16), cand_grad], axis=1)
    message_grad_t = lax.dot_general(w_in, gates, contract, preferred_element_type=F32).astype(BF16)
    own[...] = (
        out_grad * update
        + reset_in * reset
        + lax.dot_general(gates[:, : 2 * hidden], w_state, contract, preferred_element_type=F32)
    )
    total = jnp.zeros((hidden, local), F32)
    for e in range(count_ref.shape[1] // local):
        picked = dot(message_grad_t, count_ref[:, e * local : (e + 1) * local]).astype(BF16)
        total += dot(w_edge_ref[:, e * hidden : (e + 1) * hidden], picked)
    spread[...] = total.T
    far = back_ref.shape[1] // piece
    place = (lax.axis_index("x") * far + lax.axis_index("z")) * piece
    spread[pl.ds(pl.multiple_of(place, piece), piece), :] += own[
        pl.ds(pl.multiple_of(cut_index() * piece, piece), piece), :
    ]
    back_ref[...] = spread[...].astype(BF16).reshape(back_ref.shape)


def grad_kernel(part_ref, exact_ref, out_ref):
    total = jnp.sum(part_ref[...].astype(F32), axis=0)
    exact = exact_ref[...]
    grad = (total * (1.0 - exact * exact)).astype(BF16)
    for q in range(out_ref.shape[0]):
        out_ref[q] = grad


def spread_kernel(
    dst_any, src_any, count_any, new_any, grads_ref, adj, out_ref, low_ref, new_out,
    turned, acc, dst_ref, src_ref, count_ref, sems, *, near, far,
):
    slots, block, _ = adj.shape
    hidden = grads_ref.shape[2]
    piece = grads_ref.shape[1] // far
    pairs = grads_ref.shape[0] // near
    copies = start_all(
        [(dst_any, dst_ref), (src_any, src_ref), (count_any, count_ref), (new_any, new_out)], sems
    )
    acc[...] = jnp.zeros_like(acc)
    for z in range(far):
        for x in range(near):
            rows = jnp.concatenate(
                [grads_ref[y * near + x, z * piece : (z + 1) * piece, :] for y in range(pairs)],
                axis=0,
            )
            turned[z * near + x] = rows.T
    for copy in copies[:3]:
        copy.wait()
    core = lax.axis_index("core")
    count = count_ref[0]
    step = 32

    def some_slots(group, carry):
        for j in range(step):
            slot = group * step + j
            result = dot(turned[dst_ref[slot]], own_rows(adj, slot, core, piece))
            acc[src_ref[slot]] += jnp.where(slot < count, result, 0.0)
        return carry

    lax.fori_loop(0, slots // step, some_slots, 0)
    for s in range(acc.shape[0]):
        high = acc[s].astype(BF16)
        out_ref[:, s * block : (s + 1) * block] = high
        low_ref[:, s * block : (s + 1) * block] = (acc[s] - high.astype(F32)).astype(BF16)
    copies[3].wait()


def weight_kernel(high_ref, low_ref, feats_ref, out_ref):
    hidden = high_ref.shape[0]
    both = jnp.concatenate([high_ref[...], low_ref[...]], axis=0)
    total = dot(both, feats_ref[...])
    out_ref[...] = total[:hidden] + total[hidden:]


def weight_out_kernel(spread_ref, feats_ref, part_ref, out_ref):
    total = part_ref[...] + dot(spread_ref[...], feats_ref[...])
    out_ref[...] = total.T.astype(BF16).reshape(out_ref.shape)


def body(
    feats,
    adjacency,
    blk_dst,
    blk_src,
    blk_count,
    nbr_ids,
    edge_types,
    w_first,
    w_edge,
    w_gate_in,
    w_gate_state,
    w_cand,
    out_grad,
):
    slots, block, _ = adjacency.shape
    nodes, feat_cols = feats.shape
    hidden = w_first.shape[1]
    rows = out_grad.shape[0]
    far = lax.axis_size("z")
    near = lax.axis_size("x")
    pairs = lax.axis_size("y")
    domains = far * near
    cuts = 2 * pairs
    piece = block // cuts
    local = domains * piece

    def over_dom(x):
        return lax.all_to_all(x, ("z", "x"), 0, 0, tiled=True)

    def over_plane(x):
        return lax.all_to_all(x, ("y", "x"), 0, 0, tiled=True)

    def over_near(x):
        return lax.all_to_all(x, "x", 0, 0, tiled=True)

    def over_far(x):
        return lax.all_to_all(x, "z", 0, 0, tiled=True)

    def swap(x):
        return lax.ppermute(x, "core", [(0, 1), (1, 0)])

    first_rows = nodes // 2
    rest_rows = nodes - first_rows
    projected, rest, w = pl.pallas_call(
        project_kernel,
        out_shape=(
            jax.ShapeDtypeStruct((first_rows, hidden), F32),
            jax.ShapeDtypeStruct((rest_rows, feat_cols), BF16),
            jax.ShapeDtypeStruct((feat_cols, hidden), BF16),
        ),
        in_specs=[hspec()] * 2,
        out_specs=(vspec(), vspec(), vspec()),
        scratch_shapes=[VMEM((first_rows, feat_cols), BF16), pltpu.SemaphoreType.DMA((9,))],
        compiler_params=params(),
        name="project",
    )(
        pltpu.with_memory_space_constraint(feats, pltpu.HBM),
        pltpu.with_memory_space_constraint(w_first, pltpu.HBM),
    )
    projected_rest = pl.pallas_call(
        project_rest_kernel,
        out_shape=jax.ShapeDtypeStruct((rest_rows, hidden), F32),
        in_specs=[vspec(), vspec()],
        out_specs=vspec(),
        compiler_params=params(),
        name="project_rest",
    )(rest, w)
    mine_parts = [projected, projected_rest]
    swapped = [swap(p) for p in mine_parts]
    counts, adj = pl.pallas_call(
        lambda *refs: count_kernel(*refs, cuts=cuts, block=block, near=near, far=far),
        out_shape=(
            jax.ShapeDtypeStruct((rows, 4 * local), BF16),
            jax.ShapeDtypeStruct(adjacency.shape, BF16),
        ),
        in_specs=[vspec(), vspec(), hspec()],
        out_specs=(vspec(), vspec()),
        scratch_shapes=[pltpu.SemaphoreType.DMA((1,))],
        compiler_params=params(),
        name="counts",
    )(nbr_ids.T, edge_types.T, pltpu.with_memory_space_constraint(adjacency, pltpu.HBM))
    partial = pl.pallas_call(
        lambda *refs: partial_kernel(*refs, near=near, far=far),
        out_shape=jax.ShapeDtypeStruct((pairs * near, far * piece, hidden), BF16),
        in_specs=[aspec()] * 4 + [vspec()] * (1 + 2 * len(mine_parts)),
        out_specs=vspec(),
        scratch_shapes=[
            VMEM((nodes, 2 * hidden), BF16),
            VMEM((pairs, local, hidden), F32),
            SMEM((slots,), jnp.int32),
            SMEM((slots,), jnp.int32),
            SMEM((1,), jnp.int32),
            pltpu.SemaphoreType.DMA((3,)),
        ],
        compiler_params=params(),
        name="partial",
    )(blk_dst, blk_src, blk_count, counts, adj, *mine_parts, *swapped)
    group = far * piece
    tiled = lambda n: jax.ShapeDtypeStruct((n, group, hidden), BF16)

    def fold(x):
        return pl.pallas_call(
            fold_kernel,
            out_shape=tiled(far),
            in_specs=[vspec()],
            out_specs=vspec(),
            compiler_params=params(),
            name="fold",
        )(x)

    by_far = over_far(fold(over_plane(partial)))
    exact, own_states, tiled_states = pl.pallas_call(
        state_kernel,
        out_shape=(
            jax.ShapeDtypeStruct((group, hidden), F32),
            jax.ShapeDtypeStruct((piece, hidden), BF16),
            tiled(near),
        ),
        in_specs=[vspec()],
        out_specs=(vspec(), vspec(), vspec()),
        compiler_params=params(),
        name="state",
    )(by_far)
    states = over_near(tiled_states)
    sent = pl.pallas_call(
        message_kernel,
        out_shape=jax.ShapeDtypeStruct((cuts, rows + piece, hidden), BF16),
        in_specs=[vspec(), vspec(), vspec(), vspec()],
        out_specs=vspec(),
        compiler_params=params(),
        name="message",
    )(counts, states, own_states, w_edge)
    recv = lax.all_to_all(sent, ("y", "core"), 0, 0, tiled=True)
    new_rows, back = pl.pallas_call(
        gate_kernel,
        out_shape=(jax.ShapeDtypeStruct((rows, hidden), BF16), tiled(near)),
        in_specs=[vspec()] * 7,
        out_specs=(vspec(), vspec()),
        scratch_shapes=[VMEM((rows, hidden), F32), VMEM((local, hidden), F32)],
        compiler_params=params(),
        name="gates",
    )(recv, counts, out_grad, w_edge, w_gate_in, w_gate_state, w_cand)
    grad_part = over_far(fold(over_near(back)))
    own_grad = pl.pallas_call(
        grad_kernel,
        out_shape=tiled(pairs * near),
        in_specs=[vspec()] * 2,
        out_specs=vspec(),
        compiler_params=params(),
        name="first_grad",
    )(grad_part, exact)
    grads = over_plane(own_grad)
    mine, mine_low, new_state = pl.pallas_call(
        lambda *refs: spread_kernel(*refs, near=near, far=far),
        out_shape=(
            jax.ShapeDtypeStruct((hidden, nodes), BF16),
            jax.ShapeDtypeStruct((hidden, nodes), BF16),
            jax.ShapeDtypeStruct((rows, hidden), BF16),
        ),
        in_specs=[aspec()] * 4 + [vspec()] * 2,
        out_specs=(vspec(), vspec(), aspec()),
        scratch_shapes=[
            VMEM((domains, hidden, pairs * piece), BF16),
            VMEM((nodes // block, hidden, block), F32),
            SMEM((slots,), jnp.int32),
            SMEM((slots,), jnp.int32),
            SMEM((1,), jnp.int32),
            pltpu.SemaphoreType.DMA((4,)),
        ],
        compiler_params=params(),
        name="spread",
    )(blk_dst, blk_src, blk_count, new_rows, grads, adj)
    other = swap(mine)
    own_part = pl.pallas_call(
        weight_kernel,
        out_shape=jax.ShapeDtypeStruct((hidden, feat_cols), F32),
        in_specs=[vspec()] * 3,
        out_specs=vspec(),
        compiler_params=params(),
        name="weight_own",
    )(mine, mine_low, feats)
    weight_part = pl.pallas_call(
        weight_out_kernel,
        out_shape=jax.ShapeDtypeStruct((domains, feat_cols // domains, hidden), BF16),
        in_specs=[vspec()] * 3,
        out_specs=vspec(),
        compiler_params=params(),
        name="weight_all",
    )(other, feats, own_part)
    w_first_grad = jnp.sum(over_dom(weight_part).astype(F32), axis=0)
    return (new_state, w_first_grad)


def solution(mesh):
    cuts, domains = mesh.devices.shape
    fine = jax.sharding.Mesh(
        mesh.devices.reshape(cuts // 2, 2, domains // 4, 4), ("y", "core", "z", "x")
    )
    dom = ("z", "x")
    cut = ("y", "core")
    return jax.shard_map(
        body,
        mesh=fine,
        in_specs=(
            P(dom, cut),
            P(dom, None, None),
            P(dom),
            P(dom),
            P(dom),
            P(dom, None),
            P(dom, None),
            P(cut, None),
            P(),
            P(),
            P(),
            P(),
            P(dom, None),
        ),
        out_specs=(P(dom, None), P(cut + dom, None)),
        check_vma=False,
    )
```

```python
import jax
import jax.numpy as jnp
from jax import lax
from jax.experimental import pallas as pl
from jax.experimental.pallas import tpu as pltpu
from jax.sharding import PartitionSpec as P

F32 = jnp.float32
BF16 = jnp.bfloat16
VMEM = pltpu.VMEM
SMEM = pltpu.SMEM


def vspec():
    return pl.BlockSpec(memory_space=pltpu.VMEM)


def sspec():
    return pl.BlockSpec(memory_space=pltpu.SMEM)


def hspec():
    return pl.BlockSpec(memory_space=pltpu.HBM)


def aspec():
    return pl.BlockSpec(memory_space=pl.ANY)


def start_all(pairs, sems):
    copies = [
        pltpu.make_async_copy(source, target, sems.at[i])
        for i, (source, target) in enumerate(pairs)
    ]
    for copy in copies:
        copy.start()
    return copies


def params():
    return pltpu.CompilerParams(vmem_limit_bytes=12 * 1024 * 1024)


def cut_index():
    return 2 * lax.axis_index("y") + lax.axis_index("core")


def dot(a, b):
    return jnp.dot(a, b, preferred_element_type=F32)


def project_kernel(feats_hbm, w_hbm, out_ref, rest_ref, w_ref, feats, sems):
    rows, rest = feats.shape[0], rest_ref.shape[0]
    parts = 4
    chunk, rest_chunk = rows // parts, rest // parts
    copies = start_all(
        [(w_hbm, w_ref)]
        + [
            (feats_hbm.at[pl.ds(i * chunk, chunk)], feats.at[pl.ds(i * chunk, chunk)])
            for i in range(parts)
        ]
        + [
            (
                feats_hbm.at[pl.ds(rows + i * rest_chunk, rest_chunk)],
                rest_ref.at[pl.ds(i * rest_chunk, rest_chunk)],
            )
            for i in range(parts)
        ],
        sems,
    )
    copies[0].wait()
    for i in range(parts):
        copies[1 + i].wait()
        at = pl.ds(i * chunk, chunk)
        out_ref[at, :] = dot(feats[at, :], w_ref[...])
    for copy in copies[1 + parts :]:
        copy.wait()


def project_rest_kernel(rest_ref, w_ref, out_ref):
    out_ref[...] = dot(rest_ref[...], w_ref[...])


def own_rows(adj, slot, core, piece):
    pairs = adj.shape[1] // (2 * piece)
    return jnp.concatenate(
        [
            adj[slot, pl.ds(pl.multiple_of((2 * y + core) * piece, piece), piece), :]
            for y in range(pairs)
        ],
        axis=0,
    )


def partial_kernel(
    dst_any, src_any, count_any, counts_any, adj, *refs, near, far,
):
    parts = refs[:-7]
    out_ref, projected, acc, dst_ref, src_ref, count_ref, sems = refs[-7:]
    copies = start_all(
        [(dst_any, dst_ref), (src_any, src_ref), (count_any, count_ref)], sems
    )
    slots, block, _ = adj.shape
    pairs = acc.shape[0]
    piece = acc.shape[1] // (near * far)
    hidden = acc.shape[2]
    half = len(parts) // 2
    acc[...] = jnp.zeros_like(acc)
    start = 0
    for i in range(half):
        both = parts[i][...] + parts[half + i][...]
        high = both.astype(BF16)
        at = pl.ds(start, both.shape[0])
        start += both.shape[0]
        projected[at, :hidden] = high
        projected[at, hidden:] = (both - high.astype(F32)).astype(BF16)
    for copy in copies:
        copy.wait()
    core = lax.axis_index("core")
    count = count_ref[0]
    step = 32

    def some_slots(group, carry):
        for j in range(step):
            slot = group * step + j
            right = projected[pl.ds(pl.multiple_of(src_ref[slot] * block, block), block), :]
            result = dot(own_rows(adj, slot, core, piece), right)
            result = result[:, :hidden] + result[:, hidden:]
            result = jnp.where(slot < count, result, 0.0)
            d = dst_ref[slot]
            place = ((d % near) * far + d // near) * piece
            at = pl.ds(pl.multiple_of(place, piece), piece)
            for y in range(pairs):
                acc[y, at, :] += result[y * piece : (y + 1) * piece]
        return carry

    lax.fori_loop(0, slots // step, some_slots, 0)
    out_ref[...] = acc[...].astype(BF16).reshape(out_ref.shape)


def count_kernel(
    nbr_ref, type_ref, adj_hbm, count_ref, adj_ref, sems, *, cuts, block, near, far
):
    copies = start_all([(adj_hbm, adj_ref)], sems)
    fanout, rows = nbr_ref.shape
    cells = count_ref.shape[0]
    types = count_ref.shape[1] // rows
    piece = block // cuts
    nbr = nbr_ref[...]
    within = nbr % block
    owner = nbr // block
    cut = within // piece
    group = ((cut // 2) * near + owner % near) * far + owner // near
    key = jnp.where(cut % 2 == lax.axis_index("core"), group * piece + within % piece, -1)
    digit = jnp.left_shift(1, 4 * type_ref[...])
    tile = 128
    for start in range(0, cells, tile):
        place = lax.broadcasted_iota(jnp.int32, (tile, rows), 0) + start
        total = jnp.zeros((tile, rows), jnp.int32)
        for k in range(fanout):
            total += jnp.where(key[k : k + 1] == place, digit[k : k + 1], 0)
        for e in range(types):
            part = jnp.bitwise_and(jnp.right_shift(total, 4 * e), 15)
            count_ref[start : start + tile, e * rows : (e + 1) * rows] = part.astype(F32).astype(BF16)
    copies[0].wait()


def fold_kernel(part_ref, out_ref):
    total = jnp.sum(part_ref[...].astype(F32), axis=0).astype(BF16)
    for i in range(out_ref.shape[0]):
        out_ref[i] = total


def state_kernel(part_ref, exact_ref, out_ref):
    total = jnp.sum(part_ref[...].astype(F32), axis=0)
    exact = jnp.tanh(total)
    exact_ref[...] = exact
    states = exact.astype(BF16)
    for i in range(out_ref.shape[0]):
        out_ref[i] = states


def message_kernel(count_ref, states_ref, w_ref, out_ref):
    planes, group, hidden = states_ref.shape
    rows = out_ref.shape[0] * 2 // 3
    near = lax.axis_size("x")
    pairs = planes // near
    piece = (out_ref.shape[0] - rows) // pairs
    turned = jnp.concatenate([states_ref[i].T for i in range(planes)], axis=1)
    picked = dot(turned, count_ref[...]).astype(BF16)
    total = jnp.zeros((hidden, rows), F32)
    for e in range(count_ref.shape[1] // rows):
        total += dot(
            w_ref[:, e * hidden : (e + 1) * hidden].T, picked[:, e * rows : (e + 1) * rows]
        )
    out_ref[:rows, :] = total
    at = pl.ds(pl.multiple_of(lax.axis_index("z") * piece, piece), piece)
    for y in range(pairs):
        own = states_ref[y * near + lax.axis_index("x"), at, :]
        out_ref[rows + y * piece : rows + (y + 1) * piece, :] = own.astype(F32)


def gate_kernel(
    mine_ref, other_ref, count_ref, grad_ref, w_edge_ref, w_in_ref, w_state_ref, w_cand_ref,
    new_ref, back_ref, own, spread, state_rows,
):
    rows, hidden = grad_ref.shape
    near, group, _ = back_ref.shape
    local = near * group
    pairs = count_ref.shape[0] // local
    piece = rows // (2 * pairs)
    core = lax.axis_index("core")
    message = (mine_ref[:rows, :] + other_ref[:rows, :]).T
    for y in range(pairs):
        source = slice(rows + y * piece, rows + (y + 1) * piece)
        at = pl.ds(pl.multiple_of((2 * y + core) * piece, piece), piece)
        state_rows[at, :] = mine_ref[source, :].astype(BF16)
        at = pl.ds(pl.multiple_of((2 * y + 1 - core) * piece, piece), piece)
        state_rows[at, :] = other_ref[source, :].astype(BF16)
    states = state_rows[...]
    message_in = message.astype(BF16)
    w_in = w_in_ref[...]
    w_state = w_state_ref[...]
    w_cand = w_cand_ref[...]
    gate_in = dot(message_in, w_in)
    gate_state = dot(states, w_state)
    value = states.astype(F32)
    update = jax.nn.sigmoid(gate_in[:, :hidden] + gate_state[:, :hidden])
    reset = jax.nn.sigmoid(gate_in[:, hidden : 2 * hidden] + gate_state[:, hidden:])
    candidate = jnp.tanh(gate_in[:, 2 * hidden :] + dot((reset * value).astype(BF16), w_cand))
    new_ref[...] = ((1.0 - update) * candidate + update * value).astype(BF16)
    out_grad = grad_ref[...].astype(F32)
    cand_pre = out_grad * (1.0 - update) * (1.0 - candidate * candidate)
    update_pre = out_grad * (value - candidate) * update * (1.0 - update)
    contract = (((1,), (1,)), ((), ()))
    cand_grad = cand_pre.astype(BF16)
    reset_in = lax.dot_general(cand_grad, w_cand, contract, preferred_element_type=F32)
    reset_pre = reset_in * value * reset * (1.0 - reset)
    gates = jnp.concatenate([update_pre.astype(BF16), reset_pre.astype(BF16), cand_grad], axis=1)
    message_grad_t = lax.dot_general(w_in, gates, contract, preferred_element_type=F32).astype(BF16)
    own[...] = (
        out_grad * update
        + reset_in * reset
        + lax.dot_general(gates[:, : 2 * hidden], w_state, contract, preferred_element_type=F32)
    )
    total = jnp.zeros((hidden, local), F32)
    mine = pl.ds(pl.multiple_of(lax.axis_index("y") * local, local), local)
    for e in range(count_ref.shape[1] // rows):
        counts = count_ref[mine, e * rows : (e + 1) * rows]
        picked = lax.dot_general(
            message_grad_t, counts, contract, preferred_element_type=F32
        ).astype(BF16)
        total += dot(w_edge_ref[:, e * hidden : (e + 1) * hidden], picked)
    spread[...] = total.T
    far = back_ref.shape[1] // piece
    place = (lax.axis_index("x") * far + lax.axis_index("z")) * piece
    spread[pl.ds(pl.multiple_of(place, piece), piece), :] += own[
        pl.ds(pl.multiple_of(cut_index() * piece, piece), piece), :
    ]
    back_ref[...] = spread[...].astype(BF16).reshape(back_ref.shape)


def grad_kernel(part_ref, exact_ref, out_ref):
    total = jnp.sum(part_ref[...].astype(F32), axis=0)
    exact = exact_ref[...]
    grad = (total * (1.0 - exact * exact)).astype(BF16)
    for q in range(out_ref.shape[0]):
        out_ref[q] = grad


def spread_kernel(
    dst_any, src_any, count_any, new_any, grads_ref, adj, out_ref, low_ref, new_out,
    turned, acc, dst_ref, src_ref, count_ref, sems, *, near, far,
):
    slots, block, _ = adj.shape
    hidden = grads_ref.shape[2]
    piece = grads_ref.shape[1] // far
    pairs = grads_ref.shape[0] // near
    copies = start_all(
        [(dst_any, dst_ref), (src_any, src_ref), (count_any, count_ref), (new_any, new_out)], sems
    )
    acc[...] = jnp.zeros_like(acc)
    for z in range(far):
        for x in range(near):
            rows = jnp.concatenate(
                [grads_ref[y * near + x, z * piece : (z + 1) * piece, :] for y in range(pairs)],
                axis=0,
            )
            turned[z * near + x] = rows.T
    for copy in copies[:3]:
        copy.wait()
    core = lax.axis_index("core")
    count = count_ref[0]
    step = 32

    def some_slots(group, carry):
        for j in range(step):
            slot = group * step + j
            result = dot(turned[dst_ref[slot]], own_rows(adj, slot, core, piece))
            acc[src_ref[slot]] += jnp.where(slot < count, result, 0.0)
        return carry

    lax.fori_loop(0, slots // step, some_slots, 0)
    for s in range(acc.shape[0]):
        high = acc[s].astype(BF16)
        out_ref[:, s * block : (s + 1) * block] = high
        low_ref[:, s * block : (s + 1) * block] = (acc[s] - high.astype(F32)).astype(BF16)
    copies[3].wait()


def weight_kernel(high_ref, low_ref, feats_ref, out_ref):
    hidden = high_ref.shape[0]
    both = jnp.concatenate([high_ref[...], low_ref[...]], axis=0)
    total = dot(both, feats_ref[...])
    out_ref[...] = total[:hidden] + total[hidden:]


def weight_out_kernel(spread_ref, feats_ref, part_ref, out_ref):
    total = part_ref[...] + dot(spread_ref[...], feats_ref[...])
    out_ref[...] = total.T.astype(BF16).reshape(out_ref.shape)


def body(
    feats,
    adjacency,
    blk_dst,
    blk_src,
    blk_count,
    nbr_ids,
    edge_types,
    w_first,
    w_edge,
    w_gate_in,
    w_gate_state,
    w_cand,
    out_grad,
):
    slots, block, _ = adjacency.shape
    nodes, feat_cols = feats.shape
    hidden = w_first.shape[1]
    rows = out_grad.shape[0]
    types = w_edge.shape[1] // hidden
    far = lax.axis_size("z")
    near = lax.axis_size("x")
    pairs = lax.axis_size("y")
    domains = far * near
    cuts = 2 * pairs
    piece = block // cuts
    local = domains * piece

    def over_dom(x):
        return lax.all_to_all(x, ("z", "x"), 0, 0, tiled=True)

    def over_plane(x):
        return lax.all_to_all(x, ("y", "x"), 0, 0, tiled=True)

    def over_near(x):
        return lax.all_to_all(x, "x", 0, 0, tiled=True)

    def over_far(x):
        return lax.all_to_all(x, "z", 0, 0, tiled=True)

    def swap(x):
        return lax.ppermute(x, "core", [(0, 1), (1, 0)])

    first_rows = nodes // 2
    rest_rows = nodes - first_rows
    projected, rest, w = pl.pallas_call(
        project_kernel,
        out_shape=(
            jax.ShapeDtypeStruct((first_rows, hidden), F32),
            jax.ShapeDtypeStruct((rest_rows, feat_cols), BF16),
            jax.ShapeDtypeStruct((feat_cols, hidden), BF16),
        ),
        in_specs=[hspec()] * 2,
        out_specs=(vspec(), vspec(), vspec()),
        scratch_shapes=[VMEM((first_rows, feat_cols), BF16), pltpu.SemaphoreType.DMA((9,))],
        compiler_params=params(),
        name="project",
    )(
        pltpu.with_memory_space_constraint(feats, pltpu.HBM),
        pltpu.with_memory_space_constraint(w_first, pltpu.HBM),
    )
    projected_rest = pl.pallas_call(
        project_rest_kernel,
        out_shape=jax.ShapeDtypeStruct((rest_rows, hidden), F32),
        in_specs=[vspec(), vspec()],
        out_specs=vspec(),
        compiler_params=params(),
        name="project_rest",
    )(rest, w)
    mine_parts = [projected, projected_rest]
    swapped = [swap(p) for p in mine_parts]
    counts, adj = pl.pallas_call(
        lambda *refs: count_kernel(*refs, cuts=cuts, block=block, near=near, far=far),
        out_shape=(
            jax.ShapeDtypeStruct((pairs * local, types * rows), BF16),
            jax.ShapeDtypeStruct(adjacency.shape, BF16),
        ),
        in_specs=[vspec(), vspec(), hspec()],
        out_specs=(vspec(), vspec()),
        scratch_shapes=[pltpu.SemaphoreType.DMA((1,))],
        compiler_params=params(),
        name="counts",
    )(nbr_ids.T, edge_types.T, pltpu.with_memory_space_constraint(adjacency, pltpu.HBM))
    partial = pl.pallas_call(
        lambda *refs: partial_kernel(*refs, near=near, far=far),
        out_shape=jax.ShapeDtypeStruct((pairs * near, far * piece, hidden), BF16),
        in_specs=[aspec()] * 4 + [vspec()] * (1 + 2 * len(mine_parts)),
        out_specs=vspec(),
        scratch_shapes=[
            VMEM((nodes, 2 * hidden), BF16),
            VMEM((pairs, local, hidden), F32),
            SMEM((slots,), jnp.int32),
            SMEM((slots,), jnp.int32),
            SMEM((1,), jnp.int32),
            pltpu.SemaphoreType.DMA((3,)),
        ],
        compiler_params=params(),
        name="partial",
    )(blk_dst, blk_src, blk_count, counts, adj, *mine_parts, *swapped)
    group = far * piece
    tiled = lambda n: jax.ShapeDtypeStruct((n, group, hidden), BF16)

    def fold(x):
        return pl.pallas_call(
            fold_kernel,
            out_shape=tiled(far),
            in_specs=[vspec()],
            out_specs=vspec(),
            compiler_params=params(),
            name="fold",
        )(x)

    by_far = over_far(fold(over_plane(partial)))
    exact, tiled_states = pl.pallas_call(
        state_kernel,
        out_shape=(jax.ShapeDtypeStruct((group, hidden), F32), tiled(pairs * near)),
        in_specs=[vspec()],
        out_specs=(vspec(), vspec()),
        compiler_params=params(),
        name="state",
    )(by_far)
    states = over_plane(tiled_states)
    half_message = pl.pallas_call(
        message_kernel,
        out_shape=jax.ShapeDtypeStruct((rows + rows // 2, hidden), F32),
        in_specs=[vspec()] * 3,
        out_specs=vspec(),
        compiler_params=params(),
        name="message",
    )(counts, states, w_edge)
    other_message = swap(half_message)
    new_rows, back = pl.pallas_call(
        gate_kernel,
        out_shape=(jax.ShapeDtypeStruct((rows, hidden), BF16), tiled(near)),
        in_specs=[vspec()] * 8,
        out_specs=(vspec(), vspec()),
        scratch_shapes=[
            VMEM((rows, hidden), F32),
            VMEM((local, hidden), F32),
            VMEM((rows, hidden), BF16),
        ],
        compiler_params=params(),
        name="gates",
    )(half_message, other_message, counts, out_grad, w_edge, w_gate_in, w_gate_state, w_cand)
    grad_part = over_far(fold(over_near(back)))
    own_grad = pl.pallas_call(
        grad_kernel,
        out_shape=tiled(pairs * near),
        in_specs=[vspec()] * 2,
        out_specs=vspec(),
        compiler_params=params(),
        name="first_grad",
    )(grad_part, exact)
    grads = over_plane(own_grad)
    mine, mine_low, new_state = pl.pallas_call(
        lambda *refs: spread_kernel(*refs, near=near, far=far),
        out_shape=(
            jax.ShapeDtypeStruct((hidden, nodes), BF16),
            jax.ShapeDtypeStruct((hidden, nodes), BF16),
            jax.ShapeDtypeStruct((rows, hidden), BF16),
        ),
        in_specs=[aspec()] * 4 + [vspec()] * 2,
        out_specs=(vspec(), vspec(), aspec()),
        scratch_shapes=[
            VMEM((domains, hidden, pairs * piece), BF16),
            VMEM((nodes // block, hidden, block), F32),
            SMEM((slots,), jnp.int32),
            SMEM((slots,), jnp.int32),
            SMEM((1,), jnp.int32),
            pltpu.SemaphoreType.DMA((4,)),
        ],
        compiler_params=params(),
        name="spread",
    )(blk_dst, blk_src, blk_count, new_rows, grads, adj)
    other = swap(mine)
    own_part = pl.pallas_call(
        weight_kernel,
        out_shape=jax.ShapeDtypeStruct((hidden, feat_cols), F32),
        in_specs=[vspec()] * 3,
        out_specs=vspec(),
        compiler_params=params(),
        name="weight_own",
    )(mine, mine_low, feats)
    weight_part = pl.pallas_call(
        weight_out_kernel,
        out_shape=jax.ShapeDtypeStruct((domains, feat_cols // domains, hidden), BF16),
        in_specs=[vspec()] * 3,
        out_specs=vspec(),
        compiler_params=params(),
        name="weight_all",
    )(other, feats, own_part)
    w_first_grad = jnp.sum(over_dom(weight_part).astype(F32), axis=0)
    return (new_state, w_first_grad)


def solution(mesh):
    cuts, domains = mesh.devices.shape
    fine = jax.sharding.Mesh(
        mesh.devices.reshape(cuts // 2, 2, domains // 4, 4), ("y", "core", "z", "x")
    )
    dom = ("z", "x")
    cut = ("y", "core")
    return jax.shard_map(
        body,
        mesh=fine,
        in_specs=(
            P(dom, cut),
            P(dom, None, None),
            P(dom),
            P(dom),
            P(dom),
            P(dom, None),
            P(dom, None),
            P(cut, None),
            P(),
            P(),
            P(),
            P(),
            P(dom, None),
        ),
        out_specs=(P(dom, None), P(cut + dom, None)),
        check_vma=False,
    )
```

```python
import jax
import jax.numpy as jnp
from jax import lax
from jax.experimental import pallas as pl
from jax.experimental.pallas import tpu as pltpu
from jax.sharding import PartitionSpec as P

F32 = jnp.float32
BF16 = jnp.bfloat16
VMEM = pltpu.VMEM
SMEM = pltpu.SMEM


def vspec():
    return pl.BlockSpec(memory_space=pltpu.VMEM)


def sspec():
    return pl.BlockSpec(memory_space=pltpu.SMEM)


def hspec():
    return pl.BlockSpec(memory_space=pltpu.HBM)


def aspec():
    return pl.BlockSpec(memory_space=pl.ANY)


def start_all(pairs, sems):
    copies = [
        pltpu.make_async_copy(source, target, sems.at[i])
        for i, (source, target) in enumerate(pairs)
    ]
    for copy in copies:
        copy.start()
    return copies


def params():
    return pltpu.CompilerParams(vmem_limit_bytes=12 * 1024 * 1024)


def cut_index():
    return 2 * lax.axis_index("y") + lax.axis_index("core")


def dot(a, b):
    return jnp.dot(a, b, preferred_element_type=F32)


def project_kernel(feats_hbm, w_hbm, out_ref, feats, w, sems):
    parts = sems.shape[0] - 1
    chunk = feats.shape[0] // parts
    places = [pl.ds(i * chunk, chunk) for i in range(parts)]
    copies = start_all(
        [(w_hbm, w)] + [(feats_hbm.at[at], feats.at[at]) for at in places], sems
    )
    copies[0].wait()
    for copy, at in zip(copies[1:], places):
        copy.wait()
        out_ref[at, :] = dot(feats[at, :], w[...])


def own_rows(adj, slot, core, piece):
    pairs = adj.shape[1] // (2 * piece)
    return jnp.concatenate(
        [
            adj[slot, pl.ds(pl.multiple_of((2 * y + core) * piece, piece), piece), :]
            for y in range(pairs)
        ],
        axis=0,
    )


def partial_kernel(
    dst_any, src_any, count_any, counts_any, adj, *refs, near, far,
):
    parts = refs[:-7]
    out_ref, projected, acc, dst_ref, src_ref, count_ref, sems = refs[-7:]
    copies = start_all(
        [(dst_any, dst_ref), (src_any, src_ref), (count_any, count_ref)], sems
    )
    slots, block, _ = adj.shape
    pairs = acc.shape[0]
    piece = acc.shape[1] // (near * far)
    hidden = acc.shape[2]
    half = len(parts) // 2
    acc[...] = jnp.zeros_like(acc)
    start = 0
    for i in range(half):
        both = parts[i][...] + parts[half + i][...]
        high = both.astype(BF16)
        at = pl.ds(start, both.shape[0])
        start += both.shape[0]
        projected[at, :hidden] = high
        projected[at, hidden:] = (both - high.astype(F32)).astype(BF16)
    for copy in copies:
        copy.wait()
    core = lax.axis_index("core")
    count = count_ref[0]
    step = 64

    def some_slots(group, carry):
        for j in range(step):
            slot = group * step + j
            right = projected[pl.ds(pl.multiple_of(src_ref[slot] * block, block), block), :]
            result = dot(own_rows(adj, slot, core, piece), right)
            result = result[:, :hidden] + result[:, hidden:]
            result = jnp.where(slot < count, result, 0.0)
            d = dst_ref[slot]
            place = ((d % near) * far + d // near) * piece
            at = pl.ds(pl.multiple_of(place, piece), piece)
            for y in range(pairs):
                acc[y, at, :] += result[y * piece : (y + 1) * piece]
        return carry

    lax.fori_loop(0, slots // step, some_slots, 0)
    out_ref[...] = acc[...].astype(BF16).reshape(out_ref.shape)


def count_kernel(
    nbr_ref, type_ref, adj_hbm, count_ref, adj_ref, sems, *, cuts, block, near, far
):
    copies = start_all([(adj_hbm, adj_ref)], sems)
    fanout, rows = nbr_ref.shape
    cells = count_ref.shape[0]
    types = count_ref.shape[1] // rows
    piece = block // cuts
    nbr = nbr_ref[...]
    within = nbr % block
    owner = nbr // block
    cut = within // piece
    group = ((cut // 2) * near + owner % near) * far + owner // near
    key = jnp.where(cut % 2 == lax.axis_index("core"), group * piece + within % piece, -1)
    digit = jnp.left_shift(1, 4 * type_ref[...])
    tile = 128
    for start in range(0, cells, tile):
        place = lax.broadcasted_iota(jnp.int32, (tile, rows), 0) + start
        total = jnp.zeros((tile, rows), jnp.int32)
        for k in range(fanout):
            total += jnp.where(key[k : k + 1] == place, digit[k : k + 1], 0)
        for e in range(types):
            part = jnp.bitwise_and(jnp.right_shift(total, 4 * e), 15)
            count_ref[start : start + tile, e * rows : (e + 1) * rows] = part.astype(F32).astype(BF16)
    copies[0].wait()


def fold_kernel(part_ref, out_ref):
    total = jnp.sum(part_ref[...].astype(F32), axis=0).astype(BF16)
    for i in range(out_ref.shape[0]):
        out_ref[i] = total


def state_kernel(part_ref, exact_ref, out_ref):
    total = jnp.sum(part_ref[...].astype(F32), axis=0)
    exact = jnp.tanh(total)
    exact_ref[...] = exact
    states = exact.astype(BF16)
    for i in range(out_ref.shape[0]):
        out_ref[i] = states


def message_kernel(count_ref, states_ref, w_ref, out_ref):
    planes, group, hidden = states_ref.shape
    rows = out_ref.shape[0] * 2 // 3
    near = lax.axis_size("x")
    pairs = planes // near
    piece = (out_ref.shape[0] - rows) // pairs
    turned = jnp.concatenate([states_ref[i].T for i in range(planes)], axis=1)
    picked = dot(turned, count_ref[...]).astype(BF16)
    total = jnp.zeros((hidden, rows), F32)
    for e in range(count_ref.shape[1] // rows):
        total += dot(
            w_ref[:, e * hidden : (e + 1) * hidden].T, picked[:, e * rows : (e + 1) * rows]
        )
    out_ref[:rows, :] = total
    at = pl.ds(pl.multiple_of(lax.axis_index("z") * piece, piece), piece)
    for y in range(pairs):
        own = states_ref[y * near + lax.axis_index("x"), at, :]
        out_ref[rows + y * piece : rows + (y + 1) * piece, :] = own.astype(F32)


def gate_kernel(
    mine_ref, other_ref, count_ref, grad_ref, w_edge_ref, w_in_ref, w_state_ref, w_cand_ref,
    new_ref, back_ref, own, spread, state_rows,
):
    rows, hidden = grad_ref.shape
    near, group, _ = back_ref.shape
    local = near * group
    pairs = count_ref.shape[0] // local
    piece = rows // (2 * pairs)
    core = lax.axis_index("core")
    message = (mine_ref[:rows, :] + other_ref[:rows, :]).T
    for y in range(pairs):
        source = slice(rows + y * piece, rows + (y + 1) * piece)
        at = pl.ds(pl.multiple_of((2 * y + core) * piece, piece), piece)
        state_rows[at, :] = mine_ref[source, :].astype(BF16)
        at = pl.ds(pl.multiple_of((2 * y + 1 - core) * piece, piece), piece)
        state_rows[at, :] = other_ref[source, :].astype(BF16)
    states = state_rows[...]
    message_in = message.astype(BF16)
    w_in = w_in_ref[...]
    w_state = w_state_ref[...]
    w_cand = w_cand_ref[...]
    gate_in = dot(message_in, w_in)
    gate_state = dot(states, w_state)
    value = states.astype(F32)
    update = jax.nn.sigmoid(gate_in[:, :hidden] + gate_state[:, :hidden])
    reset = jax.nn.sigmoid(gate_in[:, hidden : 2 * hidden] + gate_state[:, hidden:])
    candidate = jnp.tanh(gate_in[:, 2 * hidden :] + dot((reset * value).astype(BF16), w_cand))
    new_ref[...] = ((1.0 - update) * candidate + update * value).astype(BF16)
    out_grad = grad_ref[...].astype(F32)
    cand_pre = out_grad * (1.0 - update) * (1.0 - candidate * candidate)
    update_pre = out_grad * (value - candidate) * update * (1.0 - update)
    contract = (((1,), (1,)), ((), ()))
    cand_grad = cand_pre.astype(BF16)
    reset_in = lax.dot_general(cand_grad, w_cand, contract, preferred_element_type=F32)
    reset_pre = reset_in * value * reset * (1.0 - reset)
    gates = jnp.concatenate([update_pre.astype(BF16), reset_pre.astype(BF16), cand_grad], axis=1)
    message_grad_t = lax.dot_general(w_in, gates, contract, preferred_element_type=F32).astype(BF16)
    own[...] = (
        out_grad * update
        + reset_in * reset
        + lax.dot_general(gates[:, : 2 * hidden], w_state, contract, preferred_element_type=F32)
    )
    total = jnp.zeros((hidden, local), F32)
    mine = pl.ds(pl.multiple_of(lax.axis_index("y") * local, local), local)
    for e in range(count_ref.shape[1] // rows):
        counts = count_ref[mine, e * rows : (e + 1) * rows]
        picked = lax.dot_general(
            message_grad_t, counts, contract, preferred_element_type=F32
        ).astype(BF16)
        total += dot(w_edge_ref[:, e * hidden : (e + 1) * hidden], picked)
    spread[...] = total.T
    far = back_ref.shape[1] // piece
    place = (lax.axis_index("x") * far + lax.axis_index("z")) * piece
    spread[pl.ds(pl.multiple_of(place, piece), piece), :] += own[
        pl.ds(pl.multiple_of(cut_index() * piece, piece), piece), :
    ]
    back_ref[...] = spread[...].astype(BF16).reshape(back_ref.shape)


def grad_kernel(part_ref, exact_ref, out_ref):
    total = jnp.sum(part_ref[...].astype(F32), axis=0)
    exact = exact_ref[...]
    grad = (total * (1.0 - exact * exact)).astype(BF16)
    for q in range(out_ref.shape[0]):
        out_ref[q] = grad


def spread_kernel(
    dst_any, src_any, count_any, new_any, grads_ref, adj, out_ref, low_ref, new_out,
    turned, acc, dst_ref, src_ref, count_ref, sems, *, near, far,
):
    slots, block, _ = adj.shape
    hidden = grads_ref.shape[2]
    piece = grads_ref.shape[1] // far
    pairs = grads_ref.shape[0] // near
    copies = start_all(
        [(dst_any, dst_ref), (src_any, src_ref), (count_any, count_ref), (new_any, new_out)], sems
    )
    acc[...] = jnp.zeros_like(acc)
    for z in range(far):
        for x in range(near):
            rows = jnp.concatenate(
                [grads_ref[y * near + x, z * piece : (z + 1) * piece, :] for y in range(pairs)],
                axis=0,
            )
            turned[z * near + x] = rows.T
    for copy in copies[:3]:
        copy.wait()
    core = lax.axis_index("core")
    count = count_ref[0]
    step = 64

    def some_slots(group, carry):
        for j in range(step):
            slot = group * step + j
            result = dot(turned[dst_ref[slot]], own_rows(adj, slot, core, piece))
            acc[src_ref[slot]] += jnp.where(slot < count, result, 0.0)
        return carry

    lax.fori_loop(0, slots // step, some_slots, 0)
    for s in range(acc.shape[0]):
        high = acc[s].astype(BF16)
        out_ref[:, s * block : (s + 1) * block] = high
        low_ref[:, s * block : (s + 1) * block] = (acc[s] - high.astype(F32)).astype(BF16)
    copies[3].wait()


def weight_kernel(high_ref, low_ref, feats_ref, out_ref):
    hidden = high_ref.shape[0]
    both = jnp.concatenate([high_ref[...], low_ref[...]], axis=0)
    total = dot(both, feats_ref[...])
    out_ref[...] = total[:hidden] + total[hidden:]


def weight_out_kernel(spread_ref, feats_ref, part_ref, out_ref):
    total = part_ref[...] + dot(spread_ref[...], feats_ref[...])
    out_ref[...] = total.T.astype(BF16).reshape(out_ref.shape)


def body(
    feats,
    adjacency,
    blk_dst,
    blk_src,
    blk_count,
    nbr_ids,
    edge_types,
    w_first,
    w_edge,
    w_gate_in,
    w_gate_state,
    w_cand,
    out_grad,
):
    slots, block, _ = adjacency.shape
    nodes, feat_cols = feats.shape
    hidden = w_first.shape[1]
    rows = out_grad.shape[0]
    types = w_edge.shape[1] // hidden
    far = lax.axis_size("z")
    near = lax.axis_size("x")
    pairs = lax.axis_size("y")
    domains = far * near
    cuts = 2 * pairs
    piece = block // cuts
    local = domains * piece

    def over_dom(x):
        return lax.all_to_all(x, ("z", "x"), 0, 0, tiled=True)

    def over_plane(x):
        return lax.all_to_all(x, ("y", "x"), 0, 0, tiled=True)

    def over_near(x):
        return lax.all_to_all(x, "x", 0, 0, tiled=True)

    def over_far(x):
        return lax.all_to_all(x, "z", 0, 0, tiled=True)

    def swap(x):
        return lax.ppermute(x, "core", [(0, 1), (1, 0)])

    projected = pl.pallas_call(
        project_kernel,
        out_shape=jax.ShapeDtypeStruct((nodes, hidden), F32),
        in_specs=[hspec()] * 2,
        out_specs=vspec(),
        scratch_shapes=[
            VMEM((nodes, feat_cols), BF16),
            VMEM((feat_cols, hidden), BF16),
            pltpu.SemaphoreType.DMA((9,)),
        ],
        compiler_params=params(),
        name="project",
    )(
        pltpu.with_memory_space_constraint(feats, pltpu.HBM),
        pltpu.with_memory_space_constraint(w_first, pltpu.HBM),
    )
    mine_parts = [projected]
    swapped = [swap(projected)]
    counts, adj = pl.pallas_call(
        lambda *refs: count_kernel(*refs, cuts=cuts, block=block, near=near, far=far),
        out_shape=(
            jax.ShapeDtypeStruct((pairs * local, types * rows), BF16),
            jax.ShapeDtypeStruct(adjacency.shape, BF16),
        ),
        in_specs=[vspec(), vspec(), hspec()],
        out_specs=(vspec(), vspec()),
        scratch_shapes=[pltpu.SemaphoreType.DMA((1,))],
        compiler_params=params(),
        name="counts",
    )(nbr_ids.T, edge_types.T, pltpu.with_memory_space_constraint(adjacency, pltpu.HBM))
    partial = pl.pallas_call(
        lambda *refs: partial_kernel(*refs, near=near, far=far),
        out_shape=jax.ShapeDtypeStruct((pairs * near, far * piece, hidden), BF16),
        in_specs=[aspec()] * 4 + [vspec()] * (1 + 2 * len(mine_parts)),
        out_specs=vspec(),
        scratch_shapes=[
            VMEM((nodes, 2 * hidden), BF16),
            VMEM((pairs, local, hidden), F32),
            SMEM((slots,), jnp.int32),
            SMEM((slots,), jnp.int32),
            SMEM((1,), jnp.int32),
            pltpu.SemaphoreType.DMA((3,)),
        ],
        compiler_params=params(),
        name="partial",
    )(blk_dst, blk_src, blk_count, counts, adj, *mine_parts, *swapped)
    group = far * piece
    tiled = lambda n: jax.ShapeDtypeStruct((n, group, hidden), BF16)

    def fold(x):
        return pl.pallas_call(
            fold_kernel,
            out_shape=tiled(far),
            in_specs=[vspec()],
            out_specs=vspec(),
            compiler_params=params(),
            name="fold",
        )(x)

    by_far = over_far(fold(over_plane(partial)))
    exact, tiled_states = pl.pallas_call(
        state_kernel,
        out_shape=(jax.ShapeDtypeStruct((group, hidden), F32), tiled(pairs * near)),
        in_specs=[vspec()],
        out_specs=(vspec(), vspec()),
        compiler_params=params(),
        name="state",
    )(by_far)
    states = over_plane(tiled_states)
    half_message = pl.pallas_call(
        message_kernel,
        out_shape=jax.ShapeDtypeStruct((rows + rows // 2, hidden), F32),
        in_specs=[vspec()] * 3,
        out_specs=vspec(),
        compiler_params=params(),
        name="message",
    )(counts, states, w_edge)
    other_message = swap(half_message)
    new_rows, back = pl.pallas_call(
        gate_kernel,
        out_shape=(jax.ShapeDtypeStruct((rows, hidden), BF16), tiled(near)),
        in_specs=[vspec()] * 8,
        out_specs=(vspec(), vspec()),
        scratch_shapes=[
            VMEM((rows, hidden), F32),
            VMEM((local, hidden), F32),
            VMEM((rows, hidden), BF16),
        ],
        compiler_params=params(),
        name="gates",
    )(half_message, other_message, counts, out_grad, w_edge, w_gate_in, w_gate_state, w_cand)
    grad_part = over_far(fold(over_near(back)))
    own_grad = pl.pallas_call(
        grad_kernel,
        out_shape=tiled(pairs * near),
        in_specs=[vspec()] * 2,
        out_specs=vspec(),
        compiler_params=params(),
        name="first_grad",
    )(grad_part, exact)
    grads = over_plane(own_grad)
    mine, mine_low, new_state = pl.pallas_call(
        lambda *refs: spread_kernel(*refs, near=near, far=far),
        out_shape=(
            jax.ShapeDtypeStruct((hidden, nodes), BF16),
            jax.ShapeDtypeStruct((hidden, nodes), BF16),
            jax.ShapeDtypeStruct((rows, hidden), BF16),
        ),
        in_specs=[aspec()] * 4 + [vspec()] * 2,
        out_specs=(vspec(), vspec(), aspec()),
        scratch_shapes=[
            VMEM((domains, hidden, pairs * piece), BF16),
            VMEM((nodes // block, hidden, block), F32),
            SMEM((slots,), jnp.int32),
            SMEM((slots,), jnp.int32),
            SMEM((1,), jnp.int32),
            pltpu.SemaphoreType.DMA((4,)),
        ],
        compiler_params=params(),
        name="spread",
    )(blk_dst, blk_src, blk_count, new_rows, grads, adj)
    other = swap(mine)
    own_part = pl.pallas_call(
        weight_kernel,
        out_shape=jax.ShapeDtypeStruct((hidden, feat_cols), F32),
        in_specs=[vspec()] * 3,
        out_specs=vspec(),
        compiler_params=params(),
        name="weight_own",
    )(mine, mine_low, feats)
    weight_part = pl.pallas_call(
        weight_out_kernel,
        out_shape=jax.ShapeDtypeStruct((domains, feat_cols // domains, hidden), BF16),
        in_specs=[vspec()] * 3,
        out_specs=vspec(),
        compiler_params=params(),
        name="weight_all",
    )(other, feats, own_part)
    w_first_grad = jnp.sum(over_dom(weight_part).astype(F32), axis=0)
    return (new_state, w_first_grad)


def solution(mesh):
    cuts, domains = mesh.devices.shape
    fine = jax.sharding.Mesh(
        mesh.devices.reshape(cuts // 2, 2, domains // 4, 4), ("y", "core", "z", "x")
    )
    dom = ("z", "x")
    cut = ("y", "core")
    return jax.shard_map(
        body,
        mesh=fine,
        in_specs=(
            P(dom, cut),
            P(dom, None, None),
            P(dom),
            P(dom),
            P(dom),
            P(dom, None),
            P(dom, None),
            P(cut, None),
            P(),
            P(),
            P(),
            P(),
            P(dom, None),
        ),
        out_specs=(P(dom, None), P(cut + dom, None)),
        check_vma=False,
    )
```

```python
import jax
import jax.numpy as jnp
from jax import lax
from jax.experimental import pallas as pl
from jax.experimental.pallas import tpu as pltpu
from jax.sharding import PartitionSpec as P


F32 = jnp.float32
BF16 = jnp.bfloat16
VMEM = pltpu.VMEM
SMEM = pltpu.SMEM


def vspec():
    return pl.BlockSpec(memory_space=pltpu.VMEM)


def hspec():
    return pl.BlockSpec(memory_space=pltpu.HBM)


def aspec():
    return pl.BlockSpec(memory_space=pl.ANY)


def start_all(pairs, sems):
    copies = [
        pltpu.make_async_copy(source, target, sems.at[i])
        for i, (source, target) in enumerate(pairs)
    ]
    for copy in copies:
        copy.start()
    return copies


def params():
    return pltpu.CompilerParams(vmem_limit_bytes=12 * 1024 * 1024)


def cut_index():
    return 2 * lax.axis_index("y") + lax.axis_index("core")


def dot(a, b):
    return jnp.dot(a, b, preferred_element_type=F32)


def project_kernel(feats_hbm, w_hbm, out_ref, rest_ref, w_ref, feats, sems):
    rows, rest = feats.shape[0], rest_ref.shape[0]
    parts = 4
    chunk, rest_chunk = rows // parts, rest // parts
    copies = start_all(
        [(w_hbm, w_ref)]
        + [
            (feats_hbm.at[pl.ds(i * chunk, chunk)], feats.at[pl.ds(i * chunk, chunk)])
            for i in range(parts)
        ]
        + [
            (
                feats_hbm.at[pl.ds(rows + i * rest_chunk, rest_chunk)],
                rest_ref.at[pl.ds(i * rest_chunk, rest_chunk)],
            )
            for i in range(parts)
        ],
        sems,
    )
    copies[0].wait()
    for i in range(parts):
        copies[1 + i].wait()
        at = pl.ds(i * chunk, chunk)
        out_ref[at, :] = dot(feats[at, :], w_ref[...])
    for copy in copies[1 + parts :]:
        copy.wait()


def project_rest_kernel(rest_ref, w_ref, out_ref):
    out_ref[...] = dot(rest_ref[...], w_ref[...])


def own_rows(adj, slot, core, piece):
    pairs = adj.shape[1] // (2 * piece)
    return jnp.concatenate(
        [
            adj[slot, pl.ds(pl.multiple_of((2 * y + core) * piece, piece), piece), :]
            for y in range(pairs)
        ],
        axis=0,
    )


def partial_kernel(
    dst_any, src_any, count_any, counts_any, adj, *refs, near, far,
):
    parts = refs[:-7]
    out_ref, projected, acc, dst_ref, src_ref, count_ref, sems = refs[-7:]
    copies = start_all(
        [(dst_any, dst_ref), (src_any, src_ref), (count_any, count_ref)], sems
    )
    slots, block, _ = adj.shape
    pairs = acc.shape[0]
    piece = acc.shape[1] // (near * far)
    hidden = acc.shape[2]
    half = len(parts) // 2
    acc[...] = jnp.zeros_like(acc)
    start = 0
    for i in range(half):
        both = parts[i][...] + parts[half + i][...]
        high = both.astype(BF16)
        at = pl.ds(start, both.shape[0])
        start += both.shape[0]
        projected[at, :hidden] = high
        projected[at, hidden:] = (both - high.astype(F32)).astype(BF16)
    for copy in copies:
        copy.wait()
    core = lax.axis_index("core")
    count = count_ref[0]
    step = 64

    def some_slots(group, carry):
        for j in range(step):
            slot = group * step + j
            right = projected[pl.ds(pl.multiple_of(src_ref[slot] * block, block), block), :]
            result = dot(own_rows(adj, slot, core, piece), right)
            result = result[:, :hidden] + result[:, hidden:]
            result = jnp.where(slot < count, result, 0.0)
            d = dst_ref[slot]
            place = ((d % near) * far + d // near) * piece
            at = pl.ds(pl.multiple_of(place, piece), piece)
            for y in range(pairs):
                acc[y, at, :] += result[y * piece : (y + 1) * piece]
        return carry

    lax.fori_loop(0, slots // step, some_slots, 0)
    out_ref[...] = acc[...].astype(BF16).reshape(out_ref.shape)


def count_kernel(
    nbr_ref, type_ref, count_ref, *, cuts, block, near, far
):
    fanout, rows = nbr_ref.shape
    cells = count_ref.shape[0]
    types = count_ref.shape[1] // rows
    piece = block // cuts
    nbr = nbr_ref[...]
    within = nbr % block
    owner = nbr // block
    cut = within // piece
    group = ((cut // 2) * near + owner % near) * far + owner // near
    key = jnp.where(cut % 2 == lax.axis_index("core"), group * piece + within % piece, -1)
    digit = jnp.left_shift(1, 4 * type_ref[...])
    tile = 128
    for start in range(0, cells, tile):
        place = lax.broadcasted_iota(jnp.int32, (tile, rows), 0) + start
        total = jnp.zeros((tile, rows), jnp.int32)
        for k in range(fanout):
            total += jnp.where(key[k : k + 1] == place, digit[k : k + 1], 0)
        for e in range(types):
            part = jnp.bitwise_and(jnp.right_shift(total, 4 * e), 15)
            count_ref[start : start + tile, e * rows : (e + 1) * rows] = part.astype(F32).astype(BF16)


def fold_kernel(part_ref, out_ref):
    total = jnp.sum(part_ref[...].astype(F32), axis=0).astype(BF16)
    for i in range(out_ref.shape[0]):
        out_ref[i] = total


def state_kernel(part_ref, exact_ref, out_ref):
    total = jnp.sum(part_ref[...].astype(F32), axis=0)
    exact = jnp.tanh(total)
    exact_ref[...] = exact
    states = exact.astype(BF16)
    for i in range(out_ref.shape[0]):
        out_ref[i] = states


def message_kernel(count_ref, states_ref, w_ref, out_ref):
    planes, _, hidden = states_ref.shape
    rows = out_ref.shape[0] * 2 // 3
    near = lax.axis_size("x")
    pairs = planes // near
    piece = (out_ref.shape[0] - rows) // pairs
    turned = jnp.concatenate([states_ref[i].T for i in range(planes)], axis=1)
    picked = dot(turned, count_ref[...]).astype(BF16)
    total = jnp.zeros((hidden, rows), F32)
    for e in range(count_ref.shape[1] // rows):
        total += dot(
            w_ref[:, e * hidden : (e + 1) * hidden].T, picked[:, e * rows : (e + 1) * rows]
        )
    out_ref[:rows, :] = total
    at = pl.ds(pl.multiple_of(lax.axis_index("z") * piece, piece), piece)
    for y in range(pairs):
        own = states_ref[y * near + lax.axis_index("x"), at, :]
        out_ref[rows + y * piece : rows + (y + 1) * piece, :] = own.astype(F32)


def gate_kernel(
    mine_ref, other_ref, count_ref, grad_ref, w_edge_ref, w_in_ref, w_state_ref, w_cand_ref,
    new_ref, back_ref, own, spread, state_rows,
):
    rows, hidden = grad_ref.shape
    near, group, _ = back_ref.shape
    local = near * group
    pairs = count_ref.shape[0] // local
    piece = rows // (2 * pairs)
    core = lax.axis_index("core")
    message = (mine_ref[:rows, :] + other_ref[:rows, :]).T
    for y in range(pairs):
        source = slice(rows + y * piece, rows + (y + 1) * piece)
        at = pl.ds(pl.multiple_of((2 * y + core) * piece, piece), piece)
        state_rows[at, :] = mine_ref[source, :].astype(BF16)
        at = pl.ds(pl.multiple_of((2 * y + 1 - core) * piece, piece), piece)
        state_rows[at, :] = other_ref[source, :].astype(BF16)
    states = state_rows[...]
    message_in = message.astype(BF16)
    w_in = w_in_ref[...]
    w_state = w_state_ref[...]
    w_cand = w_cand_ref[...]
    gate_in = dot(message_in, w_in)
    gate_state = dot(states, w_state)
    value = states.astype(F32)
    update = jax.nn.sigmoid(gate_in[:, :hidden] + gate_state[:, :hidden])
    reset = jax.nn.sigmoid(gate_in[:, hidden : 2 * hidden] + gate_state[:, hidden:])
    candidate = jnp.tanh(gate_in[:, 2 * hidden :] + dot((reset * value).astype(BF16), w_cand))
    new_ref[...] = ((1.0 - update) * candidate + update * value).astype(BF16)
    out_grad = grad_ref[...].astype(F32)
    cand_pre = out_grad * (1.0 - update) * (1.0 - candidate * candidate)
    update_pre = out_grad * (value - candidate) * update * (1.0 - update)
    contract = (((1,), (1,)), ((), ()))
    cand_grad = cand_pre.astype(BF16)
    reset_in = lax.dot_general(cand_grad, w_cand, contract, preferred_element_type=F32)
    reset_pre = reset_in * value * reset * (1.0 - reset)
    gates = jnp.concatenate([update_pre.astype(BF16), reset_pre.astype(BF16), cand_grad], axis=1)
    message_grad_t = lax.dot_general(w_in, gates, contract, preferred_element_type=F32).astype(BF16)
    own[...] = (
        out_grad * update
        + reset_in * reset
        + lax.dot_general(gates[:, : 2 * hidden], w_state, contract, preferred_element_type=F32)
    )
    total = jnp.zeros((hidden, local), F32)
    mine = pl.ds(pl.multiple_of(lax.axis_index("y") * local, local), local)
    for e in range(count_ref.shape[1] // rows):
        counts = count_ref[mine, e * rows : (e + 1) * rows]
        picked = lax.dot_general(
            message_grad_t, counts, contract, preferred_element_type=F32
        ).astype(BF16)
        total += dot(w_edge_ref[:, e * hidden : (e + 1) * hidden], picked)
    spread[...] = total.T
    far = back_ref.shape[1] // piece
    place = (lax.axis_index("x") * far + lax.axis_index("z")) * piece
    spread[pl.ds(pl.multiple_of(place, piece), piece), :] += own[
        pl.ds(pl.multiple_of(cut_index() * piece, piece), piece), :
    ]
    back_ref[...] = spread[...].astype(BF16).reshape(back_ref.shape)


def grad_kernel(part_ref, exact_ref, out_ref):
    total = jnp.sum(part_ref[...].astype(F32), axis=0)
    exact = exact_ref[...]
    grad = (total * (1.0 - exact * exact)).astype(BF16)
    for q in range(out_ref.shape[0]):
        out_ref[q] = grad


def spread_kernel(
    dst_any, src_any, count_any, new_any, grads_ref, adj, out_ref, low_ref, new_out,
    turned, acc, dst_ref, src_ref, count_ref, sems, *, near, far,
):
    slots, block, _ = adj.shape
    piece = grads_ref.shape[1] // far
    pairs = grads_ref.shape[0] // near
    copies = start_all(
        [(dst_any, dst_ref), (src_any, src_ref), (count_any, count_ref), (new_any, new_out)], sems
    )
    acc[...] = jnp.zeros_like(acc)
    for z in range(far):
        for x in range(near):
            rows = jnp.concatenate(
                [grads_ref[y * near + x, z * piece : (z + 1) * piece, :] for y in range(pairs)],
                axis=0,
            )
            turned[z * near + x] = rows.T
    for copy in copies[:3]:
        copy.wait()
    core = lax.axis_index("core")
    count = count_ref[0]
    step = 64

    def some_slots(group, carry):
        for j in range(step):
            slot = group * step + j
            result = dot(turned[dst_ref[slot]], own_rows(adj, slot, core, piece))
            acc[src_ref[slot]] += jnp.where(slot < count, result, 0.0)
        return carry

    lax.fori_loop(0, slots // step, some_slots, 0)
    for s in range(acc.shape[0]):
        high = acc[s].astype(BF16)
        out_ref[:, s * block : (s + 1) * block] = high
        low_ref[:, s * block : (s + 1) * block] = (acc[s] - high.astype(F32)).astype(BF16)
    copies[3].wait()


def weight_kernel(high_ref, low_ref, feats_ref, out_ref):
    hidden = high_ref.shape[0]
    both = jnp.concatenate([high_ref[...], low_ref[...]], axis=0)
    total = dot(both, feats_ref[...])
    out_ref[...] = total[:hidden] + total[hidden:]


def weight_out_kernel(spread_ref, feats_ref, part_ref, out_ref):
    total = part_ref[...] + dot(spread_ref[...], feats_ref[...])
    out_ref[...] = total.T.astype(BF16).reshape(out_ref.shape)


def body(
    feats,
    adjacency,
    blk_dst,
    blk_src,
    blk_count,
    nbr_ids,
    edge_types,
    w_first,
    w_edge,
    w_gate_in,
    w_gate_state,
    w_cand,
    out_grad,
):
    slots, block, _ = adjacency.shape
    nodes, feat_cols = feats.shape
    hidden = w_first.shape[1]
    rows = out_grad.shape[0]
    types = w_edge.shape[1] // hidden
    far = lax.axis_size("z")
    near = lax.axis_size("x")
    pairs = lax.axis_size("y")
    domains = far * near
    cuts = 2 * pairs
    piece = block // cuts
    local = domains * piece

    def over_dom(x):
        return lax.all_to_all(x, ("z", "x"), 0, 0, tiled=True)

    def over_plane(x):
        return lax.all_to_all(x, ("y", "x"), 0, 0, tiled=True)

    def over_near(x):
        return lax.all_to_all(x, "x", 0, 0, tiled=True)

    def over_far(x):
        return lax.all_to_all(x, "z", 0, 0, tiled=True)

    def swap(x):
        return lax.ppermute(x, "core", [(0, 1), (1, 0)])

    first_rows = nodes // 2
    rest_rows = nodes - first_rows
    projected, rest, w = pl.pallas_call(
        project_kernel,
        out_shape=(
            jax.ShapeDtypeStruct((first_rows, hidden), F32),
            jax.ShapeDtypeStruct((rest_rows, feat_cols), BF16),
            jax.ShapeDtypeStruct((feat_cols, hidden), BF16),
        ),
        in_specs=[hspec()] * 2,
        out_specs=(vspec(), vspec(), vspec()),
        scratch_shapes=[VMEM((first_rows, feat_cols), BF16), pltpu.SemaphoreType.DMA((9,))],
        compiler_params=params(),
        name="project",
    )(
        pltpu.with_memory_space_constraint(feats, pltpu.HBM),
        pltpu.with_memory_space_constraint(w_first, pltpu.HBM),
    )
    projected_rest = pl.pallas_call(
        project_rest_kernel,
        out_shape=jax.ShapeDtypeStruct((rest_rows, hidden), F32),
        in_specs=[vspec(), vspec()],
        out_specs=vspec(),
        compiler_params=params(),
        name="project_rest",
    )(rest, w)
    mine_parts = [projected, projected_rest]
    swapped = []
    for part in mine_parts:
        swapped.append(swap(part))
    counts = pl.pallas_call(
        lambda *refs: count_kernel(*refs, cuts=cuts, block=block, near=near, far=far),
        out_shape=jax.ShapeDtypeStruct((pairs * local, types * rows), BF16),
        in_specs=[vspec(), vspec()],
        out_specs=vspec(),
        compiler_params=params(),
        name="counts",
    )(nbr_ids.T, edge_types.T)
    partial = pl.pallas_call(
        lambda *refs: partial_kernel(*refs, near=near, far=far),
        out_shape=jax.ShapeDtypeStruct((pairs * near, far * piece, hidden), BF16),
        in_specs=[aspec()] * 4 + [vspec()] * (1 + 2 * len(mine_parts)),
        out_specs=vspec(),
        scratch_shapes=[
            VMEM((nodes, 2 * hidden), BF16),
            VMEM((pairs, local, hidden), F32),
            SMEM((slots,), jnp.int32),
            SMEM((slots,), jnp.int32),
            SMEM((1,), jnp.int32),
            pltpu.SemaphoreType.DMA((3,)),
        ],
        compiler_params=params(),
        name="partial",
    )(blk_dst, blk_src, blk_count, counts, adjacency, *mine_parts, *swapped)
    group = far * piece
    tiled = lambda n: jax.ShapeDtypeStruct((n, group, hidden), BF16)

    def fold(x):
        return pl.pallas_call(
            fold_kernel,
            out_shape=tiled(far),
            in_specs=[vspec()],
            out_specs=vspec(),
            compiler_params=params(),
            name="fold",
        )(x)

    by_far = over_far(fold(over_plane(partial)))
    exact, tiled_states = pl.pallas_call(
        state_kernel,
        out_shape=(jax.ShapeDtypeStruct((group, hidden), F32), tiled(pairs * near)),
        in_specs=[vspec()],
        out_specs=(vspec(), vspec()),
        compiler_params=params(),
        name="state",
    )(by_far)
    states = over_plane(tiled_states)
    half_message = pl.pallas_call(
        message_kernel,
        out_shape=jax.ShapeDtypeStruct((rows + rows // 2, hidden), F32),
        in_specs=[vspec()] * 3,
        out_specs=vspec(),
        compiler_params=params(),
        name="message",
    )(counts, states, w_edge)
    other_message = swap(half_message)
    new_rows, back = pl.pallas_call(
        gate_kernel,
        out_shape=(jax.ShapeDtypeStruct((rows, hidden), BF16), tiled(near)),
        in_specs=[vspec()] * 8,
        out_specs=(vspec(), vspec()),
        scratch_shapes=[
            VMEM((rows, hidden), F32),
            VMEM((local, hidden), F32),
            VMEM((rows, hidden), BF16),
        ],
        compiler_params=params(),
        name="gates",
    )(half_message, other_message, counts, out_grad, w_edge, w_gate_in, w_gate_state, w_cand)
    grad_part = over_far(fold(over_near(back)))
    own_grad = pl.pallas_call(
        grad_kernel,
        out_shape=tiled(pairs * near),
        in_specs=[vspec()] * 2,
        out_specs=vspec(),
        compiler_params=params(),
        name="first_grad",
    )(grad_part, exact)
    grads = over_plane(own_grad)
    mine, mine_low, new_state = pl.pallas_call(
        lambda *refs: spread_kernel(*refs, near=near, far=far),
        out_shape=(
            jax.ShapeDtypeStruct((hidden, nodes), BF16),
            jax.ShapeDtypeStruct((hidden, nodes), BF16),
            jax.ShapeDtypeStruct((rows, hidden), BF16),
        ),
        in_specs=[aspec()] * 4 + [vspec()] * 2,
        out_specs=(vspec(), vspec(), aspec()),
        scratch_shapes=[
            VMEM((domains, hidden, pairs * piece), BF16),
            VMEM((nodes // block, hidden, block), F32),
            SMEM((slots,), jnp.int32),
            SMEM((slots,), jnp.int32),
            SMEM((1,), jnp.int32),
            pltpu.SemaphoreType.DMA((4,)),
        ],
        compiler_params=params(),
        name="spread",
    )(blk_dst, blk_src, blk_count, new_rows, grads, adjacency)
    other = swap(mine)
    own_part = pl.pallas_call(
        weight_kernel,
        out_shape=jax.ShapeDtypeStruct((hidden, feat_cols), F32),
        in_specs=[vspec()] * 3,
        out_specs=vspec(),
        compiler_params=params(),
        name="weight_own",
    )(mine, mine_low, feats)
    weight_part = pl.pallas_call(
        weight_out_kernel,
        out_shape=jax.ShapeDtypeStruct((domains, feat_cols // domains, hidden), BF16),
        in_specs=[vspec()] * 3,
        out_specs=vspec(),
        compiler_params=params(),
        name="weight_all",
    )(other, feats, own_part)
    w_first_grad = jnp.sum(over_dom(weight_part).astype(F32), axis=0)
    return (new_state, w_first_grad)


def solution(mesh):
    cuts, domains = mesh.devices.shape
    fine = jax.sharding.Mesh(
        mesh.devices.reshape(cuts // 2, 2, domains // 4, 4), ("y", "core", "z", "x")
    )
    dom = ("z", "x")
    cut = ("y", "core")

    return jax.shard_map(
        body,
        mesh=fine,
        in_specs=(
            P(dom, cut),
            P(dom, None, None),
            P(dom),
            P(dom),
            P(dom),
            P(dom, None),
            P(dom, None),
            P(cut, None),
            P(),
            P(),
            P(),
            P(),
            P(dom, None),
        ),
        out_specs=(P(dom, None), P(cut + dom, None)),
        check_vma=False,
    )
```

```python
import jax
import jax.numpy as jnp
from jax import lax
from jax.experimental import pallas as pl
from jax.experimental.pallas import tpu as pltpu
from jax.sharding import PartitionSpec as P


F32 = jnp.float32
BF16 = jnp.bfloat16
VMEM = pltpu.VMEM
SMEM = pltpu.SMEM


def vspec():
    return pl.BlockSpec(memory_space=pltpu.VMEM)


def hspec():
    return pl.BlockSpec(memory_space=pltpu.HBM)


def aspec():
    return pl.BlockSpec(memory_space=pl.ANY)


def start_all(pairs, sems):
    copies = [
        pltpu.make_async_copy(source, target, sems.at[i])
        for i, (source, target) in enumerate(pairs)
    ]
    for copy in copies:
        copy.start()
    return copies


def params():
    return pltpu.CompilerParams(vmem_limit_bytes=12 * 1024 * 1024)


def cut_index():
    return 2 * lax.axis_index("y") + lax.axis_index("core")


def dot(a, b):
    return jnp.dot(a, b, preferred_element_type=F32)


def project_kernel(feats_hbm, w_hbm, out_ref, rest_ref, w_ref, feats, sems):
    rows, rest = feats.shape[0], rest_ref.shape[0]
    parts = 4
    chunk, rest_chunk = rows // parts, rest // parts
    copies = start_all(
        [(w_hbm, w_ref)]
        + [
            (feats_hbm.at[pl.ds(i * chunk, chunk)], feats.at[pl.ds(i * chunk, chunk)])
            for i in range(parts)
        ]
        + [
            (
                feats_hbm.at[pl.ds(rows + i * rest_chunk, rest_chunk)],
                rest_ref.at[pl.ds(i * rest_chunk, rest_chunk)],
            )
            for i in range(parts)
        ],
        sems,
    )
    copies[0].wait()
    for i in range(parts):
        copies[1 + i].wait()
        at = pl.ds(i * chunk, chunk)
        out_ref[at, :] = dot(feats[at, :], w_ref[...])
    for copy in copies[1 + parts :]:
        copy.wait()


def project_rest_kernel(rest_ref, w_ref, out_ref):
    out_ref[...] = dot(rest_ref[...], w_ref[...])


def own_rows(adj, slot, core, piece):
    pairs = adj.shape[1] // (2 * piece)
    return jnp.concatenate(
        [
            adj[slot, pl.ds(pl.multiple_of((2 * y + core) * piece, piece), piece), :]
            for y in range(pairs)
        ],
        axis=0,
    )


def partial_kernel(
    dst_any, src_any, count_any, counts_any, adj, *refs, near, far,
):
    parts = refs[:-7]
    out_ref, projected, acc, dst_ref, src_ref, count_ref, sems = refs[-7:]
    copies = start_all(
        [(dst_any, dst_ref), (src_any, src_ref), (count_any, count_ref)], sems
    )
    slots, block, _ = adj.shape
    pairs = acc.shape[0]
    piece = acc.shape[1] // (near * far + 1)
    hidden = acc.shape[2]
    half = len(parts) // 2
    acc[...] = jnp.zeros_like(acc)
    start = 0
    for i in range(half):
        both = parts[i][...] + parts[half + i][...]
        high = both.astype(BF16)
        at = pl.ds(start, both.shape[0])
        start += both.shape[0]
        projected[at, :hidden] = high
        projected[at, hidden:] = (both - high.astype(F32)).astype(BF16)
    for copy in copies:
        copy.wait()
    core = lax.axis_index("core")
    count = count_ref[0]
    step = 64

    def some_slots(group, carry):
        for j in range(step):
            slot = group * step + j
            right = projected[pl.ds(pl.multiple_of(src_ref[slot] * block, block), block), :]
            result = dot(own_rows(adj, slot, core, piece), right)
            result = result[:, :hidden] + result[:, hidden:]
            d = dst_ref[slot]
            place = ((d % near) * far + d // near) * piece
            place = jnp.where(slot < count, place, near * far * piece)
            at = pl.ds(pl.multiple_of(place, piece), piece)
            for y in range(pairs):
                acc[y, at, :] += result[y * piece : (y + 1) * piece]
        return carry

    lax.fori_loop(0, slots // step, some_slots, 0)
    out_ref[...] = acc[:, : near * far * piece, :].astype(BF16).reshape(out_ref.shape)


def count_kernel(
    nbr_ref, type_ref, count_ref, *, cuts, block, near, far
):
    fanout, rows = nbr_ref.shape
    cells = count_ref.shape[0]
    types = count_ref.shape[1] // rows
    piece = block // cuts
    nbr = nbr_ref[...]
    within = nbr % block
    owner = nbr // block
    cut = within // piece
    group = ((cut // 2) * near + owner % near) * far + owner // near
    key = jnp.where(cut % 2 == lax.axis_index("core"), group * piece + within % piece, -1)
    digit = jnp.left_shift(1, 4 * type_ref[...])
    tile = 128
    for start in range(0, cells, tile):
        place = lax.broadcasted_iota(jnp.int32, (tile, rows), 0) + start
        total = jnp.zeros((tile, rows), jnp.int32)
        for k in range(fanout):
            total += jnp.where(key[k : k + 1] == place, digit[k : k + 1], 0)
        for e in range(types):
            part = jnp.bitwise_and(jnp.right_shift(total, 4 * e), 15)
            count_ref[start : start + tile, e * rows : (e + 1) * rows] = part.astype(F32).astype(BF16)


def fold_kernel(part_ref, out_ref):
    total = jnp.sum(part_ref[...].astype(F32), axis=0).astype(BF16)
    for i in range(out_ref.shape[0]):
        out_ref[i] = total


def state_kernel(part_ref, exact_ref, out_ref):
    total = jnp.sum(part_ref[...].astype(F32), axis=0)
    exact = jnp.tanh(total)
    exact_ref[...] = exact
    states = exact.astype(BF16)
    for i in range(out_ref.shape[0]):
        out_ref[i] = states


def message_kernel(count_ref, states_ref, w_ref, out_ref):
    planes, _, hidden = states_ref.shape
    rows = out_ref.shape[0] * 2 // 3
    near = lax.axis_size("x")
    pairs = planes // near
    piece = (out_ref.shape[0] - rows) // pairs
    turned = jnp.concatenate([states_ref[i].T for i in range(planes)], axis=1)
    picked = dot(turned, count_ref[...]).astype(BF16)
    total = jnp.zeros((hidden, rows), F32)
    for e in range(count_ref.shape[1] // rows):
        total += dot(
            w_ref[:, e * hidden : (e + 1) * hidden].T, picked[:, e * rows : (e + 1) * rows]
        )
    out_ref[:rows, :] = total
    at = pl.ds(pl.multiple_of(lax.axis_index("z") * piece, piece), piece)
    for y in range(pairs):
        own = states_ref[y * near + lax.axis_index("x"), at, :]
        out_ref[rows + y * piece : rows + (y + 1) * piece, :] = own.astype(F32)


def gate_kernel(
    mine_ref, other_ref, count_ref, grad_ref, w_edge_ref, w_in_ref, w_state_ref, w_cand_ref,
    new_ref, back_ref, own, spread, state_rows,
):
    rows, hidden = grad_ref.shape
    near, group, _ = back_ref.shape
    local = near * group
    pairs = count_ref.shape[0] // local
    piece = rows // (2 * pairs)
    core = lax.axis_index("core")
    message = (mine_ref[:rows, :] + other_ref[:rows, :]).T
    for y in range(pairs):
        source = slice(rows + y * piece, rows + (y + 1) * piece)
        at = pl.ds(pl.multiple_of((2 * y + core) * piece, piece), piece)
        state_rows[at, :] = mine_ref[source, :].astype(BF16)
        at = pl.ds(pl.multiple_of((2 * y + 1 - core) * piece, piece), piece)
        state_rows[at, :] = other_ref[source, :].astype(BF16)
    states = state_rows[...]
    message_in = message.astype(BF16)
    w_in = w_in_ref[...]
    w_state = w_state_ref[...]
    w_cand = w_cand_ref[...]
    gate_in = dot(message_in, w_in)
    gate_state = dot(states, w_state)
    value = states.astype(F32)
    update = jax.nn.sigmoid(gate_in[:, :hidden] + gate_state[:, :hidden])
    reset = jax.nn.sigmoid(gate_in[:, hidden : 2 * hidden] + gate_state[:, hidden:])
    candidate = jnp.tanh(gate_in[:, 2 * hidden :] + dot((reset * value).astype(BF16), w_cand))
    new_ref[...] = ((1.0 - update) * candidate + update * value).astype(BF16)
    out_grad = grad_ref[...].astype(F32)
    cand_pre = out_grad * (1.0 - update) * (1.0 - candidate * candidate)
    update_pre = out_grad * (value - candidate) * update * (1.0 - update)
    contract = (((1,), (1,)), ((), ()))
    cand_grad = cand_pre.astype(BF16)
    reset_in = lax.dot_general(cand_grad, w_cand, contract, preferred_element_type=F32)
    reset_pre = reset_in * value * reset * (1.0 - reset)
    gates = jnp.concatenate([update_pre.astype(BF16), reset_pre.astype(BF16), cand_grad], axis=1)
    message_grad = lax.dot_general(gates, w_in, contract, preferred_element_type=F32).astype(BF16)
    own[...] = (
        out_grad * update
        + reset_in * reset
        + lax.dot_general(gates[:, : 2 * hidden], w_state, contract, preferred_element_type=F32)
    )
    mine = pl.ds(pl.multiple_of(lax.axis_index("y") * local, local), local)
    picked = jnp.concatenate(
        [
            dot(count_ref[mine, e * rows : (e + 1) * rows], message_grad).astype(BF16)
            for e in range(count_ref.shape[1] // rows)
        ],
        axis=1,
    )
    spread[...] = lax.dot_general(
        picked, w_edge_ref[...], contract, preferred_element_type=F32
    )
    far = back_ref.shape[1] // piece
    place = (lax.axis_index("x") * far + lax.axis_index("z")) * piece
    spread[pl.ds(pl.multiple_of(place, piece), piece), :] += own[
        pl.ds(pl.multiple_of(cut_index() * piece, piece), piece), :
    ]
    back_ref[...] = spread[...].astype(BF16).reshape(back_ref.shape)


def grad_kernel(part_ref, exact_ref, out_ref):
    total = jnp.sum(part_ref[...].astype(F32), axis=0)
    exact = exact_ref[...]
    grad = (total * (1.0 - exact * exact)).astype(BF16)
    for q in range(out_ref.shape[0]):
        out_ref[q] = grad


def spread_kernel(
    dst_any, src_any, count_any, new_any, grads_ref, adj, out_ref, low_ref, new_out,
    turned, acc, dst_ref, src_ref, count_ref, sems, *, near, far,
):
    slots, block, _ = adj.shape
    piece = grads_ref.shape[1] // far
    pairs = grads_ref.shape[0] // near
    copies = start_all(
        [(dst_any, dst_ref), (src_any, src_ref), (count_any, count_ref), (new_any, new_out)], sems
    )
    acc[...] = jnp.zeros_like(acc)
    for z in range(far):
        for x in range(near):
            rows = jnp.concatenate(
                [grads_ref[y * near + x, z * piece : (z + 1) * piece, :] for y in range(pairs)],
                axis=0,
            )
            turned[z * near + x] = rows.T
    for copy in copies[:3]:
        copy.wait()
    core = lax.axis_index("core")
    count = count_ref[0]
    step = 64

    def some_slots(group, carry):
        for j in range(step):
            slot = group * step + j
            result = dot(turned[dst_ref[slot]], own_rows(adj, slot, core, piece))
            acc[jnp.where(slot < count, src_ref[slot], acc.shape[0] - 1)] += result
        return carry

    lax.fori_loop(0, slots // step, some_slots, 0)
    for s in range(acc.shape[0] - 1):
        high = acc[s].astype(BF16)
        out_ref[:, s * block : (s + 1) * block] = high
        low_ref[:, s * block : (s + 1) * block] = (acc[s] - high.astype(F32)).astype(BF16)
    copies[3].wait()


def weight_kernel(high_ref, low_ref, feats_ref, out_ref):
    hidden = high_ref.shape[0]
    both = jnp.concatenate([high_ref[...], low_ref[...]], axis=0)
    total = dot(both, feats_ref[...])
    out_ref[...] = total[:hidden] + total[hidden:]


def weight_out_kernel(spread_ref, feats_ref, part_ref, out_ref):
    total = part_ref[...] + dot(spread_ref[...], feats_ref[...])
    out_ref[...] = total.T.astype(BF16).reshape(out_ref.shape)


def body(
    feats,
    adjacency,
    blk_dst,
    blk_src,
    blk_count,
    nbr_ids,
    edge_types,
    w_first,
    w_edge,
    w_gate_in,
    w_gate_state,
    w_cand,
    out_grad,
):
    slots, block, _ = adjacency.shape
    nodes, feat_cols = feats.shape
    hidden = w_first.shape[1]
    rows = out_grad.shape[0]
    types = w_edge.shape[1] // hidden
    far = lax.axis_size("z")
    near = lax.axis_size("x")
    pairs = lax.axis_size("y")
    domains = far * near
    cuts = 2 * pairs
    piece = block // cuts
    local = domains * piece

    def over_dom(x):
        return lax.all_to_all(x, ("z", "x"), 0, 0, tiled=True)

    def over_plane(x):
        return lax.all_to_all(x, ("y", "x"), 0, 0, tiled=True)

    def over_near(x):
        return lax.all_to_all(x, "x", 0, 0, tiled=True)

    def over_far(x):
        return lax.all_to_all(x, "z", 0, 0, tiled=True)

    def swap(x):
        return lax.ppermute(x, "core", [(0, 1), (1, 0)])

    first_rows = nodes // 2
    rest_rows = nodes - first_rows
    projected, rest, w = pl.pallas_call(
        project_kernel,
        out_shape=(
            jax.ShapeDtypeStruct((first_rows, hidden), F32),
            jax.ShapeDtypeStruct((rest_rows, feat_cols), BF16),
            jax.ShapeDtypeStruct((feat_cols, hidden), BF16),
        ),
        in_specs=[hspec()] * 2,
        out_specs=(vspec(), vspec(), vspec()),
        scratch_shapes=[VMEM((first_rows, feat_cols), BF16), pltpu.SemaphoreType.DMA((9,))],
        compiler_params=params(),
        name="project",
    )(
        pltpu.with_memory_space_constraint(feats, pltpu.HBM),
        pltpu.with_memory_space_constraint(w_first, pltpu.HBM),
    )
    projected_rest = pl.pallas_call(
        project_rest_kernel,
        out_shape=jax.ShapeDtypeStruct((rest_rows, hidden), F32),
        in_specs=[vspec(), vspec()],
        out_specs=vspec(),
        compiler_params=params(),
        name="project_rest",
    )(rest, w)
    mine_parts = [projected, projected_rest]
    swapped = []
    for part in mine_parts:
        swapped.append(swap(part))
    counts = pl.pallas_call(
        lambda *refs: count_kernel(*refs, cuts=cuts, block=block, near=near, far=far),
        out_shape=jax.ShapeDtypeStruct((pairs * local, types * rows), BF16),
        in_specs=[vspec(), vspec()],
        out_specs=vspec(),
        compiler_params=params(),
        name="counts",
    )(nbr_ids.T, edge_types.T)
    partial = pl.pallas_call(
        lambda *refs: partial_kernel(*refs, near=near, far=far),
        out_shape=jax.ShapeDtypeStruct((pairs * near, far * piece, hidden), BF16),
        in_specs=[aspec()] * 4 + [vspec()] * (1 + 2 * len(mine_parts)),
        out_specs=vspec(),
        scratch_shapes=[
            VMEM((nodes, 2 * hidden), BF16),
            VMEM((pairs, local + piece, hidden), F32),
            SMEM((slots,), jnp.int32),
            SMEM((slots,), jnp.int32),
            SMEM((1,), jnp.int32),
            pltpu.SemaphoreType.DMA((3,)),
        ],
        compiler_params=params(),
        name="partial",
    )(blk_dst, blk_src, blk_count, counts, adjacency, *mine_parts, *swapped)
    group = far * piece
    tiled = lambda n: jax.ShapeDtypeStruct((n, group, hidden), BF16)

    def fold(x):
        return pl.pallas_call(
            fold_kernel,
            out_shape=tiled(far),
            in_specs=[vspec()],
            out_specs=vspec(),
            compiler_params=params(),
            name="fold",
        )(x)

    by_far = over_far(fold(over_plane(partial)))
    exact, tiled_states = pl.pallas_call(
        state_kernel,
        out_shape=(jax.ShapeDtypeStruct((group, hidden), F32), tiled(pairs * near)),
        in_specs=[vspec()],
        out_specs=(vspec(), vspec()),
        compiler_params=params(),
        name="state",
    )(by_far)
    states = over_plane(tiled_states)
    half_message = pl.pallas_call(
        message_kernel,
        out_shape=jax.ShapeDtypeStruct((rows + rows // 2, hidden), F32),
        in_specs=[vspec()] * 3,
        out_specs=vspec(),
        compiler_params=params(),
        name="message",
    )(counts, states, w_edge)
    other_message = swap(half_message)
    new_rows, back = pl.pallas_call(
        gate_kernel,
        out_shape=(jax.ShapeDtypeStruct((rows, hidden), BF16), tiled(near)),
        in_specs=[vspec()] * 8,
        out_specs=(vspec(), vspec()),
        scratch_shapes=[
            VMEM((rows, hidden), F32),
            VMEM((local, hidden), F32),
            VMEM((rows, hidden), BF16),
        ],
        compiler_params=params(),
        name="gates",
    )(half_message, other_message, counts, out_grad, w_edge, w_gate_in, w_gate_state, w_cand)
    grad_part = over_far(fold(over_near(back)))
    own_grad = pl.pallas_call(
        grad_kernel,
        out_shape=tiled(pairs * near),
        in_specs=[vspec()] * 2,
        out_specs=vspec(),
        compiler_params=params(),
        name="first_grad",
    )(grad_part, exact)
    grads = over_plane(own_grad)
    mine, mine_low, new_state = pl.pallas_call(
        lambda *refs: spread_kernel(*refs, near=near, far=far),
        out_shape=(
            jax.ShapeDtypeStruct((hidden, nodes), BF16),
            jax.ShapeDtypeStruct((hidden, nodes), BF16),
            jax.ShapeDtypeStruct((rows, hidden), BF16),
        ),
        in_specs=[aspec()] * 4 + [vspec()] * 2,
        out_specs=(vspec(), vspec(), aspec()),
        scratch_shapes=[
            VMEM((domains, hidden, pairs * piece), BF16),
            VMEM((nodes // block + 1, hidden, block), F32),
            SMEM((slots,), jnp.int32),
            SMEM((slots,), jnp.int32),
            SMEM((1,), jnp.int32),
            pltpu.SemaphoreType.DMA((4,)),
        ],
        compiler_params=params(),
        name="spread",
    )(blk_dst, blk_src, blk_count, new_rows, grads, adjacency)
    other = swap(mine)
    own_part = pl.pallas_call(
        weight_kernel,
        out_shape=jax.ShapeDtypeStruct((hidden, feat_cols), F32),
        in_specs=[vspec()] * 3,
        out_specs=vspec(),
        compiler_params=params(),
        name="weight_own",
    )(mine, mine_low, feats)
    weight_part = pl.pallas_call(
        weight_out_kernel,
        out_shape=jax.ShapeDtypeStruct((domains, feat_cols // domains, hidden), BF16),
        in_specs=[vspec()] * 3,
        out_specs=vspec(),
        compiler_params=params(),
        name="weight_all",
    )(other, feats, own_part)
    w_first_grad = jnp.sum(over_dom(weight_part).astype(F32), axis=0)
    return (new_state, w_first_grad)


def solution(mesh):
    cuts, domains = mesh.devices.shape
    fine = jax.sharding.Mesh(
        mesh.devices.reshape(cuts // 2, 2, domains // 4, 4), ("y", "core", "z", "x")
    )
    dom = ("z", "x")
    cut = ("y", "core")

    return jax.shard_map(
        body,
        mesh=fine,
        in_specs=(
            P(dom, cut),
            P(dom, None, None),
            P(dom),
            P(dom),
            P(dom),
            P(dom, None),
            P(dom, None),
            P(cut, None),
            P(),
            P(),
            P(),
            P(),
            P(dom, None),
        ),
        out_specs=(P(dom, None), P(cut + dom, None)),
        check_vma=False,
    )
```

```python
import jax
import jax.numpy as jnp
from jax import lax
from jax.experimental import pallas as pl
from jax.experimental.pallas import tpu as pltpu
from jax.sharding import PartitionSpec as P


F32 = jnp.float32
BF16 = jnp.bfloat16
VMEM = pltpu.VMEM
SMEM = pltpu.SMEM


def vspec():
    return pl.BlockSpec(memory_space=pltpu.VMEM)


def hspec():
    return pl.BlockSpec(memory_space=pltpu.HBM)


def aspec():
    return pl.BlockSpec(memory_space=pl.ANY)


def start_all(pairs, sems):
    copies = [
        pltpu.make_async_copy(source, target, sems.at[i])
        for i, (source, target) in enumerate(pairs)
    ]
    for copy in copies:
        copy.start()
    return copies


def params():
    return pltpu.CompilerParams(vmem_limit_bytes=12 * 1024 * 1024)


def cut_index():
    return 2 * lax.axis_index("y") + lax.axis_index("core")


def dot(a, b):
    return jnp.dot(a, b, preferred_element_type=F32)


def project_kernel(feats_hbm, w_hbm, out_ref, rest_ref, w_ref, feats, sems):
    rows, rest = feats.shape[0], rest_ref.shape[0]
    copies = start_all(
        [
            (w_hbm, w_ref),
            (feats_hbm.at[pl.ds(0, rows)], feats),
            (feats_hbm.at[pl.ds(rows, rest)], rest_ref),
        ],
        sems,
    )
    copies[0].wait()
    copies[1].wait()
    out_ref[...] = dot(feats[...], w_ref[...])
    copies[2].wait()


def project_rest_kernel(rest_ref, w_ref, out_ref):
    out_ref[...] = dot(rest_ref[...], w_ref[...])


def own_rows(adj, slot, core, piece):
    pairs = adj.shape[1] // (2 * piece)
    return jnp.concatenate(
        [
            adj[slot, pl.ds(pl.multiple_of((2 * y + core) * piece, piece), piece), :]
            for y in range(pairs)
        ],
        axis=0,
    )


def partial_kernel(
    dst_any, src_any, count_any, counts_any, adj, *refs, near, far,
):
    parts = refs[:-7]
    out_ref, projected, acc, dst_ref, src_ref, count_ref, sems = refs[-7:]
    copies = start_all(
        [(dst_any, dst_ref), (src_any, src_ref), (count_any, count_ref)], sems
    )
    slots, block, _ = adj.shape
    pairs = acc.shape[0]
    piece = acc.shape[1] // (near * far + 1)
    hidden = acc.shape[2]
    half = len(parts) // 2
    acc[...] = jnp.zeros_like(acc)
    start = 0
    for i in range(half):
        both = parts[i][...] + parts[half + i][...]
        high = both.astype(BF16)
        at = pl.ds(start, both.shape[0])
        start += both.shape[0]
        projected[at, :hidden] = high
        projected[at, hidden:] = (both - high.astype(F32)).astype(BF16)
    for copy in copies:
        copy.wait()
    core = lax.axis_index("core")
    count = count_ref[0]
    step = 64

    def some_slots(group, carry):
        for j in range(step):
            slot = group * step + j
            right = projected[pl.ds(pl.multiple_of(src_ref[slot] * block, block), block), :]
            result = dot(own_rows(adj, slot, core, piece), right)
            result = result[:, :hidden] + result[:, hidden:]
            d = dst_ref[slot]
            place = ((d % near) * far + d // near) * piece
            place = jnp.where(slot < count, place, near * far * piece)
            at = pl.ds(pl.multiple_of(place, piece), piece)
            for y in range(pairs):
                acc[y, at, :] += result[y * piece : (y + 1) * piece]
        return carry

    lax.fori_loop(0, slots // step, some_slots, 0)
    out_ref[...] = acc[:, : near * far * piece, :].astype(BF16).reshape(out_ref.shape)


def count_kernel(
    nbr_ref, type_ref, count_ref, *, cuts, block, near, far
):
    fanout, rows = nbr_ref.shape
    cells = count_ref.shape[0]
    types = count_ref.shape[1] // rows
    piece = block // cuts
    nbr = nbr_ref[...]
    within = nbr % block
    owner = nbr // block
    cut = within // piece
    group = ((cut // 2) * near + owner % near) * far + owner // near
    key = jnp.where(cut % 2 == lax.axis_index("core"), group * piece + within % piece, -1)
    digit = jnp.left_shift(1, 4 * type_ref[...])
    tile = 32
    for start in range(0, cells, tile):
        place = lax.broadcasted_iota(jnp.int32, (tile, rows), 0) + start
        total = jnp.zeros((tile, rows), jnp.int32)
        for k in range(fanout):
            total += jnp.where(key[k : k + 1] == place, digit[k : k + 1], 0)
        for e in range(types):
            part = jnp.right_shift(total, 4 * e) if e else total
            if e < types - 1:
                part = jnp.bitwise_and(part, 15)
            count_ref[start : start + tile, e * rows : (e + 1) * rows] = part.astype(F32).astype(BF16)


def fold_kernel(part_ref, out_ref):
    total = jnp.sum(part_ref[...].astype(F32), axis=0).astype(BF16)
    for i in range(out_ref.shape[0]):
        out_ref[i] = total


def state_kernel(part_ref, exact_ref, out_ref):
    total = jnp.sum(part_ref[...].astype(F32), axis=0)
    exact = jnp.tanh(total)
    exact_ref[...] = exact
    states = exact.astype(BF16)
    for i in range(out_ref.shape[0]):
        out_ref[i] = states


def message_kernel(count_ref, states_ref, w_ref, out_ref):
    planes, _, hidden = states_ref.shape
    rows = out_ref.shape[0] * 2 // 3
    near = lax.axis_size("x")
    pairs = planes // near
    piece = (out_ref.shape[0] - rows) // pairs
    turned = jnp.concatenate([states_ref[i].T for i in range(planes)], axis=1)
    picked = dot(turned, count_ref[...]).astype(BF16)
    total = jnp.zeros((hidden, rows), F32)
    for e in range(count_ref.shape[1] // rows):
        total += dot(
            w_ref[:, e * hidden : (e + 1) * hidden].T, picked[:, e * rows : (e + 1) * rows]
        )
    out_ref[:rows, :] = total
    at = pl.ds(pl.multiple_of(lax.axis_index("z") * piece, piece), piece)
    for y in range(pairs):
        own = states_ref[y * near + lax.axis_index("x"), at, :]
        out_ref[rows + y * piece : rows + (y + 1) * piece, :] = own.astype(F32)


def gate_kernel(
    mine_ref, other_ref, count_ref, grad_ref, w_edge_ref, w_in_ref, w_state_ref, w_cand_ref,
    new_ref, back_ref, own, spread, state_rows,
):
    rows, hidden = grad_ref.shape
    near, group, _ = back_ref.shape
    local = near * group
    pairs = count_ref.shape[0] // local
    piece = rows // (2 * pairs)
    core = lax.axis_index("core")
    message = (mine_ref[:rows, :] + other_ref[:rows, :]).T
    for y in range(pairs):
        source = slice(rows + y * piece, rows + (y + 1) * piece)
        at = pl.ds(pl.multiple_of((2 * y + core) * piece, piece), piece)
        state_rows[at, :] = mine_ref[source, :].astype(BF16)
        at = pl.ds(pl.multiple_of((2 * y + 1 - core) * piece, piece), piece)
        state_rows[at, :] = other_ref[source, :].astype(BF16)
    states = state_rows[...]
    message_in = message.astype(BF16)
    w_in = w_in_ref[...]
    w_state = w_state_ref[...]
    w_cand = w_cand_ref[...]
    gate_in = dot(message_in, w_in)
    gate_state = dot(states, w_state)
    value = states.astype(F32)
    update = jax.nn.sigmoid(gate_in[:, :hidden] + gate_state[:, :hidden])
    reset = jax.nn.sigmoid(gate_in[:, hidden : 2 * hidden] + gate_state[:, hidden:])
    candidate = jnp.tanh(gate_in[:, 2 * hidden :] + dot((reset * value).astype(BF16), w_cand))
    new_ref[...] = ((1.0 - update) * candidate + update * value).astype(BF16)
    out_grad = grad_ref[...].astype(F32)
    cand_pre = out_grad * (1.0 - update) * (1.0 - candidate * candidate)
    update_pre = out_grad * (value - candidate) * update * (1.0 - update)
    contract = (((1,), (1,)), ((), ()))
    cand_grad = cand_pre.astype(BF16)
    reset_in = lax.dot_general(cand_grad, w_cand, contract, preferred_element_type=F32)
    reset_pre = reset_in * value * reset * (1.0 - reset)
    gates = jnp.concatenate([update_pre.astype(BF16), reset_pre.astype(BF16), cand_grad], axis=1)
    message_grad = lax.dot_general(gates, w_in, contract, preferred_element_type=F32).astype(BF16)
    own[...] = (
        out_grad * update
        + reset_in * reset
        + lax.dot_general(gates[:, : 2 * hidden], w_state, contract, preferred_element_type=F32)
    )
    mine = pl.ds(pl.multiple_of(lax.axis_index("y") * local, local), local)
    picked = jnp.concatenate(
        [
            dot(count_ref[mine, e * rows : (e + 1) * rows], message_grad).astype(BF16)
            for e in range(count_ref.shape[1] // rows)
        ],
        axis=1,
    )
    spread[...] = lax.dot_general(
        picked, w_edge_ref[...], contract, preferred_element_type=F32
    )
    far = back_ref.shape[1] // piece
    place = (lax.axis_index("x") * far + lax.axis_index("z")) * piece
    spread[pl.ds(pl.multiple_of(place, piece), piece), :] += own[
        pl.ds(pl.multiple_of(cut_index() * piece, piece), piece), :
    ]
    back_ref[...] = spread[...].astype(BF16).reshape(back_ref.shape)


def grad_kernel(part_ref, exact_ref, out_ref):
    total = jnp.sum(part_ref[...].astype(F32), axis=0)
    exact = exact_ref[...]
    grad = (total * (1.0 - exact * exact)).astype(BF16)
    for q in range(out_ref.shape[0]):
        out_ref[q] = grad


def spread_kernel(
    dst_any, src_any, count_any, new_any, grads_ref, adj, out_ref, low_ref, new_out,
    turned, acc, dst_ref, src_ref, count_ref, sems, *, near, far,
):
    slots, block, _ = adj.shape
    piece = grads_ref.shape[1] // far
    pairs = grads_ref.shape[0] // near
    copies = start_all(
        [(dst_any, dst_ref), (src_any, src_ref), (count_any, count_ref), (new_any, new_out)], sems
    )
    acc[...] = jnp.zeros_like(acc)
    for z in range(far):
        for x in range(near):
            rows = jnp.concatenate(
                [grads_ref[y * near + x, z * piece : (z + 1) * piece, :] for y in range(pairs)],
                axis=0,
            )
            turned[z * near + x] = rows.T
    for copy in copies[:3]:
        copy.wait()
    core = lax.axis_index("core")
    count = count_ref[0]
    step = 64

    def some_slots(group, carry):
        for j in range(step):
            slot = group * step + j
            result = dot(turned[dst_ref[slot]], own_rows(adj, slot, core, piece))
            acc[jnp.where(slot < count, src_ref[slot], acc.shape[0] - 1)] += result
        return carry

    lax.fori_loop(0, slots // step, some_slots, 0)
    for s in range(acc.shape[0] - 1):
        high = acc[s].astype(BF16)
        out_ref[:, s * block : (s + 1) * block] = high
        low_ref[:, s * block : (s + 1) * block] = (acc[s] - high.astype(F32)).astype(BF16)
    copies[3].wait()


def weight_kernel(high_ref, low_ref, feats_ref, out_ref):
    hidden = high_ref.shape[0]
    both = jnp.concatenate([high_ref[...], low_ref[...]], axis=0)
    total = dot(both, feats_ref[...])
    out_ref[...] = total[:hidden] + total[hidden:]


def weight_out_kernel(spread_ref, feats_ref, part_ref, out_ref):
    total = part_ref[...] + dot(spread_ref[...], feats_ref[...])
    out_ref[...] = total.T.astype(BF16).reshape(out_ref.shape)


def body(
    feats,
    adjacency,
    blk_dst,
    blk_src,
    blk_count,
    nbr_ids,
    edge_types,
    w_first,
    w_edge,
    w_gate_in,
    w_gate_state,
    w_cand,
    out_grad,
):
    slots, block, _ = adjacency.shape
    nodes, feat_cols = feats.shape
    hidden = w_first.shape[1]
    rows = out_grad.shape[0]
    types = w_edge.shape[1] // hidden
    far = lax.axis_size("z")
    near = lax.axis_size("x")
    pairs = lax.axis_size("y")
    domains = far * near
    cuts = 2 * pairs
    piece = block // cuts
    local = domains * piece

    def over_dom(x):
        return lax.all_to_all(x, ("z", "x"), 0, 0, tiled=True)

    def over_plane(x):
        return lax.all_to_all(x, ("y", "x"), 0, 0, tiled=True)

    def over_near(x):
        return lax.all_to_all(x, "x", 0, 0, tiled=True)

    def over_far(x):
        return lax.all_to_all(x, "z", 0, 0, tiled=True)

    def swap(x):
        return lax.ppermute(x, "core", [(0, 1), (1, 0)])

    first_rows = nodes * 3 // 8
    rest_rows = nodes - first_rows
    projected, rest, w = pl.pallas_call(
        project_kernel,
        out_shape=(
            jax.ShapeDtypeStruct((first_rows, hidden), F32),
            jax.ShapeDtypeStruct((rest_rows, feat_cols), BF16),
            jax.ShapeDtypeStruct((feat_cols, hidden), BF16),
        ),
        in_specs=[hspec()] * 2,
        out_specs=(vspec(), vspec(), vspec()),
        scratch_shapes=[VMEM((first_rows, feat_cols), BF16), pltpu.SemaphoreType.DMA((3,))],
        compiler_params=params(),
        name="project",
    )(
        pltpu.with_memory_space_constraint(feats, pltpu.HBM),
        pltpu.with_memory_space_constraint(w_first, pltpu.HBM),
    )
    projected_rest = pl.pallas_call(
        project_rest_kernel,
        out_shape=jax.ShapeDtypeStruct((rest_rows, hidden), F32),
        in_specs=[vspec(), vspec()],
        out_specs=vspec(),
        compiler_params=params(),
        name="project_rest",
    )(rest, w)
    mine_parts = [projected, projected_rest]
    swapped = []
    for part in mine_parts:
        swapped.append(swap(part))
    counts = pl.pallas_call(
        lambda *refs: count_kernel(*refs, cuts=cuts, block=block, near=near, far=far),
        out_shape=jax.ShapeDtypeStruct((pairs * local, types * rows), BF16),
        in_specs=[vspec(), vspec()],
        out_specs=vspec(),
        compiler_params=params(),
        name="counts",
    )(nbr_ids.T, edge_types.T)
    partial = pl.pallas_call(
        lambda *refs: partial_kernel(*refs, near=near, far=far),
        out_shape=jax.ShapeDtypeStruct((pairs * near, far * piece, hidden), BF16),
        in_specs=[aspec()] * 4 + [vspec()] * (1 + 2 * len(mine_parts)),
        out_specs=vspec(),
        scratch_shapes=[
            VMEM((nodes, 2 * hidden), BF16),
            VMEM((pairs, local + piece, hidden), F32),
            SMEM((slots,), jnp.int32),
            SMEM((slots,), jnp.int32),
            SMEM((1,), jnp.int32),
            pltpu.SemaphoreType.DMA((3,)),
        ],
        compiler_params=params(),
        name="partial",
    )(blk_dst, blk_src, blk_count, counts, adjacency, *mine_parts, *swapped)
    group = far * piece
    tiled = lambda n: jax.ShapeDtypeStruct((n, group, hidden), BF16)

    def fold(x):
        return pl.pallas_call(
            fold_kernel,
            out_shape=tiled(far),
            in_specs=[vspec()],
            out_specs=vspec(),
            compiler_params=params(),
            name="fold",
        )(x)

    by_far = over_far(fold(over_plane(partial)))
    exact, tiled_states = pl.pallas_call(
        state_kernel,
        out_shape=(jax.ShapeDtypeStruct((group, hidden), F32), tiled(pairs * near)),
        in_specs=[vspec()],
        out_specs=(vspec(), vspec()),
        compiler_params=params(),
        name="state",
    )(by_far)
    states = over_plane(tiled_states)
    half_message = pl.pallas_call(
        message_kernel,
        out_shape=jax.ShapeDtypeStruct((rows + rows // 2, hidden), F32),
        in_specs=[vspec()] * 3,
        out_specs=vspec(),
        compiler_params=params(),
        name="message",
    )(counts, states, w_edge)
    other_message = swap(half_message)
    new_rows, back = pl.pallas_call(
        gate_kernel,
        out_shape=(jax.ShapeDtypeStruct((rows, hidden), BF16), tiled(near)),
        in_specs=[vspec()] * 8,
        out_specs=(vspec(), vspec()),
        scratch_shapes=[
            VMEM((rows, hidden), F32),
            VMEM((local, hidden), F32),
            VMEM((rows, hidden), BF16),
        ],
        compiler_params=params(),
        name="gates",
    )(half_message, other_message, counts, out_grad, w_edge, w_gate_in, w_gate_state, w_cand)
    grad_part = over_far(fold(over_near(back)))
    own_grad = pl.pallas_call(
        grad_kernel,
        out_shape=tiled(pairs * near),
        in_specs=[vspec()] * 2,
        out_specs=vspec(),
        compiler_params=params(),
        name="first_grad",
    )(grad_part, exact)
    grads = over_plane(own_grad)
    mine, mine_low, new_state = pl.pallas_call(
        lambda *refs: spread_kernel(*refs, near=near, far=far),
        out_shape=(
            jax.ShapeDtypeStruct((hidden, nodes), BF16),
            jax.ShapeDtypeStruct((hidden, nodes), BF16),
            jax.ShapeDtypeStruct((rows, hidden), BF16),
        ),
        in_specs=[aspec()] * 4 + [vspec()] * 2,
        out_specs=(vspec(), vspec(), aspec()),
        scratch_shapes=[
            VMEM((domains, hidden, pairs * piece), BF16),
            VMEM((nodes // block + 1, hidden, block), F32),
            SMEM((slots,), jnp.int32),
            SMEM((slots,), jnp.int32),
            SMEM((1,), jnp.int32),
            pltpu.SemaphoreType.DMA((4,)),
        ],
        compiler_params=params(),
        name="spread",
    )(blk_dst, blk_src, blk_count, new_rows, grads, adjacency)
    other = swap(mine)
    own_part = pl.pallas_call(
        weight_kernel,
        out_shape=jax.ShapeDtypeStruct((hidden, feat_cols), F32),
        in_specs=[vspec()] * 3,
        out_specs=vspec(),
        compiler_params=params(),
        name="weight_own",
    )(mine, mine_low, feats)
    weight_part = pl.pallas_call(
        weight_out_kernel,
        out_shape=jax.ShapeDtypeStruct((domains, feat_cols // domains, hidden), BF16),
        in_specs=[vspec()] * 3,
        out_specs=vspec(),
        compiler_params=params(),
        name="weight_all",
    )(other, feats, own_part)
    w_first_grad = jnp.sum(over_dom(weight_part).astype(F32), axis=0)
    return (new_state, w_first_grad)


def solution(mesh):
    cuts, domains = mesh.devices.shape
    fine = jax.sharding.Mesh(
        mesh.devices.reshape(cuts // 2, 2, domains // 4, 4), ("y", "core", "z", "x")
    )
    dom = ("z", "x")
    cut = ("y", "core")

    return jax.shard_map(
        body,
        mesh=fine,
        in_specs=(
            P(dom, cut),
            P(dom, None, None),
            P(dom),
            P(dom),
            P(dom),
            P(dom, None),
            P(dom, None),
            P(cut, None),
            P(),
            P(),
            P(),
            P(),
            P(dom, None),
        ),
        out_specs=(P(dom, None), P(cut + dom, None)),
        check_vma=False,
    )
```
